32 devices in a mesh: dp: 16 (over z, y, x), tensor: 2 (over core).
Axes of the slice: x: 2, y: 2, z: 4, core: 2. Of those that a mesh axis runs over, the one named last changes fastest.
Arguments:
- embedded: bfloat16 [16, 1024, 768], P('dp', 'tensor'), may hold values from -6 to 6
- lengths: int32 [16], P('dp'), may hold values from 256 to 1024, as said below
- patch_proj: bfloat16 [6144, 768], P(('dp', 'tensor')), may hold values from -0.078125 to 0.078125
- global_proj: bfloat16 [768, 6144], P(None, ('dp', 'tensor')), may hold values from -0.21875 to 0.21875
- qkv_weight: bfloat16 [2, 768, 3, 768], P(None, 'dp', None, 'tensor'), may hold values from -0.21875 to 0.21875
- out_weight: bfloat16 [2, 768, 768], P(None, 'tensor', 'dp'), may hold values from -0.875 to 0.875
- up_weight: bfloat16 [2, 768, 3072], P(None, 'dp', 'tensor'), may hold values from -0.21875 to 0.21875
- down_weight: bfloat16 [2, 3072, 768], P(None, 'tensor', 'dp'), may hold values from -0.109375 to 0.109375
- norm_gain: bfloat16 [3072], P(('dp', 'tensor')), may hold values from 0.25 to 1.75
- norm_bias: bfloat16 [3072], P(('dp', 'tensor')), may hold values from -1.5 to 1.5
- cotangent: bfloat16 [16, 1024, 768], P('dp', 'tensor'), may hold values from -6 to 6
Outputs:
- result: bfloat16 [16, 1024, 768], P('dp', 'tensor')
- grad_embedded: bfloat16 [16, 1024, 768], P('dp', 'tensor')
- grad_patch_proj: float32 [6144, 768], P(('dp', 'tensor'))
- grad_global_proj: float32 [768, 6144], P(None, ('dp', 'tensor'))
- grad_qkv_weight: float32 [2, 768, 3, 768], P(None, 'dp', None, 'tensor')
- grad_out_weight: float32 [2, 768, 768], P(None, 'tensor', 'dp')
- grad_up_weight: float32 [2, 768, 3072], P(None, 'dp', 'tensor')
- grad_down_weight: float32 [2, 3072, 768], P(None, 'tensor', 'dp')
- grad_norm_gain: float32 [3072], P(('dp', 'tensor'))
- grad_norm_bias: float32 [3072], P(('dp', 'tensor'))
The draws below stay inside these ranges and needn't reach their ends.
Inputs may be any that keep to these rules, and one draw needn't show every extreme that they name: `lengths`: one slot has exactly 1024 valid bytes and another exactly 256.
All inputs are finite; a program needn't handle non-finite values.
Results may differ from the reference program's by a relative error of at most 0.03.
Values may be sent and summed in bfloat16 or wider, within the bound.
No kernel may reach another device: no remote copies, remote signals or barrier semaphores. Data moves between devices by JAX's collectives and lax.ppermute only.
A program may use at most 256 MiB of HBM per device.

```python
import jax
import jax.numpy as jnp
from jax import lax

D = 768
HD = 64
FF = 3072
P_SIZE = 8
NORMS = 4
LEN = 1024
SLOTS = 16


def draw_lengths(key, part):
    key_base = jax.random.fold_in(key, 11)
    key_long = jax.random.fold_in(key, 12)
    key_short = jax.random.fold_in(key, 13)
    drawn_lengths = jax.random.randint(key_base, (SLOTS,), LEN // 4, LEN + 1)
    long_slot = jax.random.randint(key_long, (), 0, SLOTS)
    short_slot = (long_slot + 1 + jax.random.randint(key_short, (), 0, SLOTS - 1)) % SLOTS
    places = jnp.arange(SLOTS)
    chosen = jnp.where(places == long_slot, LEN, jnp.where(places == short_slot, LEN // 4, drawn_lengths))
    return chosen.astype(jnp.int32)


def block_scale(own_key, shape, pieces, smallest, largest):
    level = 1.0
    for position, shards_of in pieces:
        heights = jax.random.uniform(jax.random.fold_in(jax.random.fold_in(own_key, 6), position), (shards_of,), jnp.float32, smallest / len(pieces), largest / len(pieces))
        level = level * jnp.repeat(jnp.exp(heights), shape[position] // shards_of).reshape((-1,) + (1,) * (len(shape) - 1 - position))
    return level


def centred(own_key, shape, scale, reach, pieces=(), kind=jnp.bfloat16):
    values = scale * jax.random.normal(own_key, shape, jnp.float32)
    if pieces:
        values = values * block_scale(own_key, shape, pieces, -0.22, 0.18)
    return jnp.clip(values, -reach, reach).astype(kind)


def setup_inputs(seed: int = 0) -> dict:
    keys = jax.random.split(jax.random.key(seed), 12)
    embedded = centred(keys[0], (SLOTS, LEN, D), 1.0, 6.0, ((0, 16), (1, 2)))
    lengths = draw_lengths(jax.random.fold_in(keys[11], 71), 0)
    patch_proj = centred(keys[2], (P_SIZE * D, D), (P_SIZE * D) ** -0.5, 0.078125, ((0, 32),))
    global_proj = centred(keys[3], (D, P_SIZE * D), D ** -0.5, 0.21875, ((1, 32),))
    qkv_weight = centred(keys[4], (2, D, 3, D), D ** -0.5, 0.21875, ((1, 16), (3, 2)))
    out_weight = centred(keys[5], (2, D, D), (D // 16) ** -0.5, 0.875, ((1, 2), (2, 16)))
    up_weight = centred(keys[6], (2, D, FF), D ** -0.5, 0.21875, ((1, 16), (2, 2)))
    down_weight = centred(keys[7], (2, FF, D), FF ** -0.5, 0.109375, ((1, 2), (2, 16)))
    norm_gain = jnp.clip(1.0 + 0.15 * jax.random.normal(keys[8], (NORMS * D,), jnp.float32), 0.25, 1.75).astype(jnp.bfloat16)
    norm_bias = centred(keys[9], (NORMS * D,), 0.3, 1.5, ((0, 32),))
    cotangent = centred(keys[10], (SLOTS, LEN, D), 1.0, 6.0, ((0, 16), (1, 2)))
    return dict(embedded=embedded, lengths=lengths, patch_proj=patch_proj, global_proj=global_proj, qkv_weight=qkv_weight, out_weight=out_weight, up_weight=up_weight, down_weight=down_weight, norm_gain=norm_gain, norm_bias=norm_bias, cotangent=cotangent)


EPSILON = 1e-05
NEGATIVE = -1e+30
HIGHEST = lax.Precision.HIGHEST

@jax.custom_vjp
def low(v):
    return lax.optimization_barrier(v.astype(jnp.bfloat16)).astype(jnp.float32)

@jax.custom_vjp
def low_back(v):
    return v

def low_keep(v):
    return (low(v), None)

def low_pass(kept, grad):
    return (grad,)

def back_keep(v):
    return (v, None)

def back_low(kept, grad):
    return (low(grad),)
low.defvjp(low_keep, low_pass)
low_back.defvjp(back_keep, back_low)

def layer_norm(stream, gain_row, bias_row):
    average = lax.optimization_barrier(jnp.mean(stream, axis=-1, keepdims=True))
    centered = stream - average
    variance = lax.optimization_barrier(jnp.mean(centered * centered, axis=-1, keepdims=True))
    return centered * lax.rsqrt(variance + EPSILON) * gain_row + bias_row

def attention(normed, joint_proj, output_proj, group_size):
    row_count = normed.shape[0]
    groups = row_count // group_size
    head_count = joint_proj.shape[2] // HD
    packed = low(low_back(jnp.einsum('rd,dce->rce', normed, joint_proj, precision=HIGHEST)))
    head_shape = (groups, group_size, head_count, HD)
    queries = packed[:, 0].reshape(head_shape)
    keys_all = packed[:, 1].reshape(head_shape)
    values_all = packed[:, 2].reshape(head_shape)
    scores = low_back(jnp.einsum('gihe,gjhe->ghij', queries, keys_all, precision=HIGHEST) * HD ** (-0.5))
    places = jnp.arange(group_size)
    causal = places[:, None] >= places[None, :]
    softened = low(jax.nn.softmax(jnp.where(causal, scores, NEGATIVE), axis=-1))
    mixture = jnp.einsum('ghij,gjhe->gihe', softened, values_all, precision=HIGHEST).reshape(row_count, head_count * HD)
    mixture = low(low_back(mixture))
    return low_back(jnp.dot(mixture, output_proj, precision=HIGHEST))

def feed_forward(normed, upward, downward):
    hidden = low_back(jnp.dot(normed, upward, precision=HIGHEST))
    active = low(jax.nn.gelu(hidden))
    return low_back(jnp.dot(active, downward, precision=HIGHEST))

def layer(stream, joint_proj, output_proj, upward, downward, gain_rows, bias_rows, norm_index, group_size):
    normed = low(layer_norm(stream, gain_rows[norm_index], bias_rows[norm_index]))
    middle = stream + attention(normed, joint_proj, output_proj, group_size)
    second = low(layer_norm(middle, gain_rows[norm_index + 1], bias_rows[norm_index + 1]))
    return middle + feed_forward(second, upward, downward)

def forward(inputs, patch_proj, global_proj, qkv_weight, out_weight, up_weight, down_weight, norm_gain, norm_bias, keep_mask):
    gain_rows = norm_gain.reshape(NORMS, D)
    bias_rows = norm_bias.reshape(NORMS, D)
    masked = inputs * keep_mask[:, None]
    patches = masked.reshape(masked.shape[0] // P_SIZE, P_SIZE * D)
    initial = low_back(jnp.dot(patches, patch_proj, precision=HIGHEST))
    global_out = layer(initial, qkv_weight[0], out_weight[0], up_weight[0], down_weight[0], gain_rows, bias_rows, 0, initial.shape[0])
    spread = low_back(jnp.dot(low(global_out), global_proj, precision=HIGHEST)).reshape(masked.shape)
    return layer(masked + spread, qkv_weight[1], out_weight[1], up_weight[1], down_weight[1], gain_rows, bias_rows, 2, P_SIZE)

def reference(embedded, lengths, patch_proj, global_proj, qkv_weight, out_weight, up_weight, down_weight, norm_gain, norm_bias, cotangent):
    weights = tuple((weight_array.astype(jnp.float32) for weight_array in (patch_proj, global_proj, qkv_weight, out_weight, up_weight, down_weight, norm_gain, norm_bias)))

    def per_slot(totals, sliced):
        inputs, length, grad_final = sliced
        keep_mask = (jnp.arange(LEN).astype(jnp.int32) < length).astype(jnp.float32)

        def forward_slot(inputs_in, *params):
            return forward(inputs_in, *params, keep_mask)
        output, pullback = jax.vjp(forward_slot, inputs, *weights)
        gradients = pullback(grad_final * keep_mask[:, None])
        totals = tuple((summed + fresh for summed, fresh in zip(totals, gradients[1:])))
        return (totals, (output.astype(jnp.bfloat16), gradients[0].astype(jnp.bfloat16)))
    initial = tuple((jnp.zeros(weight_array.shape, jnp.float32) for weight_array in weights))
    totals, (outputs, input_grads) = lax.scan(per_slot, initial, (embedded.astype(jnp.float32), lengths, cotangent.astype(jnp.float32)))
    return (outputs, input_grads, totals[0], totals[1], totals[2], totals[3], totals[4], totals[5], totals[6], totals[7])
```

```python
import jax
import jax.numpy as jnp
from jax import lax
from jax.sharding import PartitionSpec as P

D = 768
HD = 64
P_SIZE = 8
NORMS = 4
QUAD = 4

EPSILON = 1e-05
NEGATIVE = -1e30
BF16 = jnp.bfloat16
F32 = jnp.float32


def dp_size():
    return lax.axis_size("dp")


def line_size():
    return dp_size() // 4


def x_place():
    return lax.axis_index("dp") % 2


def y_place():
    return (lax.axis_index("dp") // 2) % 2


def line_place():
    return lax.axis_index("dp") // 4


def quad_place():
    return x_place() * 2 + lax.axis_index("tensor")


def flip_dp(values_in, bit):
    return lax.ppermute(values_in, "dp", [(i, i ^ bit) for i in range(dp_size())])


def flip_core(values_in):
    return lax.ppermute(values_in, "tensor", [(0, 1), (1, 0)])


def flip_quad(values_in, bits):
    return lax.ppermute(
        values_in, ("dp", "tensor"), [(i, i ^ bits) for i in range(2 * dp_size())]
    )


def step_up(values_in):
    return lax.ppermute(values_in, "dp", [(i, i + 4) for i in range(dp_size() - 4)])


def step_down(values_in):
    return lax.ppermute(values_in, "dp", [(i + 4, i) for i in range(dp_size() - 4)])


def line_groups():
    return [[line * 4 + rest for line in range(line_size())] for rest in range(4)]


def pick(place, choices):
    if len(choices) == 2:
        return lax.select_n(place == 1, *choices)
    return lax.select_n(place, *choices)


def line_gather(values_in):
    count = line_size()
    if count > 4:
        return lax.all_gather(values_in, "dp", axis=0, axis_index_groups=line_groups())
    below, above = [], []
    rising = falling = values_in
    for step in range(count - 1):
        rising, falling = step_up(rising), step_down(falling)
        below.append(rising)
        above.append(falling)
    place = line_place()
    slots = []
    for slot in range(count):
        choices = [
            values_in
            if slot == here
            else (below[here - slot - 1] if slot < here else above[slot - here - 1])
            for here in range(count)
        ]
        slots.append(pick(place, choices) if count > 1 else values_in)
    return jnp.stack(slots)


def pair_up(own, other, place):
    return jnp.stack([pick(place, [own, other]), pick(place, [other, own])], axis=0)


def line_y_gather(values_in):
    lined = line_gather(values_in)
    other = flip_dp(lined, 2)
    place = y_place()
    return jnp.stack([pick(place, [lined, other]), pick(place, [other, lined])], axis=1)


def dp_gather(values_in):
    gathered = line_y_gather(values_in)
    other = flip_dp(gathered, 1)
    place = x_place()
    whole = jnp.stack([pick(place, [gathered, other]), pick(place, [other, gathered])], axis=2)
    return whole.reshape(-1, values_in.shape[-1])


def line_scatter(parts):
    count = line_size()
    if count > 4:
        return lax.psum_scatter(
            parts, "dp", scatter_dimension=0, axis_index_groups=line_groups(), tiled=False
        )
    place = line_place()
    own = lax.dynamic_index_in_dim(parts, place, 0, keepdims=False)
    if count == 1:
        return own
    rising = falling = None
    for step in range(count - 1, 0, -1):
        to_above = lax.dynamic_index_in_dim(
            parts, jnp.minimum(place + step, count - 1), 0, keepdims=False
        )
        to_below = lax.dynamic_index_in_dim(
            parts, jnp.maximum(place - step, 0), 0, keepdims=False
        )
        if rising is not None:
            to_above = to_above + rising
            to_below = to_below + falling
        rising = step_up(to_above.astype(BF16)).astype(F32)
        falling = step_down(to_below.astype(BF16)).astype(F32)
    return own + rising + falling


def halve(parts, place, axis, bit):
    own = lax.dynamic_index_in_dim(parts, place, axis, keepdims=False)
    theirs = lax.dynamic_index_in_dim(parts, 1 - place, axis, keepdims=False)
    return own.astype(F32) + flip_dp(theirs.astype(BF16), bit).astype(F32)


def line_y_scatter(parts):
    shaped = parts.reshape((line_size(), 2) + parts.shape[1:])
    return line_scatter(halve(shaped, y_place(), 1, 2))


def dp_scatter(parts):
    count = line_size()
    rows = parts.shape[0] // (count * 4)
    shaped = parts.reshape(count, 2, 2, rows, parts.shape[1])
    shaped = halve(shaped, x_place(), 2, 1)
    shaped = halve(shaped, y_place(), 1, 2)
    return line_scatter(shaped)


def quad_gather(values_in):
    return jnp.concatenate(
        [values_in] + [flip_quad(values_in, bits) for bits in range(1, QUAD)], axis=0
    )


def quad_scatter(partial_value):
    rows = partial_value.shape[0] // QUAD
    low = partial_value.astype(BF16)
    total = partial_value[:rows].astype(F32)
    for bits in range(1, QUAD):
        total = total + flip_quad(low[bits * rows : (bits + 1) * rows], bits).astype(F32)
    return total


def quad_deal(blocks):
    place = quad_place()
    taken = []
    for bits in range(QUAD):
        piece = lax.dynamic_index_in_dim(blocks, place ^ bits, 2, keepdims=False)
        taken.append(flip_quad(piece, bits) if bits else piece)
    return jnp.concatenate(taken, axis=0)


def quad_collect(blocks):
    rows = blocks.shape[0] // QUAD
    place = quad_place()
    got = [
        flip_quad(blocks[bits * rows : (bits + 1) * rows], bits)
        if bits
        else blocks[bits * rows : (bits + 1) * rows]
        for bits in range(QUAD)
    ]
    return jnp.stack(
        [pick(place, [got[slot ^ here] for here in range(QUAD)]) for slot in range(QUAD)], axis=2
    )


def layer_norm(stream, gain_row, bias_row):
    average = jnp.mean(stream, axis=-1, keepdims=True)
    centered = stream - average
    variance = jnp.mean(centered * centered, axis=-1, keepdims=True)
    return centered * lax.rsqrt(variance + EPSILON) * gain_row + bias_row


def dot_nn(left, right):
    return lax.dot_general(left, right, (((1,), (0,)), ((), ())), preferred_element_type=F32)


def dot_nt(left, right):
    return lax.dot_general(left, right, (((1,), (1,)), ((), ())), preferred_element_type=F32)


def dot_tn(left, right):
    return lax.dot_general(left, right, (((0,), (0,)), ((), ())), preferred_element_type=F32)


def split_heads(packed, group_size):
    row_count, columns = packed.shape
    head_count = columns // (3 * HD)
    shaped = packed.reshape(row_count // group_size, group_size, 3, head_count, HD)
    return shaped[:, :, 0], shaped[:, :, 1], shaped[:, :, 2]


def causal_scores(queries, keys_all, places):
    scores = jnp.einsum(
        "gihe,gjhe->ghij", queries, keys_all, preferred_element_type=F32
    ) * HD ** (-0.5)
    return jnp.where(places[:, None] >= places[None, :], scores, NEGATIVE)


def attend_forward(packed, places):
    queries, keys_all, values_all = split_heads(packed, places.shape[0])
    scores = causal_scores(queries, keys_all, places)
    row_max = jnp.max(scores, axis=-1, keepdims=True)
    shifted = jnp.exp(scores - row_max)
    softened = shifted / jnp.sum(shifted, axis=-1, keepdims=True)
    mixture = jnp.einsum(
        "ghij,gjhe->gihe", softened.astype(BF16), values_all, preferred_element_type=F32
    )
    return mixture.reshape(packed.shape[0], -1).astype(BF16), softened


def attend_backward(packed, softened, grad_mix, places):
    queries, keys_all, values_all = split_heads(packed, places.shape[0])
    grad_heads = grad_mix.reshape(queries.shape)
    grad_soft = jnp.einsum(
        "gihe,gjhe->ghij", grad_heads, values_all, preferred_element_type=F32
    )
    centre = jnp.sum(grad_soft * softened, axis=-1, keepdims=True)
    grad_scores = (softened * (grad_soft - centre)).astype(BF16)
    grad_values = jnp.einsum(
        "ghij,gihe->gjhe", softened.astype(BF16), grad_heads, preferred_element_type=F32
    )
    grad_queries = jnp.einsum(
        "ghij,gjhe->gihe", grad_scores, keys_all, preferred_element_type=F32
    ) * HD ** (-0.5)
    grad_keys = jnp.einsum(
        "ghij,gihe->gjhe", grad_scores, queries, preferred_element_type=F32
    ) * HD ** (-0.5)
    row_count = packed.shape[0]
    return jnp.concatenate(
        [part.reshape(row_count, -1) for part in (grad_queries, grad_keys, grad_values)], axis=1
    ).astype(BF16)


def layer_forward(stream, weights, gain_rows, bias_rows, norm_index, places, widen, narrow):
    joint_proj, output_proj, upward, downward = weights
    normed_all = widen(
        layer_norm(stream, gain_rows[norm_index], bias_rows[norm_index]).astype(BF16)
    )
    packed = dot_nn(normed_all, joint_proj).astype(BF16)
    mixture, softened = attend_forward(packed, places)
    middle = stream + narrow(dot_nt(mixture, output_proj))
    second_all = widen(
        layer_norm(middle, gain_rows[norm_index + 1], bias_rows[norm_index + 1]).astype(BF16)
    )
    hidden = dot_nn(second_all, upward)
    active = jax.nn.gelu(hidden).astype(BF16)
    outcome = middle + narrow(dot_nt(active, downward))
    return (
        outcome,
        (stream, normed_all, packed, mixture, softened, middle, second_all, hidden, active),
    )


def layer_backward(grad_layer, saved, weights, gain_rows, bias_rows, norm_index, places, widen, narrow):
    stream, normed_all, packed, mixture, softened, middle, second_all, hidden, active = saved
    joint_proj, output_proj, upward, downward = weights
    grad_all = widen(grad_layer.astype(BF16))
    grad_active = dot_nn(grad_all, downward)
    gelu_value, gelu_pull = jax.vjp(jax.nn.gelu, hidden)
    grad_hidden = gelu_pull(grad_active)[0].astype(BF16)
    grad_second = narrow(dot_nt(grad_hidden, upward))
    norm_value, second_pull = jax.vjp(
        layer_norm, middle, gain_rows[norm_index + 1], bias_rows[norm_index + 1]
    )
    grad_middle_norm, grad_gain_two, grad_bias_two = second_pull(grad_second)
    grad_middle = grad_layer + grad_middle_norm
    grad_branch = widen(grad_middle.astype(BF16))
    grad_mix = dot_nn(grad_branch, output_proj).astype(BF16)
    grad_packed = attend_backward(packed, softened, grad_mix, places)
    grad_normed = narrow(dot_nt(grad_packed, joint_proj))
    first_value, first_pull = jax.vjp(
        layer_norm, stream, gain_rows[norm_index], bias_rows[norm_index]
    )
    grad_stream_norm, grad_gain_one, grad_bias_one = first_pull(grad_normed)
    grad_stream = grad_middle + grad_stream_norm
    grad_down = dot_tn(grad_all, active)
    grad_up = dot_tn(second_all, grad_hidden)
    grad_output = dot_tn(grad_branch, mixture)
    grad_joint = dot_tn(normed_all, grad_packed)
    return (
        grad_stream,
        (grad_joint, grad_output, grad_up, grad_down),
        (grad_gain_one, grad_gain_two),
        (grad_bias_one, grad_bias_two),
    )


def unchanged(values_in):
    return values_in


def shards(
    embedded,
    lengths,
    patch_proj,
    global_proj,
    qkv_weight,
    out_weight,
    up_weight,
    down_weight,
    norm_gain,
    norm_bias,
    cotangent,
):
    half_rows = embedded.shape[1]
    patch_rows = half_rows // P_SIZE
    shard_rows = qkv_weight.shape[1]
    proj_rows = patch_proj.shape[0]
    norm_part = norm_gain.shape[0]
    cells = 2 * line_size()
    heads_width = qkv_weight.shape[3]
    hidden_width = up_weight.shape[2]
    x_here = x_place()

    positions = lax.axis_index("tensor") * half_rows + jnp.arange(half_rows, dtype=jnp.int32)
    keep_mask = (positions < lengths[0]).astype(F32)[:, None]
    masked_low = (embedded[0].astype(F32) * keep_mask).astype(BF16)

    joint_part = jnp.transpose(qkv_weight, (0, 2, 1, 3))
    output_part = jnp.transpose(out_weight, (0, 2, 1))
    down_part = jnp.transpose(down_weight, (0, 2, 1))

    norm_row = jnp.pad(
        jnp.concatenate([norm_gain, norm_bias]).reshape(1, -1), ((0, 0), (0, D - 2 * norm_part))
    )
    patch_whole = line_y_gather(jnp.concatenate([patch_proj, norm_row], axis=0))
    patch_whole = patch_whole.reshape(cells, proj_rows + 1, D)
    patch_mat = patch_whole[:, :proj_rows].reshape(cells * proj_rows, D)
    norm_cells = patch_whole[:, proj_rows, : 2 * norm_part]
    norm_all = quad_collect(
        jnp.broadcast_to(norm_cells[None], (QUAD,) + norm_cells.shape)
    )[0].astype(F32)
    gain_rows = norm_all[..., :norm_part].reshape(NORMS, D)
    bias_rows = norm_all[..., norm_part:].reshape(NORMS, D)

    def x_half(part):
        return part.reshape(part.shape[:-1] + (2, part.shape[-1] // 2))

    def global_part(layer):
        pieces = []
        for piece in (
            joint_part[layer, 0],
            joint_part[layer, 1],
            joint_part[layer, 2],
            output_part[layer],
            up_weight[layer],
            down_part[layer],
        ):
            halves = x_half(piece)
            pieces.append(halves)
        return jnp.concatenate(pieces, axis=-1)

    halves = global_part(0)
    own_half = lax.dynamic_index_in_dim(halves, x_here, 1, keepdims=False)
    their_half = lax.dynamic_index_in_dim(halves, 1 - x_here, 1, keepdims=False)
    global_shard = pair_up(own_half, flip_dp(their_half, 1), x_here)
    global_shard = global_shard.reshape(2 * shard_rows, -1)
    attend_columns = 2 * heads_width
    attend_shard, forward_shard = global_shard[:, :attend_columns], global_shard[:, attend_columns:]
    attend_whole = line_y_gather(attend_shard).reshape(D, -1)
    forward_whole = line_y_gather(forward_shard).reshape(D, -1)
    joint_columns = 3 * heads_width // 2
    first_weights = (
        attend_whole[:, :joint_columns],
        attend_whole[:, joint_columns:],
        forward_whole[:, : hidden_width // 2],
        forward_whole[:, hidden_width // 2 :],
    )
    spread_mat = line_y_gather(jnp.transpose(global_proj)).reshape(cells * proj_rows, D)

    local_attend = jnp.concatenate([joint_part[1, 0], joint_part[1, 1], joint_part[1, 2], output_part[1]], axis=-1)
    local_forward = jnp.concatenate([up_weight[1], down_part[1]], axis=-1)
    attend_own = dp_gather(local_attend)
    forward_own = dp_gather(local_forward)
    attend_other = flip_core(attend_own)
    forward_other = flip_core(forward_own)
    second_weights = (
        jnp.concatenate(
            [
                source[:, k * heads_width : (k + 1) * heads_width]
                for k in range(3)
                for source in (attend_own, attend_other)
            ],
            axis=1,
        ),
        jnp.concatenate([attend_own[:, 3 * heads_width :], attend_other[:, 3 * heads_width :]], axis=1),
        jnp.concatenate([forward_own[:, :hidden_width], forward_other[:, :hidden_width]], axis=1),
        jnp.concatenate([forward_own[:, hidden_width:], forward_other[:, hidden_width:]], axis=1),
    )

    patches_dealt = quad_deal(masked_low.reshape(patch_rows, cells, QUAD, proj_rows))
    patches_mat = patches_dealt.reshape(QUAD * patch_rows, cells * proj_rows)
    initial = quad_scatter(dot_nn(patches_mat, patch_mat))
    core = lax.axis_index("tensor")
    steps = jnp.arange(patch_rows, dtype=jnp.int32)
    global_places = jnp.concatenate([core * patch_rows + steps, (1 - core) * patch_rows + steps])
    global_out, first_saved = layer_forward(
        initial, first_weights, gain_rows, bias_rows, 0, global_places, quad_gather, quad_scatter
    )
    global_low = quad_gather(global_out.astype(BF16))
    spread_dealt = dot_nt(global_low, spread_mat).astype(BF16)
    spread = quad_collect(spread_dealt.reshape(QUAD * patch_rows, cells, proj_rows))
    spread = spread.reshape(half_rows, D)

    local_places = jnp.arange(P_SIZE, dtype=jnp.int32)
    outcome, second_saved = layer_forward(
        masked_low.astype(F32) + spread.astype(F32),
        second_weights, gain_rows, bias_rows, 2, local_places, unchanged, unchanged,
    )
    grad_final = cotangent[0].astype(F32) * keep_mask
    grad_local, second_grads, second_gains, second_biases = layer_backward(
        grad_final, second_saved, second_weights, gain_rows, bias_rows, 2, local_places, unchanged, unchanged
    )
    grad_joint, grad_output, grad_up, grad_down = second_grads

    def own_columns(k, grads, width):
        return grads[:, k * width : (k + 1) * width]

    forward_grads = [
        jnp.concatenate(
            [own_columns(side, grad_up, hidden_width), own_columns(side, grad_down, hidden_width)], axis=1
        )
        for side in range(2)
    ]
    attend_grads = [
        jnp.concatenate(
            [own_columns(2 * k + side, grad_joint, heads_width) for k in range(3)]
            + [own_columns(side, grad_output, heads_width)],
            axis=1,
        )
        for side in range(2)
    ]
    forward_local = dp_scatter(forward_grads[0] + flip_core(forward_grads[1].astype(BF16)).astype(F32))
    attend_local = dp_scatter(attend_grads[0] + flip_core(attend_grads[1].astype(BF16)).astype(F32))

    grad_spread = grad_local.astype(BF16).reshape(patch_rows, cells, QUAD, proj_rows)
    spread_grads = quad_deal(grad_spread).reshape(QUAD * patch_rows, cells * proj_rows)
    grad_global = quad_scatter(dot_nn(spread_grads, spread_mat))
    grad_proj = line_y_scatter(dot_tn(spread_grads, global_low).reshape(cells, proj_rows, D))
    grad_initial, first_grads, first_gains, first_biases = layer_backward(
        grad_global, first_saved, first_weights, gain_rows, bias_rows, 0, global_places, quad_gather, quad_scatter
    )
    forward_global = line_y_scatter(
        jnp.concatenate([first_grads[2], first_grads[3]], axis=1).reshape(cells, 2 * shard_rows, -1)
    )
    attend_global = line_y_scatter(
        jnp.concatenate([first_grads[0], first_grads[1]], axis=1).reshape(cells, 2 * shard_rows, -1)
    )
    grad_start = quad_gather(grad_initial.astype(BF16))
    grad_patch_mat = dot_tn(patches_mat, grad_start).reshape(cells, proj_rows, D)
    grad_patches = dot_nt(grad_start, patch_mat).astype(BF16)
    grad_patches = quad_collect(grad_patches.reshape(QUAD * patch_rows, cells, proj_rows))
    grad_patches = grad_patches.reshape(half_rows, D).astype(F32)
    grad_input = ((grad_local + grad_patches) * keep_mask).astype(BF16)[None]

    gain_grads = jnp.stack([first_gains[0], first_gains[1], second_gains[0], second_gains[1]])
    bias_grads = jnp.stack([first_biases[0], first_biases[1], second_biases[0], second_biases[1]])
    norm_grads = jnp.concatenate(
        [
            gain_grads.reshape(cells, QUAD, norm_part),
            bias_grads.reshape(cells, QUAD, norm_part),
        ],
        axis=2,
    )
    place = quad_place()
    norm_sum = lax.dynamic_index_in_dim(norm_grads, place, 1, keepdims=False)
    for bits in range(1, QUAD):
        piece = lax.dynamic_index_in_dim(norm_grads, place ^ bits, 1, keepdims=False)
        norm_sum = norm_sum + flip_quad(piece, bits)
    norm_rows = jnp.pad(norm_sum[:, None, :], ((0, 0), (0, 0), (0, D - 2 * norm_part)))
    patch_summed = line_y_scatter(jnp.concatenate([grad_patch_mat, norm_rows], axis=1))

    def x_restore(summed):
        shaped = summed.reshape(2, shard_rows, -1)
        own = lax.dynamic_index_in_dim(shaped, x_here, 0, keepdims=False)
        theirs = lax.dynamic_index_in_dim(shaped, 1 - x_here, 0, keepdims=False)
        return pair_up(own, flip_dp(theirs.astype(BF16), 1).astype(F32), x_here)

    attend_global = x_restore(attend_global)
    forward_global = x_restore(forward_global)

    def x_columns(source, start, width):
        return jnp.concatenate([source[0, :, start : start + width], source[1, :, start : start + width]], axis=1)

    half_heads, half_hidden = heads_width // 2, hidden_width // 2
    joint_out = jnp.stack(
        [
            jnp.stack([x_columns(attend_global, k * half_heads, half_heads) for k in range(3)], axis=1),
            attend_local[:, : 3 * heads_width].reshape(shard_rows, 3, heads_width),
        ]
    )
    output_out = jnp.stack(
        [
            jnp.transpose(x_columns(attend_global, 3 * half_heads, half_heads)),
            jnp.transpose(attend_local[:, 3 * heads_width :]),
        ]
    )
    up_out = jnp.stack([x_columns(forward_global, 0, half_hidden), forward_local[:, :hidden_width]])
    down_out = jnp.stack(
        [
            jnp.transpose(x_columns(forward_global, half_hidden, half_hidden)),
            jnp.transpose(forward_local[:, hidden_width:]),
        ]
    )
    return (
        outcome.astype(BF16)[None],
        grad_input,
        patch_summed[:proj_rows],
        jnp.transpose(grad_proj),
        joint_out,
        output_out,
        up_out,
        down_out,
        patch_summed[proj_rows, :norm_part],
        patch_summed[proj_rows, norm_part : 2 * norm_part],
    )


def solution(mesh):
    placed = (
        P("dp", "tensor", None),
        P("dp"),
        P(("dp", "tensor"), None),
        P(None, ("dp", "tensor")),
        P(None, "dp", None, "tensor"),
        P(None, "tensor", "dp"),
        P(None, "dp", "tensor"),
        P(None, "tensor", "dp"),
        P(("dp", "tensor")),
        P(("dp", "tensor")),
        P("dp", "tensor", None),
    )
    return jax.shard_map(
        shards,
        mesh=mesh,
        in_specs=placed,
        out_specs=(
            P("dp", "tensor", None),
            P("dp", "tensor", None),
            P(("dp", "tensor"), None),
            P(None, ("dp", "tensor")),
            P(None, "dp", None, "tensor"),
            P(None, "tensor", "dp"),
            P(None, "dp", "tensor"),
            P(None, "tensor", "dp"),
            P(("dp", "tensor")),
            P(("dp", "tensor")),
        ),
        check_vma=False,
    )
```

```python
import jax
import jax.numpy as jnp
from jax import lax
from jax.experimental import pallas as pl
from jax.experimental.pallas import tpu as pltpu
from jax.sharding import PartitionSpec as P

D = 768
HD = 64
P_SIZE = 8
NORMS = 4
QUAD = 4

EPSILON = 1e-05
NEGATIVE = -1e30
BF16 = jnp.bfloat16
F32 = jnp.float32


def dp_size():
    return lax.axis_size("dp")


def line_size():
    return dp_size() // 4


def x_place():
    return lax.axis_index("dp") % 2


def y_place():
    return (lax.axis_index("dp") // 2) % 2


def line_place():
    return lax.axis_index("dp") // 4


def quad_place():
    return x_place() * 2 + lax.axis_index("tensor")


def flip_dp(values_in, bit):
    return lax.ppermute(values_in, "dp", [(i, i ^ bit) for i in range(dp_size())])


def flip_core(values_in):
    return lax.ppermute(values_in, "tensor", [(0, 1), (1, 0)])


def flip_quad(values_in, bits):
    return lax.ppermute(
        values_in, ("dp", "tensor"), [(i, i ^ bits) for i in range(2 * dp_size())]
    )


def step_ring(values_in):
    count = dp_size()
    return lax.ppermute(values_in, "dp", [(i, (i + 4) % count) for i in range(count)])


def line_groups():
    return [[line * 4 + rest for line in range(line_size())] for rest in range(4)]


def pick(place, choices):
    if len(choices) == 2:
        return lax.select_n(place == 1, *choices)
    return lax.select_n(place, *choices)


class Queue:
    def __init__(self, depth):
        self.arrived = [None] * depth

    def send(self, transfer, values_in):
        earlier = self.arrived.pop(0)
        if earlier is not None:
            values_in, _ = lax.optimization_barrier((values_in, earlier))
        got = transfer(values_in)
        self.arrived.append(got)
        return got


def line_gather(values_in, queue):
    count = line_size()
    if count > 4:
        return lax.all_gather(values_in, "dp", axis=0, axis_index_groups=line_groups())
    got = [values_in]
    for step in range(count - 1):
        got.append(queue.send(step_ring, got[-1]))
    place = line_place()
    if count == 1:
        return values_in[None]
    return jnp.stack(
        [pick(place, [got[(here - slot) % count] for here in range(count)]) for slot in range(count)]
    )


def pair_up(own, other, place):
    return jnp.stack([pick(place, [own, other]), pick(place, [other, own])], axis=0)


def line_y_gather(values_in, queues):
    lined = line_gather(values_in, queues["line"])
    other = queues["y"].send(lambda moved: flip_dp(moved, 2), lined)
    place = y_place()
    return jnp.stack([pick(place, [lined, other]), pick(place, [other, lined])], axis=1)


def dp_gather(values_in, queues, y_first):
    lined = line_gather(values_in, queues["line"])
    order = (("y", 2, y_place(), 1), ("x", 1, x_place(), 2 if y_first else 1))
    gathered = lined
    for name, bit, place, axis in order if y_first else order[::-1]:
        other = queues[name].send(lambda moved, bit=bit: flip_dp(moved, bit), gathered)
        gathered = jnp.stack(
            [pick(place, [gathered, other]), pick(place, [other, gathered])], axis=axis
        )
    return gathered.reshape(-1, values_in.shape[-1])


def line_scatter(parts):
    count = line_size()
    if count > 4:
        return lax.psum_scatter(
            parts, "dp", scatter_dimension=0, axis_index_groups=line_groups(), tiled=False
        )
    place = line_place()

    def slot(back):
        return lax.dynamic_index_in_dim(parts, (place + count - back) % count, 0, keepdims=False)

    total = slot(1 % count)
    for back in range(2, count + 1):
        total = slot(back % count) + step_ring(total.astype(BF16)).astype(F32)
    return total


def halve(parts, place, axis, bit):
    own = lax.dynamic_index_in_dim(parts, place, axis, keepdims=False)
    theirs = lax.dynamic_index_in_dim(parts, 1 - place, axis, keepdims=False)
    return own.astype(F32) + flip_dp(theirs.astype(BF16), bit).astype(F32)


def line_y_scatter(parts):
    shaped = parts.reshape((line_size(), 2) + parts.shape[1:])
    return line_scatter(halve(shaped, y_place(), 1, 2))


def dp_scatter(parts):
    count = line_size()
    rows = parts.shape[0] // (count * 4)
    shaped = parts.reshape(count, 2, 2, rows, parts.shape[1])
    shaped = halve(shaped, x_place(), 2, 1)
    shaped = halve(shaped, y_place(), 1, 2)
    return line_scatter(shaped)


def quad_gather(values_in):
    return jnp.concatenate(
        [values_in] + [flip_quad(values_in, bits) for bits in range(1, QUAD)], axis=0
    )


def quad_scatter(partial_value):
    rows = partial_value.shape[0] // QUAD
    low = partial_value.astype(BF16)
    total = partial_value[:rows].astype(F32)
    for bits in range(1, QUAD):
        total = total + flip_quad(low[bits * rows : (bits + 1) * rows], bits).astype(F32)
    return total


def quad_deal(blocks):
    place = quad_place()
    taken = []
    for bits in range(QUAD):
        piece = lax.dynamic_index_in_dim(blocks, place ^ bits, 2, keepdims=False)
        taken.append(flip_quad(piece, bits) if bits else piece)
    return jnp.concatenate(taken, axis=0)


def quad_collect(blocks):
    rows = blocks.shape[0] // QUAD
    place = quad_place()
    got = [
        flip_quad(blocks[bits * rows : (bits + 1) * rows], bits)
        if bits
        else blocks[bits * rows : (bits + 1) * rows]
        for bits in range(QUAD)
    ]
    return jnp.stack(
        [pick(place, [got[slot ^ here] for here in range(QUAD)]) for slot in range(QUAD)], axis=2
    )


def layer_norm(stream, gain_row, bias_row):
    average = jnp.mean(stream, axis=-1, keepdims=True)
    centered = stream - average
    variance = jnp.mean(centered * centered, axis=-1, keepdims=True)
    return centered * lax.rsqrt(variance + EPSILON) * gain_row + bias_row


def dot_nn(left, right):
    return lax.dot_general(left, right, (((1,), (0,)), ((), ())), preferred_element_type=F32)


def dot_nt(left, right):
    return lax.dot_general(left, right, (((1,), (1,)), ((), ())), preferred_element_type=F32)


def dot_tn(left, right):
    return lax.dot_general(left, right, (((0,), (0,)), ((), ())), preferred_element_type=F32)


def split_heads(packed, group_size):
    row_count, columns = packed.shape
    head_count = columns // (3 * HD)
    shaped = packed.reshape(row_count // group_size, group_size, 3, head_count, HD)
    return shaped[:, :, 0], shaped[:, :, 1], shaped[:, :, 2]


def causal_scores(queries, keys_all, places):
    scores = jnp.einsum(
        "gihe,gjhe->ghij", queries, keys_all, preferred_element_type=F32
    ) * HD ** (-0.5)
    return jnp.where(places[:, None] >= places[None, :], scores, NEGATIVE)


def attend_forward(packed, places):
    queries, keys_all, values_all = split_heads(packed, places.shape[0])
    scores = causal_scores(queries, keys_all, places)
    row_max = jnp.max(scores, axis=-1, keepdims=True)
    shifted = jnp.exp(scores - row_max)
    softened = shifted / jnp.sum(shifted, axis=-1, keepdims=True)
    mixture = jnp.einsum(
        "ghij,gjhe->gihe", softened.astype(BF16), values_all, preferred_element_type=F32
    )
    return mixture.reshape(packed.shape[0], -1).astype(BF16), softened


def attend_backward(packed, softened, grad_mix, places):
    queries, keys_all, values_all = split_heads(packed, places.shape[0])
    grad_heads = grad_mix.reshape(queries.shape)
    grad_soft = jnp.einsum(
        "gihe,gjhe->ghij", grad_heads, values_all, preferred_element_type=F32
    )
    centre = jnp.sum(grad_soft * softened, axis=-1, keepdims=True)
    grad_scores = (softened * (grad_soft - centre)).astype(BF16)
    grad_values = jnp.einsum(
        "ghij,gihe->gjhe", softened.astype(BF16), grad_heads, preferred_element_type=F32
    )
    grad_queries = jnp.einsum(
        "ghij,gjhe->gihe", grad_scores, keys_all, preferred_element_type=F32
    ) * HD ** (-0.5)
    grad_keys = jnp.einsum(
        "ghij,gihe->gjhe", grad_scores, queries, preferred_element_type=F32
    ) * HD ** (-0.5)
    row_count = packed.shape[0]
    return jnp.concatenate(
        [part.reshape(row_count, -1) for part in (grad_queries, grad_keys, grad_values)], axis=1
    ).astype(BF16)


def layer_forward(stream, weights, gain_rows, bias_rows, norm_index, places, widen, narrow):
    joint_proj, output_proj, upward, downward = weights
    normed_all = widen(
        layer_norm(stream, gain_rows[norm_index], bias_rows[norm_index]).astype(BF16)
    )
    packed = dot_nn(normed_all, joint_proj).astype(BF16)
    mixture, softened = attend_forward(packed, places)
    middle = stream + narrow(dot_nt(mixture, output_proj))
    second_all = widen(
        layer_norm(middle, gain_rows[norm_index + 1], bias_rows[norm_index + 1]).astype(BF16)
    )
    hidden = dot_nn(second_all, upward)
    active = jax.nn.gelu(hidden).astype(BF16)
    outcome = middle + narrow(dot_nt(active, downward))
    return (
        outcome,
        (stream, normed_all, packed, mixture, softened, middle, second_all, hidden, active),
    )


def layer_backward(grad_layer, saved, weights, gain_rows, bias_rows, norm_index, places, widen, narrow):
    stream, normed_all, packed, mixture, softened, middle, second_all, hidden, active = saved
    joint_proj, output_proj, upward, downward = weights
    grad_all = widen(grad_layer.astype(BF16))
    grad_active = dot_nn(grad_all, downward)
    gelu_value, gelu_pull = jax.vjp(jax.nn.gelu, hidden)
    grad_hidden = gelu_pull(grad_active)[0].astype(BF16)
    grad_second = narrow(dot_nt(grad_hidden, upward))
    norm_value, second_pull = jax.vjp(
        layer_norm, middle, gain_rows[norm_index + 1], bias_rows[norm_index + 1]
    )
    grad_middle_norm, grad_gain_two, grad_bias_two = second_pull(grad_second)
    grad_middle = grad_layer + grad_middle_norm
    grad_branch = widen(grad_middle.astype(BF16))
    grad_mix = dot_nn(grad_branch, output_proj).astype(BF16)
    grad_packed = attend_backward(packed, softened, grad_mix, places)
    grad_normed = narrow(dot_nt(grad_packed, joint_proj))
    first_value, first_pull = jax.vjp(
        layer_norm, stream, gain_rows[norm_index], bias_rows[norm_index]
    )
    grad_stream_norm, grad_gain_one, grad_bias_one = first_pull(grad_normed)
    grad_stream = grad_middle + grad_stream_norm
    grad_down = dot_tn(grad_all, active)
    grad_up = dot_tn(second_all, grad_hidden)
    grad_output = dot_tn(grad_branch, mixture)
    grad_joint = dot_tn(normed_all, grad_packed)
    return (
        grad_stream,
        (grad_joint, grad_output, grad_up, grad_down),
        (grad_gain_one, grad_gain_two),
        (grad_bias_one, grad_bias_two),
    )


def norm_forward(stream, gain_row, bias_row):
    centered = stream - jnp.mean(stream, axis=-1, keepdims=True)
    scale = lax.rsqrt(jnp.mean(centered * centered, axis=-1, keepdims=True) + EPSILON)
    unit = centered * scale
    return unit * gain_row + bias_row, unit, scale


def norm_backward(grad_out, unit, scale, gain_row):
    grad_unit = grad_out * gain_row
    first = jnp.mean(grad_unit, axis=-1, keepdims=True)
    second = jnp.mean(grad_unit * unit, axis=-1, keepdims=True)
    grad_in = scale * (grad_unit - first - unit * second)
    grad_gain = jnp.sum(grad_out * unit, axis=0, keepdims=True)
    grad_bias = jnp.sum(grad_out, axis=0, keepdims=True)
    return grad_in, grad_gain, grad_bias


GELU_A = 0.7978845608028654
GELU_B = 0.044715
TILE = 256
BAND = 128
PAIR = 2 * HD


def local_body(
    bound_ref, masked_ref, spread_ref, cotangent_ref, gain_ref, bias_ref,
    attend_own_ref, attend_other_ref, forward_own_ref, forward_other_ref,
    result_ref, grad_ref, grad_low_ref, normed_ref, second_ref, grad_out_ref, branch_ref,
    packed_own_ref, packed_other_ref, mixture_own_ref, mixture_other_ref,
    active_own_ref, active_other_ref, hidden_own_ref, hidden_other_ref, norms_ref,
    probs_ref,
):
    rows = masked_ref.shape[0]
    wide = mixture_own_ref.shape[1]
    hidden_width = active_own_ref.shape[1]
    attends = (attend_own_ref, attend_other_ref)
    forwards = (forward_own_ref, forward_other_ref)
    grad_packs = (packed_own_ref, packed_other_ref)
    mixtures = (mixture_own_ref, mixture_other_ref)
    actives = (active_own_ref, active_other_ref)
    hiddens = (hidden_own_ref, hidden_other_ref)
    bands = rows // BAND
    pairs = wide // PAIR

    row = pl.program_id(0) * rows + lax.broadcasted_iota(jnp.int32, (rows, 1), 0)
    keep = (row < bound_ref[0]).astype(F32)
    stream = masked_ref[...].astype(F32) + spread_ref[...].astype(F32)
    gain_one, gain_two = gain_ref[2:3, :], gain_ref[3:4, :]
    normed, unit_one, scale_one = norm_forward(stream, gain_one, bias_ref[2:3, :])
    normed = normed.astype(BF16)
    normed_ref[...] = normed
    packs = [dot_nn(normed, attend[:, : 3 * wide]).astype(BF16) for attend in attends]

    lanes = lax.broadcasted_iota(jnp.int32, (BAND, PAIR), 1)
    low_head = lanes < HD
    down_rows = lax.broadcasted_iota(jnp.int32, (2 * BAND, BAND), 0) % BAND
    key_rows = lax.broadcasted_iota(jnp.int32, (2 * BAND, BAND), 1)
    allowed = (down_rows // P_SIZE == key_rows // P_SIZE) & (down_rows >= key_rows)

    def apart(pair_values):
        zero = jnp.zeros_like(pair_values)
        return jnp.concatenate(
            [jnp.where(low_head, pair_values, zero), jnp.where(low_head, zero, pair_values)], axis=0
        )

    def joined(stacked):
        return jnp.where(low_head, stacked[:BAND], stacked[BAND:])

    def piece(values_in, band, part, pair):
        start = part * wide + pair * PAIR
        return values_in[band * BAND : (band + 1) * BAND, start : start + PAIR]

    scale = HD ** (-0.5)
    for side in range(2):
        for band in range(bands):
            for pair in range(pairs):
                queries = apart(piece(packs[side], band, 0, pair)) * jnp.asarray(scale, BF16)
                scores = dot_nt(queries, piece(packs[side], band, 1, pair))
                scores = jnp.where(allowed, scores, NEGATIVE)
                shifted = jnp.exp(scores - jnp.max(scores, axis=-1, keepdims=True))
                probs = shifted / jnp.sum(shifted, axis=-1, keepdims=True)
                probs_ref[(side * bands + band) * pairs + pair] = probs
                mixed = dot_nn(probs.astype(BF16), piece(packs[side], band, 2, pair))
                mixtures[side][
                    band * BAND : (band + 1) * BAND, pair * PAIR : (pair + 1) * PAIR
                ] = joined(mixed).astype(BF16)

    middle = stream
    for side in range(2):
        middle = middle + dot_nt(mixtures[side][...], attends[side][:, 3 * wide :])
    second, unit_two, scale_two = norm_forward(middle, gain_two, bias_ref[3:4, :])
    second = second.astype(BF16)
    second_ref[...] = second
    grad_final = cotangent_ref[...].astype(F32) * keep
    grad_out = grad_final.astype(BF16)
    grad_out_ref[...] = grad_out

    lifted = jnp.zeros_like(middle)
    grad_second = jnp.zeros_like(middle)
    chunk = min(768, hidden_width)
    for side in range(2):
        for start in range(0, hidden_width, chunk):
            upward = forwards[side][:, start : start + chunk]
            downward = forwards[side][:, hidden_width + start : hidden_width + start + chunk]
            hidden = dot_nn(second, upward)
            square = hidden * hidden
            bent = jnp.tanh(GELU_A * hidden * (1.0 + GELU_B * square))
            half = 0.5 * (1.0 + bent)
            active = (hidden * half).astype(BF16)
            slope = half + 0.5 * hidden * (1.0 - bent * bent) * GELU_A * (1.0 + 3.0 * GELU_B * square)
            actives[side][:, start : start + chunk] = active
            lifted = lifted + dot_nt(active, downward)
            grad_hidden = (dot_nn(grad_out, downward) * slope).astype(BF16)
            hiddens[side][:, start : start + chunk] = grad_hidden
            grad_second = grad_second + dot_nt(grad_hidden, upward)
    result_ref[...] = (middle + lifted).astype(BF16)

    grad_in, gain_grad_two, bias_grad_two = norm_backward(grad_second, unit_two, scale_two, gain_two)
    grad_middle = grad_final + grad_in
    branch = grad_middle.astype(BF16)
    branch_ref[...] = branch
    grad_normed = jnp.zeros_like(middle)
    for side in range(2):
        grad_mix = dot_nn(branch, attends[side][:, 3 * wide :]).astype(BF16)
        for band in range(bands):
            for pair in range(pairs):
                probs = probs_ref[(side * bands + band) * pairs + pair]
                grad_pair = apart(piece(grad_mix, band, 0, pair))
                grad_soft = dot_nt(grad_pair, piece(packs[side], band, 2, pair))
                centre = jnp.sum(grad_soft * probs, axis=-1, keepdims=True)
                grad_scores = (probs * (grad_soft - centre)).astype(BF16)
                queries = apart(piece(packs[side], band, 0, pair))
                grads = (
                    joined(dot_nn(grad_scores, piece(packs[side], band, 1, pair))) * scale,
                    dot_tn(grad_scores, queries) * scale,
                    dot_tn(probs.astype(BF16), grad_pair),
                )
                for part in range(3):
                    first = part * wide + pair * PAIR
                    grad_packs[side][band * BAND : (band + 1) * BAND, first : first + PAIR] = (
                        grads[part].astype(BF16)
                    )
        grad_normed = grad_normed + dot_nt(grad_packs[side][...], attends[side][:, : 3 * wide])
    grad_in, gain_grad_one, bias_grad_one = norm_backward(grad_normed, unit_one, scale_one, gain_one)
    grad_stream = grad_middle + grad_in
    grad_ref[...] = grad_stream
    grad_low_ref[...] = grad_stream.astype(BF16)

    @pl.when(pl.program_id(0) == 0)
    def _():
        norms_ref[...] = jnp.zeros_like(norms_ref)

    for place, value in enumerate((gain_grad_one, gain_grad_two, bias_grad_one, bias_grad_two)):
        norms_ref[place : place + 1, :] += value


def local_layer(bound, masked_low, spread, cotangent, gain_rows, bias_rows, attends, forwards):
    rows = masked_low.shape[0]
    wide = attends[0].shape[1] // 4
    hidden_width = forwards[0].shape[1] // 2
    tiled = lambda width: pl.BlockSpec((TILE, width), lambda i: (i, 0))
    fixed = lambda array: pl.BlockSpec(
        array.shape, lambda i: (0, 0), pipeline_mode=pl.Buffered(1)
    )
    widths = (
        [(D, BF16), (D, F32)] + [(D, BF16)] * 5 + [(3 * wide, BF16)] * 2 + [(wide, BF16)] * 2
        + [(hidden_width, BF16)] * 4
    )
    flops = 8 * rows * D * 2 * (4 * wide + 2 * hidden_width)
    return pl.pallas_call(
        local_body,
        grid=(rows // TILE,),
        in_specs=[pl.BlockSpec(memory_space=pltpu.SMEM)]
        + [tiled(D)] * 3
        + [fixed(array) for array in (gain_rows, bias_rows, *attends, *forwards)],
        out_specs=[tiled(width) for width, _ in widths] + [pl.BlockSpec((8, D), lambda i: (0, 0))],
        out_shape=[jax.ShapeDtypeStruct((rows, width), kind) for width, kind in widths]
        + [jax.ShapeDtypeStruct((8, D), F32)],
        scratch_shapes=[
            pltpu.VMEM((2 * (TILE // BAND) * (wide // PAIR), 2 * BAND, BAND), F32)
        ],
        compiler_params=pltpu.CompilerParams(
            dimension_semantics=("arbitrary",), vmem_limit_bytes=58 * 1024 * 1024
        ),
        cost_estimate=pl.CostEstimate(
            flops=flops, transcendentals=rows * 2 * hidden_width, bytes_accessed=36 * 1024 * 1024
        ),
    )(bound, masked_low, spread, cotangent, gain_rows, bias_rows, *attends, *forwards)


def grads_body(first_blocks, left_one_ref, right_one_ref, left_two_ref, right_two_ref, out_ref, turned_ref):
    step = pl.program_id(0)

    @pl.when(step == 0)
    def _():
        turned_ref[...] = left_one_ref[...].T

    @pl.when(step == first_blocks)
    def _():
        turned_ref[...] = left_two_ref[...].T

    @pl.when(step < first_blocks)
    def _():
        out_ref[...] = dot_nn(turned_ref[...], right_one_ref[...]).astype(BF16)

    @pl.when(step >= first_blocks)
    def _():
        out_ref[...] = dot_nn(turned_ref[...], right_two_ref[...]).astype(BF16)


def weight_grads(left_one, right_one, left_two, right_two):
    rows, model = left_one.shape
    block = 384
    first, last = right_one.shape[1] // block, right_two.shape[1] // block
    whole = pl.BlockSpec((rows, model), lambda j: (0, 0), pipeline_mode=pl.Buffered(1))
    return pl.pallas_call(
        lambda *refs: grads_body(first, *refs),
        grid=(first + last,),
        in_specs=[
            whole,
            pl.BlockSpec((rows, block), lambda j: (0, jnp.minimum(j, first - 1))),
            whole,
            pl.BlockSpec((rows, block), lambda j: (0, jnp.maximum(j - first, 0))),
        ],
        out_specs=pl.BlockSpec((model, block), lambda j: (0, j)),
        out_shape=jax.ShapeDtypeStruct((model, (first + last) * block), BF16),
        scratch_shapes=[pltpu.VMEM((model, rows), BF16)],
        compiler_params=pltpu.CompilerParams(
            dimension_semantics=("arbitrary",), vmem_limit_bytes=32 * 1024 * 1024
        ),
        cost_estimate=pl.CostEstimate(
            flops=2 * rows * model * (first + last) * block,
            transcendentals=0,
            bytes_accessed=2 * (2 * rows * model + (rows + model) * (first + last) * block),
        ),
    )(left_one, right_one, left_two, right_two)


def shards(
    embedded,
    lengths,
    patch_proj,
    global_proj,
    qkv_weight,
    out_weight,
    up_weight,
    down_weight,
    norm_gain,
    norm_bias,
    cotangent,
):
    half_rows = embedded.shape[1]
    patch_rows = half_rows // P_SIZE
    shard_rows = qkv_weight.shape[1]
    proj_rows = patch_proj.shape[0]
    norm_part = norm_gain.shape[0]
    cells = 2 * line_size()
    heads_width = qkv_weight.shape[3]
    hidden_width = up_weight.shape[2]
    x_here = x_place()

    positions = lax.axis_index("tensor") * half_rows + jnp.arange(half_rows, dtype=jnp.int32)
    keep_mask = (positions < lengths[0]).astype(F32)[:, None]
    masked_low = (embedded[0].astype(F32) * keep_mask).astype(BF16)

    joint_part = jnp.transpose(qkv_weight, (0, 2, 1, 3))
    output_part = jnp.transpose(out_weight, (0, 2, 1))
    down_part = jnp.transpose(down_weight, (0, 2, 1))

    norm_row = jnp.pad(
        jnp.concatenate([norm_gain, norm_bias]).reshape(1, -1), ((0, 0), (0, D - 2 * norm_part))
    )
    queues = {"line": Queue(2), "y": Queue(2), "x": Queue(2)}
    patch_whole = line_y_gather(jnp.concatenate([patch_proj, norm_row], axis=0), queues)
    patch_whole = patch_whole.reshape(cells, proj_rows + 1, D)
    patch_mat = patch_whole[:, :proj_rows].reshape(cells * proj_rows, D)
    norm_cells = patch_whole[:, proj_rows, : 2 * norm_part]
    norm_all = quad_collect(
        jnp.broadcast_to(norm_cells[None], (QUAD,) + norm_cells.shape)
    )[0].astype(F32)
    gain_rows = norm_all[..., :norm_part].reshape(NORMS, D)
    bias_rows = norm_all[..., norm_part:].reshape(NORMS, D)

    def x_half(part):
        return part.reshape(part.shape[:-1] + (2, part.shape[-1] // 2))

    def global_part(layer):
        pieces = []
        for piece in (
            joint_part[layer, 0],
            joint_part[layer, 1],
            joint_part[layer, 2],
            output_part[layer],
            up_weight[layer],
            down_part[layer],
        ):
            halves = x_half(piece)
            pieces.append(halves)
        return jnp.concatenate(pieces, axis=-1)

    halves = global_part(0)
    own_half = lax.dynamic_index_in_dim(halves, x_here, 1, keepdims=False)
    their_half = lax.dynamic_index_in_dim(halves, 1 - x_here, 1, keepdims=False)
    global_shard = pair_up(own_half, flip_dp(their_half, 1), x_here)
    global_shard = global_shard.reshape(2 * shard_rows, -1)
    attend_columns = 2 * heads_width
    attend_shard, forward_shard = global_shard[:, :attend_columns], global_shard[:, attend_columns:]
    attend_whole = line_y_gather(attend_shard, queues).reshape(D, -1)
    forward_whole = line_y_gather(forward_shard, queues).reshape(D, -1)
    joint_columns = 3 * heads_width // 2
    first_weights = (
        attend_whole[:, :joint_columns],
        attend_whole[:, joint_columns:],
        forward_whole[:, : hidden_width // 2],
        forward_whole[:, hidden_width // 2 :],
    )
    spread_mat = line_y_gather(jnp.transpose(global_proj), queues).reshape(cells * proj_rows, D)

    local_attend = jnp.concatenate([joint_part[1, 0], joint_part[1, 1], joint_part[1, 2], output_part[1]], axis=-1)
    local_forward = jnp.concatenate([up_weight[1], down_part[1]], axis=-1)
    forward_own = dp_gather(local_forward, queues, False)
    attend_own = dp_gather(local_attend, queues, True)
    attends = (attend_own, flip_core(attend_own))
    forwards = (forward_own, flip_core(forward_own))

    patches_dealt = quad_deal(masked_low.reshape(patch_rows, cells, QUAD, proj_rows))
    patches_mat = patches_dealt.reshape(QUAD * patch_rows, cells * proj_rows)
    initial = quad_scatter(dot_nn(patches_mat, patch_mat))
    core = lax.axis_index("tensor")
    steps = jnp.arange(patch_rows, dtype=jnp.int32)
    global_places = jnp.concatenate([core * patch_rows + steps, (1 - core) * patch_rows + steps])
    global_out, first_saved = layer_forward(
        initial, first_weights, gain_rows, bias_rows, 0, global_places, quad_gather, quad_scatter
    )
    global_low = quad_gather(global_out.astype(BF16))
    spread_dealt = dot_nt(global_low, spread_mat).astype(BF16)
    spread = quad_collect(spread_dealt.reshape(QUAD * patch_rows, cells, proj_rows))
    spread = spread.reshape(half_rows, D)

    bound = jnp.clip(lengths - lax.axis_index("tensor") * half_rows, 0, half_rows)
    (
        outcome, grad_local, grad_low, normed, second, grad_out, branch, packed_own, packed_other,
        mixture_own, mixture_other, active_own, active_other, hidden_own, hidden_other, local_norms,
    ) = local_layer(bound, masked_low, spread, cotangent[0], gain_rows, bias_rows, attends, forwards)
    second_gains, second_biases = (local_norms[0], local_norms[1]), (local_norms[2], local_norms[3])
    forward_given = flip_core(weight_grads(second, hidden_other, grad_out, active_other))
    forward_kept = weight_grads(second, hidden_own, grad_out, active_own)
    forward_local = dp_scatter(forward_kept.astype(F32) + forward_given.astype(F32))
    attend_given = flip_core(weight_grads(normed, packed_other, branch, mixture_other))
    attend_kept = weight_grads(normed, packed_own, branch, mixture_own)
    attend_local = dp_scatter(attend_kept.astype(F32) + attend_given.astype(F32))

    grad_spread = grad_low.reshape(patch_rows, cells, QUAD, proj_rows)
    spread_grads = quad_deal(grad_spread).reshape(QUAD * patch_rows, cells * proj_rows)
    grad_global = quad_scatter(dot_nn(spread_grads, spread_mat))
    grad_proj = line_y_scatter(dot_tn(spread_grads, global_low).reshape(cells, proj_rows, D))
    grad_initial, first_grads, first_gains, first_biases = layer_backward(
        grad_global, first_saved, first_weights, gain_rows, bias_rows, 0, global_places, quad_gather, quad_scatter
    )
    forward_global = line_y_scatter(
        jnp.concatenate([first_grads[2], first_grads[3]], axis=1).reshape(cells, 2 * shard_rows, -1)
    )
    attend_global = line_y_scatter(
        jnp.concatenate([first_grads[0], first_grads[1]], axis=1).reshape(cells, 2 * shard_rows, -1)
    )
    grad_start = quad_gather(grad_initial.astype(BF16))
    grad_patch_mat = dot_tn(patches_mat, grad_start).reshape(cells, proj_rows, D)
    grad_patches = dot_nt(grad_start, patch_mat).astype(BF16)
    grad_patches = quad_collect(grad_patches.reshape(QUAD * patch_rows, cells, proj_rows))
    grad_patches = grad_patches.reshape(half_rows, D).astype(F32)
    grad_input = ((grad_local + grad_patches) * keep_mask).astype(BF16)[None]

    gain_grads = jnp.stack([first_gains[0], first_gains[1], second_gains[0], second_gains[1]])
    bias_grads = jnp.stack([first_biases[0], first_biases[1], second_biases[0], second_biases[1]])
    norm_grads = jnp.concatenate(
        [
            gain_grads.reshape(cells, QUAD, norm_part),
            bias_grads.reshape(cells, QUAD, norm_part),
        ],
        axis=2,
    )
    place = quad_place()
    norm_sum = lax.dynamic_index_in_dim(norm_grads, place, 1, keepdims=False)
    for bits in range(1, QUAD):
        piece = lax.dynamic_index_in_dim(norm_grads, place ^ bits, 1, keepdims=False)
        norm_sum = norm_sum + flip_quad(piece, bits)
    norm_rows = jnp.pad(norm_sum[:, None, :], ((0, 0), (0, 0), (0, D - 2 * norm_part)))
    patch_summed = line_y_scatter(jnp.concatenate([grad_patch_mat, norm_rows], axis=1))

    def x_restore(summed):
        shaped = summed.reshape(2, shard_rows, -1)
        own = lax.dynamic_index_in_dim(shaped, x_here, 0, keepdims=False)
        theirs = lax.dynamic_index_in_dim(shaped, 1 - x_here, 0, keepdims=False)
        return pair_up(own, flip_dp(theirs.astype(BF16), 1).astype(F32), x_here)

    attend_global = x_restore(attend_global)
    forward_global = x_restore(forward_global)

    def x_columns(source, start, width):
        return jnp.concatenate([source[0, :, start : start + width], source[1, :, start : start + width]], axis=1)

    half_heads, half_hidden = heads_width // 2, hidden_width // 2
    joint_out = jnp.stack(
        [
            jnp.stack([x_columns(attend_global, k * half_heads, half_heads) for k in range(3)], axis=1),
            attend_local[:, : 3 * heads_width].reshape(shard_rows, 3, heads_width),
        ]
    )
    output_out = jnp.stack(
        [
            jnp.transpose(x_columns(attend_global, 3 * half_heads, half_heads)),
            jnp.transpose(attend_local[:, 3 * heads_width :]),
        ]
    )
    up_out = jnp.stack([x_columns(forward_global, 0, half_hidden), forward_local[:, :hidden_width]])
    down_out = jnp.stack(
        [
            jnp.transpose(x_columns(forward_global, half_hidden, half_hidden)),
            jnp.transpose(forward_local[:, hidden_width:]),
        ]
    )
    return (
        outcome[None],
        grad_input,
        patch_summed[:proj_rows],
        jnp.transpose(grad_proj),
        joint_out,
        output_out,
        up_out,
        down_out,
        patch_summed[proj_rows, :norm_part],
        patch_summed[proj_rows, norm_part : 2 * norm_part],
    )


def solution(mesh):
    placed = (
        P("dp", "tensor", None),
        P("dp"),
        P(("dp", "tensor"), None),
        P(None, ("dp", "tensor")),
        P(None, "dp", None, "tensor"),
        P(None, "tensor", "dp"),
        P(None, "dp", "tensor"),
        P(None, "tensor", "dp"),
        P(("dp", "tensor")),
        P(("dp", "tensor")),
        P("dp", "tensor", None),
    )
    return jax.shard_map(
        shards,
        mesh=mesh,
        in_specs=placed,
        out_specs=(
            P("dp", "tensor", None),
            P("dp", "tensor", None),
            P(("dp", "tensor"), None),
            P(None, ("dp", "tensor")),
            P(None, "dp", None, "tensor"),
            P(None, "tensor", "dp"),
            P(None, "dp", "tensor"),
            P(None, "tensor", "dp"),
            P(("dp", "tensor")),
            P(("dp", "tensor")),
        ),
        check_vma=False,
    )
```

```python
import jax
import jax.numpy as jnp
from jax import lax
from jax.experimental import pallas as pl
from jax.experimental.pallas import tpu as pltpu
from jax.sharding import PartitionSpec as P

D = 768
HD = 64
P_SIZE = 8
NORMS = 4
QUAD = 4

EPSILON = 1e-05
NEGATIVE = -1e30
BF16 = jnp.bfloat16
F32 = jnp.float32


def dp_size():
    return lax.axis_size("dp")


def line_size():
    return dp_size() // 4


def x_place():
    return lax.axis_index("dp") % 2


def y_place():
    return (lax.axis_index("dp") // 2) % 2


def line_place():
    return lax.axis_index("dp") // 4


def quad_place():
    return x_place() * 2 + lax.axis_index("tensor")


def flip_dp(values_in, bit):
    return lax.ppermute(values_in, "dp", [(i, i ^ bit) for i in range(dp_size())])


def flip_core(values_in):
    return lax.ppermute(values_in, "tensor", [(0, 1), (1, 0)])


def flip_quad(values_in, bits):
    return lax.ppermute(
        values_in, ("dp", "tensor"), [(i, i ^ bits) for i in range(2 * dp_size())]
    )


def step_line(values_in, offset):
    count = dp_size()
    return lax.ppermute(values_in, "dp", [(i, (i + 4 * offset) % count) for i in range(count)])


def after(values_in, *earlier):
    return lax.optimization_barrier((values_in,) + earlier)[0]


def line_groups():
    return [[line * 4 + rest for line in range(line_size())] for rest in range(4)]


def pick(place, choices):
    if len(choices) == 2:
        return lax.select_n(place == 1, *choices)
    return lax.select_n(place, *choices)


class LineQueue:
    def __init__(self):
        self.arrived = [(), ()]

    def step(self, values_in):
        got = step_line(after(values_in, *self.arrived.pop(0)), 1)
        self.arrived.append((got,))
        return got

    def hold(self, *earlier):
        self.arrived[0] = self.arrived[0] + earlier


def line_gather(values_in, queue):
    count = line_size()
    if count > 4:
        return lax.all_gather(values_in, "dp", axis=0, axis_index_groups=line_groups())
    if count == 1:
        return values_in[None]
    got = [values_in]
    for _ in range(1, count):
        got.append(queue.step(got[-1]))
    place = line_place()
    return jnp.stack(
        [pick(place, [got[(here - slot) % count] for here in range(count)]) for slot in range(count)]
    )


def pair_up(own, other, place):
    return jnp.stack([pick(place, [own, other]), pick(place, [other, own])], axis=0)


def y_gather(lined):
    other = flip_dp(lined, 2)
    place = y_place()
    return jnp.stack([pick(place, [lined, other]), pick(place, [other, lined])], axis=1)


def line_scatter(parts):
    count = line_size()
    if count > 4:
        return lax.psum_scatter(
            parts.astype(F32), "dp", scatter_dimension=0, axis_index_groups=line_groups(), tiled=False
        )
    place = line_place()

    def slot(offset):
        return lax.dynamic_index_in_dim(parts, (place + count + offset) % count, 0, keepdims=False)

    total = slot(-1).astype(F32)
    for back in range(2, count + 1):
        total = slot(-back).astype(F32) + step_line(total.astype(BF16), 1).astype(F32)
    return total


def halve(parts, place, axis, bit):
    own = lax.dynamic_index_in_dim(parts, place, axis, keepdims=False)
    theirs = lax.dynamic_index_in_dim(parts, 1 - place, axis, keepdims=False)
    return own.astype(F32) + flip_dp(theirs.astype(BF16), bit).astype(F32)


def y_scatter(parts):
    return halve(parts.reshape((line_size(), 2) + parts.shape[1:]), y_place(), 1, 2)


def line_y_scatter(parts):
    return line_scatter(y_scatter(parts))


def quad_gather(values_in):
    return jnp.concatenate(
        [values_in] + [flip_quad(values_in, bits) for bits in range(1, QUAD)], axis=0
    )


def quad_scatter(partial_value):
    rows = partial_value.shape[0] // QUAD
    low = partial_value.astype(BF16)
    total = partial_value[:rows].astype(F32)
    for bits in range(1, QUAD):
        total = total + flip_quad(low[bits * rows : (bits + 1) * rows], bits).astype(F32)
    return total


def quad_deal(blocks):
    place = quad_place()
    taken = []
    for bits in range(QUAD):
        piece = lax.dynamic_index_in_dim(blocks, place ^ bits, 2, keepdims=False)
        taken.append(flip_quad(piece, bits) if bits else piece)
    return jnp.concatenate(taken, axis=0)


def quad_collect(blocks):
    rows = blocks.shape[0] // QUAD
    place = quad_place()
    got = [
        flip_quad(blocks[bits * rows : (bits + 1) * rows], bits)
        if bits
        else blocks[bits * rows : (bits + 1) * rows]
        for bits in range(QUAD)
    ]
    return jnp.stack(
        [pick(place, [got[slot ^ here] for here in range(QUAD)]) for slot in range(QUAD)], axis=2
    )


def layer_norm(stream, gain_row, bias_row):
    average = jnp.mean(stream, axis=-1, keepdims=True)
    centered = stream - average
    variance = jnp.mean(centered * centered, axis=-1, keepdims=True)
    return centered * lax.rsqrt(variance + EPSILON) * gain_row + bias_row


def dot_nn(left, right):
    return lax.dot_general(left, right, (((1,), (0,)), ((), ())), preferred_element_type=F32)


def dot_nt(left, right):
    return lax.dot_general(left, right, (((1,), (1,)), ((), ())), preferred_element_type=F32)


def dot_tn(left, right):
    return lax.dot_general(left, right, (((0,), (0,)), ((), ())), preferred_element_type=F32)


def split_heads(packed, group_size):
    row_count, columns = packed.shape
    head_count = columns // (3 * HD)
    shaped = packed.reshape(row_count // group_size, group_size, 3, head_count, HD)
    return shaped[:, :, 0], shaped[:, :, 1], shaped[:, :, 2]


def causal_scores(queries, keys_all, places):
    scores = jnp.einsum(
        "gihe,gjhe->ghij", queries, keys_all, preferred_element_type=F32
    ) * HD ** (-0.5)
    return jnp.where(places[:, None] >= places[None, :], scores, NEGATIVE)


def attend_forward(packed, places):
    queries, keys_all, values_all = split_heads(packed, places.shape[0])
    scores = causal_scores(queries, keys_all, places)
    row_max = jnp.max(scores, axis=-1, keepdims=True)
    shifted = jnp.exp(scores - row_max)
    softened = shifted / jnp.sum(shifted, axis=-1, keepdims=True)
    mixture = jnp.einsum(
        "ghij,gjhe->gihe", softened.astype(BF16), values_all, preferred_element_type=F32
    )
    return mixture.reshape(packed.shape[0], -1).astype(BF16), softened


def attend_backward(packed, softened, grad_mix, places):
    queries, keys_all, values_all = split_heads(packed, places.shape[0])
    grad_heads = grad_mix.reshape(queries.shape)
    grad_soft = jnp.einsum(
        "gihe,gjhe->ghij", grad_heads, values_all, preferred_element_type=F32
    )
    centre = jnp.sum(grad_soft * softened, axis=-1, keepdims=True)
    grad_scores = (softened * (grad_soft - centre)).astype(BF16)
    grad_values = jnp.einsum(
        "ghij,gihe->gjhe", softened.astype(BF16), grad_heads, preferred_element_type=F32
    )
    grad_queries = jnp.einsum(
        "ghij,gjhe->gihe", grad_scores, keys_all, preferred_element_type=F32
    ) * HD ** (-0.5)
    grad_keys = jnp.einsum(
        "ghij,gihe->gjhe", grad_scores, queries, preferred_element_type=F32
    ) * HD ** (-0.5)
    row_count = packed.shape[0]
    return jnp.concatenate(
        [part.reshape(row_count, -1) for part in (grad_queries, grad_keys, grad_values)], axis=1
    ).astype(BF16)


def layer_forward(stream, attend_of, forward_of, gain_rows, bias_rows, norm_index, places):
    normed = layer_norm(stream, gain_rows[norm_index], bias_rows[norm_index]).astype(BF16)
    normed_all = quad_gather(normed)
    joint_proj, output_proj = attend_of()
    packed = dot_nn(normed_all, joint_proj).astype(BF16)
    mixture, softened = attend_forward(packed, places)
    middle = stream + quad_scatter(dot_nt(mixture, output_proj))
    second_all = quad_gather(
        layer_norm(middle, gain_rows[norm_index + 1], bias_rows[norm_index + 1]).astype(BF16)
    )
    upward, downward = forward_of(normed_all)
    hidden = dot_nn(second_all, upward)
    active = jax.nn.gelu(hidden).astype(BF16)
    outcome = middle + quad_scatter(dot_nt(active, downward))
    return (
        outcome,
        (stream, normed_all, packed, mixture, softened, middle, second_all, hidden, active),
        (joint_proj, output_proj, upward, downward),
    )


def layer_backward(grad_layer, saved, weights, gain_rows, bias_rows, norm_index, places, ties):
    stream, normed_all, packed, mixture, softened, middle, second_all, hidden, active = saved
    joint_proj, output_proj, upward, downward = weights
    grad_all = quad_gather(after(grad_layer.astype(BF16), *ties[0]))
    grad_active = dot_nn(grad_all, downward)
    gelu_value, gelu_pull = jax.vjp(jax.nn.gelu, hidden)
    grad_hidden = gelu_pull(grad_active)[0].astype(BF16)
    grad_second = quad_scatter(after(dot_nt(grad_hidden, upward), *ties[1]))
    forward_grads = jnp.concatenate(
        [dot_tn(second_all, grad_hidden).astype(BF16), dot_tn(grad_all, active).astype(BF16)], axis=1
    )
    norm_value, second_pull = jax.vjp(
        layer_norm, middle, gain_rows[norm_index + 1], bias_rows[norm_index + 1]
    )
    grad_middle_norm, grad_gain_two, grad_bias_two = second_pull(grad_second)
    grad_middle = grad_layer + grad_middle_norm
    grad_branch = quad_gather(after(grad_middle.astype(BF16), *ties[2]))
    grad_mix = dot_nn(grad_branch, output_proj).astype(BF16)
    forward_half = y_scatter(forward_grads.reshape(ties[5] + (-1,)))
    grad_packed = attend_backward(packed, softened, grad_mix, places)
    grad_normed = quad_scatter(after(dot_nt(grad_packed, joint_proj), *ties[3]))
    attend_grads = jnp.concatenate(
        [dot_tn(normed_all, grad_packed).astype(BF16), dot_tn(grad_branch, mixture).astype(BF16)], axis=1
    )
    first_value, first_pull = jax.vjp(
        layer_norm, stream, gain_rows[norm_index], bias_rows[norm_index]
    )
    grad_stream_norm, grad_gain_one, grad_bias_one = first_pull(grad_normed)
    grad_stream = grad_middle + grad_stream_norm
    grad_start = quad_gather(after(grad_stream.astype(BF16), *ties[4]))
    attend_half = y_scatter(attend_grads.reshape(ties[5] + (-1,)))
    return (
        grad_start,
        attend_half,
        forward_half,
        (grad_gain_one, grad_gain_two),
        (grad_bias_one, grad_bias_two),
    )


def norm_forward(stream, gain_row, bias_row):
    centered = stream - jnp.mean(stream, axis=-1, keepdims=True)
    scale = lax.rsqrt(jnp.mean(centered * centered, axis=-1, keepdims=True) + EPSILON)
    unit = centered * scale
    return unit * gain_row + bias_row, unit, scale


def norm_backward(grad_out, unit, scale, gain_row):
    grad_unit = grad_out * gain_row
    first = jnp.mean(grad_unit, axis=-1, keepdims=True)
    second = jnp.mean(grad_unit * unit, axis=-1, keepdims=True)
    grad_in = scale * (grad_unit - first - unit * second)
    grad_gain = jnp.sum(grad_out * unit, axis=0, keepdims=True)
    grad_bias = jnp.sum(grad_out, axis=0, keepdims=True)
    return grad_in, grad_gain, grad_bias


GELU_A = 0.7978845608028654
GELU_B = 0.044715
TILE = 256
BAND = 128
PAIR = 2 * HD


def local_body(
    bound_ref, masked_ref, spread_ref, cotangent_ref, gain_ref, bias_ref,
    first_ref, last_ref,
    result_ref, grad_ref, grad_low_ref, normed_ref, second_ref, grad_out_ref, branch_ref,
    joint_first_ref, joint_last_ref, value_first_ref, value_last_ref,
    mixture_first_ref, mixture_last_ref, hidden_first_ref, hidden_last_ref,
    active_first_ref, active_last_ref, norms_ref,
    probs_ref,
):
    rows = masked_ref.shape[0]
    wide = mixture_first_ref.shape[1]
    hidden_width = active_first_ref.shape[1]
    grad_joints = (joint_first_ref, joint_last_ref)
    grad_values = (value_first_ref, value_last_ref)
    mixtures = (mixture_first_ref, mixture_last_ref)
    actives = (active_first_ref, active_last_ref)
    hiddens = (hidden_first_ref, hidden_last_ref)

    def weight(side, start, stop):
        return (first_ref, last_ref)[side][:, 0, :, start:stop].reshape(D, stop - start)

    bands = rows // BAND
    pairs = wide // PAIR

    row = pl.program_id(0) * rows + lax.broadcasted_iota(jnp.int32, (rows, 1), 0)
    keep = (row < bound_ref[0]).astype(F32)
    stream = masked_ref[...].astype(F32) + spread_ref[...].astype(F32)
    gain_one, gain_two = gain_ref[2:3, :], gain_ref[3:4, :]
    normed, unit_one, scale_one = norm_forward(stream, gain_one, bias_ref[2:3, :])
    normed = normed.astype(BF16)
    normed_ref[...] = normed
    packs = [dot_nn(normed, weight(side, 0, 3 * wide)).astype(BF16) for side in range(2)]

    lanes = lax.broadcasted_iota(jnp.int32, (BAND, PAIR), 1)
    low_head = lanes < HD
    down_rows = lax.broadcasted_iota(jnp.int32, (2 * BAND, BAND), 0) % BAND
    key_rows = lax.broadcasted_iota(jnp.int32, (2 * BAND, BAND), 1)
    allowed = (down_rows // P_SIZE == key_rows // P_SIZE) & (down_rows >= key_rows)

    def apart(pair_values):
        zero = jnp.zeros_like(pair_values)
        return jnp.concatenate(
            [jnp.where(low_head, pair_values, zero), jnp.where(low_head, zero, pair_values)], axis=0
        )

    def joined(stacked):
        return jnp.where(low_head, stacked[:BAND], stacked[BAND:])

    def piece(values_in, band, part, pair):
        start = part * wide + pair * PAIR
        return values_in[band * BAND : (band + 1) * BAND, start : start + PAIR]

    scale = HD ** (-0.5)
    for side in range(2):
        for band in range(bands):
            for pair in range(pairs):
                queries = apart(piece(packs[side], band, 0, pair)) * jnp.asarray(scale, BF16)
                scores = dot_nt(queries, piece(packs[side], band, 1, pair))
                scores = jnp.where(allowed, scores, NEGATIVE)
                shifted = jnp.exp(scores - jnp.max(scores, axis=-1, keepdims=True))
                probs = shifted / jnp.sum(shifted, axis=-1, keepdims=True)
                probs_ref[(side * bands + band) * pairs + pair] = probs
                mixed = dot_nn(probs.astype(BF16), piece(packs[side], band, 2, pair))
                mixtures[side][
                    band * BAND : (band + 1) * BAND, pair * PAIR : (pair + 1) * PAIR
                ] = joined(mixed).astype(BF16)

    middle = stream
    for side in range(2):
        middle = middle + dot_nt(mixtures[side][...], weight(side, 3 * wide, 4 * wide))
    second, unit_two, scale_two = norm_forward(middle, gain_two, bias_ref[3:4, :])
    second = second.astype(BF16)
    second_ref[...] = second
    grad_final = cotangent_ref[...].astype(F32) * keep
    grad_out = grad_final.astype(BF16)
    grad_out_ref[...] = grad_out

    lifted = jnp.zeros_like(middle)
    grad_second = jnp.zeros_like(middle)
    chunk = min(768, hidden_width)
    for side in range(2):
        for start in range(0, hidden_width, chunk):
            first = 4 * wide + start
            upward = weight(side, first, first + chunk)
            downward = weight(side, first + hidden_width, first + hidden_width + chunk)
            hidden = dot_nn(second, upward)
            square = hidden * hidden
            bent = jnp.tanh(GELU_A * hidden * (1.0 + GELU_B * square))
            half = 0.5 * (1.0 + bent)
            active = (hidden * half).astype(BF16)
            slope = half + 0.5 * hidden * (1.0 - bent * bent) * GELU_A * (1.0 + 3.0 * GELU_B * square)
            actives[side][:, start : start + chunk] = active
            lifted = lifted + dot_nt(active, downward)
            grad_hidden = (dot_nn(grad_out, downward) * slope).astype(BF16)
            hiddens[side][:, start : start + chunk] = grad_hidden
            grad_second = grad_second + dot_nt(grad_hidden, upward)
    result_ref[...] = (middle + lifted).astype(BF16)

    grad_in, gain_grad_two, bias_grad_two = norm_backward(grad_second, unit_two, scale_two, gain_two)
    grad_middle = grad_final + grad_in
    branch = grad_middle.astype(BF16)
    branch_ref[...] = branch
    grad_normed = jnp.zeros_like(middle)
    for side in range(2):
        grad_mix = dot_nn(branch, weight(side, 3 * wide, 4 * wide)).astype(BF16)
        for band in range(bands):
            for pair in range(pairs):
                probs = probs_ref[(side * bands + band) * pairs + pair]
                grad_pair = apart(piece(grad_mix, band, 0, pair))
                grad_soft = dot_nt(grad_pair, piece(packs[side], band, 2, pair))
                centre = jnp.sum(grad_soft * probs, axis=-1, keepdims=True)
                grad_scores = (probs * (grad_soft - centre)).astype(BF16)
                queries = apart(piece(packs[side], band, 0, pair))
                grads = (
                    joined(dot_nn(grad_scores, piece(packs[side], band, 1, pair))) * scale,
                    dot_tn(grad_scores, queries) * scale,
                    dot_tn(probs.astype(BF16), grad_pair),
                )
                rows_here = slice(band * BAND, (band + 1) * BAND)
                for part in range(2):
                    first = part * wide + pair * PAIR
                    grad_joints[side][rows_here, first : first + PAIR] = grads[part].astype(BF16)
                grad_values[side][rows_here, pair * PAIR : (pair + 1) * PAIR] = grads[2].astype(BF16)
        grad_normed = grad_normed + dot_nt(grad_joints[side][...], weight(side, 0, 2 * wide))
        grad_normed = grad_normed + dot_nt(grad_values[side][...], weight(side, 2 * wide, 3 * wide))
    grad_in, gain_grad_one, bias_grad_one = norm_backward(grad_normed, unit_one, scale_one, gain_one)
    grad_stream = grad_middle + grad_in
    grad_ref[...] = grad_stream
    grad_low_ref[...] = grad_stream.astype(BF16)

    @pl.when(pl.program_id(0) == 0)
    def _():
        norms_ref[...] = jnp.zeros_like(norms_ref)

    for place, value in enumerate((gain_grad_one, gain_grad_two, bias_grad_one, bias_grad_two)):
        norms_ref[place : place + 1, :] += value


def local_layer(bound, masked_low, spread, cotangent, gain_rows, bias_rows, weights, wide):
    rows = masked_low.shape[0]
    hidden_width = weights.shape[3] // 2 - 2 * wide
    tiled = lambda width: pl.BlockSpec((TILE, width), lambda i: (i, 0))
    fixed = lambda array: pl.BlockSpec(
        array.shape, lambda i: (0, 0), pipeline_mode=pl.Buffered(1)
    )
    widths = (
        [(D, BF16), (D, F32)] + [(D, BF16)] * 5 + [(2 * wide, BF16)] * 2 + [(wide, BF16)] * 4
        + [(hidden_width, BF16)] * 4
    )
    flops = 8 * rows * D * 2 * (4 * wide + 2 * hidden_width)
    return pl.pallas_call(
        local_body,
        grid=(rows // TILE,),
        in_specs=[pl.BlockSpec(memory_space=pltpu.SMEM)]
        + [tiled(D)] * 3
        + [fixed(array) for array in (gain_rows, bias_rows)]
        + [
            pl.BlockSpec(
                (weights.shape[0], 1) + weights.shape[2:],
                lambda i, side=side: (0, side, 0, 0),
                pipeline_mode=pl.Buffered(1),
            )
            for side in range(2)
        ],
        out_specs=[tiled(width) for width, _ in widths] + [pl.BlockSpec((8, D), lambda i: (0, 0))],
        out_shape=[jax.ShapeDtypeStruct((rows, width), kind) for width, kind in widths]
        + [jax.ShapeDtypeStruct((8, D), F32)],
        scratch_shapes=[
            pltpu.VMEM((2 * (TILE // BAND) * (wide // PAIR), 2 * BAND, BAND), F32)
        ],
        compiler_params=pltpu.CompilerParams(
            dimension_semantics=("arbitrary",), vmem_limit_bytes=58 * 1024 * 1024
        ),
        cost_estimate=pl.CostEstimate(
            flops=flops, transcendentals=rows * 2 * hidden_width, bytes_accessed=36 * 1024 * 1024
        ),
    )(bound, masked_low, spread, cotangent, gain_rows, bias_rows, weights, weights)


def grads_body(
    normed_ref, branch_ref, second_ref, grad_out_ref,
    joint_first_ref, joint_last_ref, value_first_ref, value_last_ref,
    mixture_first_ref, mixture_last_ref, hidden_first_ref, hidden_last_ref,
    active_first_ref, active_last_ref, out_ref, turned_ref, branch_turned_ref,
):
    block, side = pl.program_id(0), pl.program_id(1)
    half = value_first_ref.shape[1]
    shape = out_ref.shape[:3]

    @pl.when((side == 0) & (block == 0))
    def _():
        turned_ref[...] = normed_ref[...].T
        branch_turned_ref[...] = branch_ref[...].T

    @pl.when((side == 0) & (block == 2))
    def _():
        turned_ref[...] = second_ref[...].T

    @pl.when((side == 0) & (block == 4))
    def _():
        turned_ref[...] = grad_out_ref[...].T

    def give(place, chosen, left_ref, right_ref, columns):
        @pl.when(chosen & (side == place))
        def _():
            product = dot_nn(left_ref[...], right_ref[...]).astype(BF16)
            out_ref[:, :, :, columns] = product.reshape(shape + (product.shape[1],))

    for place, (joint, value, mixture, hidden, active) in enumerate(
        (
            (joint_first_ref, value_first_ref, mixture_first_ref, hidden_first_ref, active_first_ref),
            (joint_last_ref, value_last_ref, mixture_last_ref, hidden_last_ref, active_last_ref),
        )
    ):
        give(place, block == 0, turned_ref, joint, slice(None))
        give(place, block == 1, turned_ref, value, slice(0, half))
        give(place, block == 1, branch_turned_ref, mixture, slice(half, 2 * half))
        give(place, (block == 2) | (block == 3), turned_ref, hidden, slice(None))
        give(place, block >= 4, turned_ref, active, slice(None))


def weight_grads(lefts, joints, values, mixtures, hiddens, actives, shape):
    rows, model = lefts[0].shape
    block = joints[0].shape[1]

    def given(array, first=None):
        if first is None:
            return pl.BlockSpec(array.shape, lambda b, s: (0, 0), pipeline_mode=pl.Buffered(1))
        return pl.BlockSpec((rows, block), lambda b, s: (0, jnp.clip(b - first, 0, 1)))

    arrays = (*lefts, *joints, *values, *mixtures, *hiddens, *actives)
    return pl.pallas_call(
        grads_body,
        grid=(shape[3] // block, 2),
        in_specs=[given(array) for array in (*lefts, *joints, *values, *mixtures)]
        + [given(array, 2) for array in hiddens]
        + [given(array, 4) for array in actives],
        out_specs=pl.BlockSpec((shape[0], 1, shape[2], block), lambda b, s: (0, s, 0, b)),
        out_shape=jax.ShapeDtypeStruct(shape, BF16),
        scratch_shapes=[pltpu.VMEM((model, rows), BF16)] * 2,
        compiler_params=pltpu.CompilerParams(
            dimension_semantics=("arbitrary", "arbitrary"), vmem_limit_bytes=48 * 1024 * 1024
        ),
        cost_estimate=pl.CostEstimate(
            flops=4 * rows * model * shape[3],
            transcendentals=0,
            bytes_accessed=2 * (4 * rows * model + 2 * (rows + model) * shape[3]),
        ),
    )(*arrays)


def shards(
    embedded,
    lengths,
    patch_proj,
    global_proj,
    qkv_weight,
    out_weight,
    up_weight,
    down_weight,
    norm_gain,
    norm_bias,
    cotangent,
):
    half_rows = embedded.shape[1]
    patch_rows = half_rows // P_SIZE
    shard_rows = qkv_weight.shape[1]
    proj_rows = patch_proj.shape[0]
    norm_part = norm_gain.shape[0]
    cells = 2 * line_size()
    heads_width = qkv_weight.shape[3]
    hidden_width = up_weight.shape[2]
    x_here = x_place()

    positions = lax.axis_index("tensor") * half_rows + jnp.arange(half_rows, dtype=jnp.int32)
    keep_mask = (positions < lengths[0]).astype(F32)[:, None]
    masked_low = jnp.where(keep_mask > 0, embedded[0], jnp.zeros_like(embedded[0]))
    masked_low = lax.optimization_barrier(masked_low)

    joint_part = jnp.transpose(qkv_weight, (0, 2, 1, 3))
    output_part = jnp.transpose(out_weight, (0, 2, 1))
    down_part = jnp.transpose(down_weight, (0, 2, 1))

    norm_row = jnp.pad(
        jnp.concatenate([norm_gain, norm_bias]).reshape(1, -1), ((0, 0), (0, D - 2 * norm_part))
    )
    local_shard = jnp.concatenate(
        [joint_part[1, 0], joint_part[1, 1], joint_part[1, 2], output_part[1], up_weight[1], down_part[1]],
        axis=-1,
    )
    local_whole = lax.all_gather(local_shard, ("dp", "tensor"), axis=0)

    patch_pieces = masked_low.reshape(patch_rows, cells, QUAD, proj_rows)
    patches_dealt = quad_deal(patch_pieces)
    queue = LineQueue()
    patch_lined = line_gather(jnp.concatenate([patch_proj, norm_row], axis=0), queue)
    patch_whole = y_gather(patch_lined)
    patch_whole = patch_whole.reshape(cells, proj_rows + 1, D)
    patch_mat = patch_whole[:, :proj_rows].reshape(cells * proj_rows, D)
    norm_cells = patch_whole[:, proj_rows, : 2 * norm_part]
    norm_all = quad_collect(
        jnp.broadcast_to(norm_cells[None], (QUAD,) + norm_cells.shape)
    )[0].astype(F32)
    gain_rows = norm_all[..., :norm_part].reshape(NORMS, D)
    bias_rows = norm_all[..., norm_part:].reshape(NORMS, D)
    gain_rows, bias_rows = lax.optimization_barrier((gain_rows, bias_rows))

    def x_half(part):
        return part.reshape(part.shape[:-1] + (2, part.shape[-1] // 2))

    def global_part(layer):
        pieces = []
        for piece in (
            joint_part[layer, 0],
            joint_part[layer, 1],
            joint_part[layer, 2],
            output_part[layer],
            up_weight[layer],
            down_part[layer],
        ):
            halves = x_half(piece)
            pieces.append(halves)
        return jnp.concatenate(pieces, axis=-1)

    halves = global_part(0)
    own_half = lax.dynamic_index_in_dim(halves, x_here, 1, keepdims=False)
    their_half = lax.dynamic_index_in_dim(halves, 1 - x_here, 1, keepdims=False)
    global_shard = pair_up(own_half, flip_dp(their_half, 1), x_here)
    global_shard = global_shard.reshape(2 * shard_rows, -1)
    attend_columns = 2 * heads_width
    attend_shard, forward_shard = global_shard[:, :attend_columns], global_shard[:, attend_columns:]
    attend_lined = line_gather(attend_shard, queue)
    forward_lined = line_gather(forward_shard, queue)
    spread_lined = line_gather(jnp.transpose(global_proj), queue)
    joint_columns = 3 * heads_width // 2

    patches_mat = patches_dealt.reshape(QUAD * patch_rows, cells * proj_rows)
    start_partial = dot_nn(patches_mat, patch_mat)
    initial = quad_scatter(start_partial)

    def attend_of():
        whole = y_gather(after(attend_lined, start_partial)).reshape(D, -1)
        return whole[:, :joint_columns], whole[:, joint_columns:]

    def forward_of(marker):
        whole = y_gather(after(forward_lined, marker)).reshape(D, -1)
        return whole[:, : hidden_width // 2], whole[:, hidden_width // 2 :]

    core = lax.axis_index("tensor")
    steps = jnp.arange(patch_rows, dtype=jnp.int32)
    global_places = jnp.concatenate([core * patch_rows + steps, (1 - core) * patch_rows + steps])
    global_out, first_saved, first_weights = layer_forward(
        initial, attend_of, forward_of, gain_rows, bias_rows, 0, global_places
    )
    spread_mat = y_gather(after(spread_lined, first_saved[6])).reshape(cells * proj_rows, D)
    global_low = quad_gather(global_out.astype(BF16))
    spread_dealt = dot_nt(global_low, spread_mat).astype(BF16)
    spread = quad_collect(spread_dealt.reshape(QUAD * patch_rows, cells, proj_rows))
    spread = spread.reshape(half_rows, D)

    dp = dp_size()
    whole_rows = shard_rows % 16 == 0
    local_weights = local_whole.reshape(dp, 2, shard_rows, -1)
    if not whole_rows:
        local_weights = jnp.transpose(local_weights, (1, 0, 2, 3)).reshape(1, 2, D, -1)
    bound = jnp.clip(lengths - lax.axis_index("tensor") * half_rows, 0, half_rows)
    (
        outcome, grad_local, grad_low, normed, second, grad_out, branch,
        *grad_factors, local_norms,
    ) = local_layer(bound, masked_low, spread, cotangent[0], gain_rows, bias_rows, local_weights, heads_width)
    second_gains, second_biases = (local_norms[0], local_norms[1]), (local_norms[2], local_norms[3])
    grad_spread = grad_low.reshape(patch_rows, cells, QUAD, proj_rows)
    spread_grads = quad_deal(grad_spread).reshape(QUAD * patch_rows, cells * proj_rows)
    factor_pairs = [grad_factors[k : k + 2] for k in range(0, 10, 2)]
    local_grads = weight_grads(
        (normed, branch, second, grad_out), *factor_pairs, local_weights.shape
    )
    spread_grads = after(spread_grads, local_grads)
    if not whole_rows:
        local_grads = jnp.transpose(local_grads.reshape(2, dp, shard_rows, -1), (1, 0, 2, 3))
    local_summed = lax.psum_scatter(
        local_grads.reshape(2 * dp, shard_rows, -1), ("dp", "tensor"), scatter_dimension=0
    ).astype(F32)

    grad_global = quad_scatter(dot_nn(spread_grads, spread_mat))
    proj_grads = dot_tn(spread_grads, global_low).astype(BF16).reshape(cells, proj_rows, D)
    proj_half = y_scatter(proj_grads)
    ties = ((), (), (), (), (), (cells, 2 * shard_rows))
    grad_start, attend_half, forward_half, first_gains, first_biases = layer_backward(
        grad_global, first_saved, first_weights, gain_rows, bias_rows, 0, global_places, ties
    )
    grad_proj = line_scatter(proj_half)
    forward_global = line_scatter(forward_half)
    attend_global = line_scatter(attend_half)
    grad_patch_mat = dot_tn(patches_mat, grad_start).astype(BF16).reshape(cells, proj_rows, D)
    grad_patches = dot_nt(grad_start, patch_mat).astype(BF16)
    grad_patches = quad_collect(grad_patches.reshape(QUAD * patch_rows, cells, proj_rows))
    grad_patches = grad_patches.reshape(half_rows, D).astype(F32)
    grad_input = ((grad_local + grad_patches) * keep_mask).astype(BF16)[None]

    gain_grads = jnp.stack([first_gains[0], first_gains[1], second_gains[0], second_gains[1]])
    bias_grads = jnp.stack([first_biases[0], first_biases[1], second_biases[0], second_biases[1]])
    norm_grads = jnp.concatenate(
        [
            gain_grads.reshape(cells, QUAD, norm_part),
            bias_grads.reshape(cells, QUAD, norm_part),
        ],
        axis=2,
    )
    place = quad_place()
    norm_sum = lax.dynamic_index_in_dim(norm_grads, place, 1, keepdims=False)
    for bits in range(1, QUAD):
        piece = lax.dynamic_index_in_dim(norm_grads, place ^ bits, 1, keepdims=False)
        norm_sum = norm_sum + flip_quad(piece, bits)
    norm_rows = jnp.pad(norm_sum[:, None, :].astype(BF16), ((0, 0), (0, 0), (0, D - 2 * norm_part)))
    patch_summed = line_y_scatter(jnp.concatenate([grad_patch_mat, norm_rows], axis=1))

    def x_restore(summed):
        shaped = summed.reshape(2, shard_rows, -1)
        own = lax.dynamic_index_in_dim(shaped, x_here, 0, keepdims=False)
        theirs = lax.dynamic_index_in_dim(shaped, 1 - x_here, 0, keepdims=False)
        return pair_up(own, flip_dp(theirs.astype(BF16), 1).astype(F32), x_here)

    attend_global = x_restore(attend_global)
    forward_global = x_restore(forward_global)

    def x_columns(source, start, width):
        return jnp.concatenate([source[0, :, start : start + width], source[1, :, start : start + width]], axis=1)

    half_heads, half_hidden = heads_width // 2, hidden_width // 2
    joint_out = jnp.stack(
        [
            jnp.stack([x_columns(attend_global, k * half_heads, half_heads) for k in range(3)], axis=1),
            local_summed[:, : 3 * heads_width].reshape(shard_rows, 3, heads_width),
        ]
    )
    output_out = jnp.stack(
        [
            jnp.transpose(x_columns(attend_global, 3 * half_heads, half_heads)),
            jnp.transpose(local_summed[:, 3 * heads_width : 4 * heads_width]),
        ]
    )
    up_out = jnp.stack([x_columns(forward_global, 0, half_hidden), local_summed[:, 4 * heads_width : 4 * heads_width + hidden_width]])
    down_out = jnp.stack(
        [
            jnp.transpose(x_columns(forward_global, half_hidden, half_hidden)),
            jnp.transpose(local_summed[:, 4 * heads_width + hidden_width :]),
        ]
    )
    return (
        outcome[None],
        grad_input,
        patch_summed[:proj_rows],
        jnp.transpose(grad_proj),
        joint_out,
        output_out,
        up_out,
        down_out,
        patch_summed[proj_rows, :norm_part],
        patch_summed[proj_rows, norm_part : 2 * norm_part],
    )


def solution(mesh):
    placed = (
        P("dp", "tensor", None),
        P("dp"),
        P(("dp", "tensor"), None),
        P(None, ("dp", "tensor")),
        P(None, "dp", None, "tensor"),
        P(None, "tensor", "dp"),
        P(None, "dp", "tensor"),
        P(None, "tensor", "dp"),
        P(("dp", "tensor")),
        P(("dp", "tensor")),
        P("dp", "tensor", None),
    )
    return jax.shard_map(
        shards,
        mesh=mesh,
        in_specs=placed,
        out_specs=(
            P("dp", "tensor", None),
            P("dp", "tensor", None),
            P(("dp", "tensor"), None),
            P(None, ("dp", "tensor")),
            P(None, "dp", None, "tensor"),
            P(None, "tensor", "dp"),
            P(None, "dp", "tensor"),
            P(None, "tensor", "dp"),
            P(("dp", "tensor")),
            P(("dp", "tensor")),
        ),
        check_vma=False,
    )
```

```python
import jax
import jax.numpy as jnp
from jax import lax
from jax.experimental import pallas as pl
from jax.experimental.pallas import tpu as pltpu
from jax.sharding import PartitionSpec as P

D = 768
HD = 64
P_SIZE = 8
NORMS = 4
QUAD = 4

EPSILON = 1e-05
NEGATIVE = -1e30
BF16 = jnp.bfloat16
F32 = jnp.float32


def dp_size():
    return lax.axis_size("dp")


def line_size():
    return dp_size() // 4


def x_place():
    return lax.axis_index("dp") % 2


def y_place():
    return (lax.axis_index("dp") // 2) % 2


def line_place():
    return lax.axis_index("dp") // 4


def quad_place():
    return x_place() * 2 + lax.axis_index("tensor")


def flip_dp(values_in, bit):
    return lax.ppermute(values_in, "dp", [(i, i ^ bit) for i in range(dp_size())])


def flip_core(values_in):
    return lax.ppermute(values_in, "tensor", [(0, 1), (1, 0)])


def flip_quad(values_in, bits):
    return lax.ppermute(
        values_in, ("dp", "tensor"), [(i, i ^ bits) for i in range(2 * dp_size())]
    )


def step_line(values_in, offset):
    count = dp_size()
    return lax.ppermute(values_in, "dp", [(i, (i + 4 * offset) % count) for i in range(count)])


def after(values_in, *earlier):
    return lax.optimization_barrier((values_in,) + earlier)[0]


def line_groups():
    return [[line * 4 + rest for line in range(line_size())] for rest in range(4)]


def pick(place, choices):
    if len(choices) == 2:
        return lax.select_n(place == 1, *choices)
    return lax.select_n(place, *choices)


class LineQueue:
    def __init__(self):
        self.arrived = [(), ()]

    def step(self, values_in):
        got = step_line(after(values_in, *self.arrived.pop(0)), 1)
        self.arrived.append((got,))
        return got

    def hold(self, *earlier):
        self.arrived[0] = self.arrived[0] + earlier


def line_pass(values_in, queue, holds=()):
    count = line_size()
    if count > 4:
        whole = lax.all_gather(values_in, "dp", axis=0, axis_index_groups=line_groups())
        return [whole[slot] for slot in range(count)]
    got = [values_in]
    for step in range(1, count):
        if step == count - 1 and holds:
            queue.hold(*holds)
        got.append(queue.step(got[-1]))
    return got


def line_place_blocks(got):
    count = len(got)
    if count == 1:
        return got[0][None]
    if count > 4:
        return jnp.stack(got)
    place = line_place()
    return jnp.stack(
        [pick(place, [got[(here - slot) % count] for here in range(count)]) for slot in range(count)]
    )


def line_gather(values_in, queue):
    return line_place_blocks(line_pass(values_in, queue))


def pair_up(own, other, place):
    return jnp.stack([pick(place, [own, other]), pick(place, [other, own])], axis=0)


def y_gather(lined):
    other = flip_dp(lined, 2)
    place = y_place()
    return jnp.stack([pick(place, [lined, other]), pick(place, [other, lined])], axis=1)


def line_scatter(parts, marks=None):
    count = line_size()
    if count > 4:
        return lax.psum_scatter(
            parts.astype(F32), "dp", scatter_dimension=0, axis_index_groups=line_groups(), tiled=False
        )
    place = line_place()

    def slot(offset):
        return lax.dynamic_index_in_dim(parts, (place + count + offset) % count, 0, keepdims=False)

    total = slot(-1).astype(F32)
    for back in range(2, count + 1):
        got = step_line(total.astype(BF16), 1)
        if marks is not None:
            marks.append(got)
        total = slot(-back).astype(F32) + got.astype(F32)
    return total


def halve(parts, place, axis, bit):
    own = lax.dynamic_index_in_dim(parts, place, axis, keepdims=False)
    theirs = lax.dynamic_index_in_dim(parts, 1 - place, axis, keepdims=False)
    return own.astype(F32) + flip_dp(theirs.astype(BF16), bit).astype(F32)


def y_scatter(parts):
    return halve(parts.reshape((line_size(), 2) + parts.shape[1:]), y_place(), 1, 2)


def line_y_scatter(parts):
    return line_scatter(y_scatter(parts))


def quad_gather(values_in):
    return jnp.concatenate(
        [values_in] + [flip_quad(values_in, bits) for bits in range(1, QUAD)], axis=0
    )


def quad_scatter(partial_value):
    rows = partial_value.shape[0] // QUAD
    low = partial_value.astype(BF16)
    total = partial_value[:rows].astype(F32)
    for bits in range(1, QUAD):
        total = total + flip_quad(low[bits * rows : (bits + 1) * rows], bits).astype(F32)
    return total


def quad_deal(blocks):
    place = quad_place()
    taken = []
    for bits in range(QUAD):
        piece = lax.dynamic_index_in_dim(blocks, place ^ bits, 2, keepdims=False)
        taken.append(flip_quad(piece, bits) if bits else piece)
    return jnp.concatenate(taken, axis=0)


def quad_collect(blocks):
    rows = blocks.shape[0] // QUAD
    place = quad_place()
    got = [
        flip_quad(blocks[bits * rows : (bits + 1) * rows], bits)
        if bits
        else blocks[bits * rows : (bits + 1) * rows]
        for bits in range(QUAD)
    ]
    return jnp.stack(
        [pick(place, [got[slot ^ here] for here in range(QUAD)]) for slot in range(QUAD)], axis=2
    )


def layer_norm(stream, gain_row, bias_row):
    average = jnp.mean(stream, axis=-1, keepdims=True)
    centered = stream - average
    variance = jnp.mean(centered * centered, axis=-1, keepdims=True)
    return centered * lax.rsqrt(variance + EPSILON) * gain_row + bias_row


def dot_nn(left, right):
    return lax.dot_general(left, right, (((1,), (0,)), ((), ())), preferred_element_type=F32)


def dot_nt(left, right):
    return lax.dot_general(left, right, (((1,), (1,)), ((), ())), preferred_element_type=F32)


def dot_tn(left, right):
    return lax.dot_general(left, right, (((0,), (0,)), ((), ())), preferred_element_type=F32)


def split_heads(packed, group_size):
    row_count, columns = packed.shape
    head_count = columns // (3 * HD)
    shaped = packed.reshape(row_count // group_size, group_size, 3, head_count, HD)
    return shaped[:, :, 0], shaped[:, :, 1], shaped[:, :, 2]


def causal_scores(queries, keys_all, places):
    scores = jnp.einsum(
        "gihe,gjhe->ghij", queries, keys_all, preferred_element_type=F32
    ) * HD ** (-0.5)
    return jnp.where(places[:, None] >= places[None, :], scores, NEGATIVE)


def attend_forward(packed, places):
    queries, keys_all, values_all = split_heads(packed, places.shape[0])
    scores = causal_scores(queries, keys_all, places)
    row_max = jnp.max(scores, axis=-1, keepdims=True)
    shifted = jnp.exp(scores - row_max)
    softened = shifted / jnp.sum(shifted, axis=-1, keepdims=True)
    mixture = jnp.einsum(
        "ghij,gjhe->gihe", softened.astype(BF16), values_all, preferred_element_type=F32
    )
    return mixture.reshape(packed.shape[0], -1).astype(BF16), softened


def attend_backward(packed, softened, grad_mix, places):
    queries, keys_all, values_all = split_heads(packed, places.shape[0])
    grad_heads = grad_mix.reshape(queries.shape)
    grad_soft = jnp.einsum(
        "gihe,gjhe->ghij", grad_heads, values_all, preferred_element_type=F32
    )
    centre = jnp.sum(grad_soft * softened, axis=-1, keepdims=True)
    grad_scores = (softened * (grad_soft - centre)).astype(BF16)
    grad_values = jnp.einsum(
        "ghij,gihe->gjhe", softened.astype(BF16), grad_heads, preferred_element_type=F32
    )
    grad_queries = jnp.einsum(
        "ghij,gjhe->gihe", grad_scores, keys_all, preferred_element_type=F32
    ) * HD ** (-0.5)
    grad_keys = jnp.einsum(
        "ghij,gihe->gjhe", grad_scores, queries, preferred_element_type=F32
    ) * HD ** (-0.5)
    row_count = packed.shape[0]
    return jnp.concatenate(
        [part.reshape(row_count, -1) for part in (grad_queries, grad_keys, grad_values)], axis=1
    ).astype(BF16)


def layer_forward(stream, attend_of, forward_of, gain_rows, bias_rows, norm_index, places):
    normed = layer_norm(stream, gain_rows[norm_index], bias_rows[norm_index]).astype(BF16)
    normed_all = quad_gather(normed)
    joint_proj, output_proj = attend_of()
    packed = dot_nn(normed_all, joint_proj).astype(BF16)
    mixture, softened = attend_forward(packed, places)
    middle = stream + quad_scatter(dot_nt(mixture, output_proj))
    second_all = quad_gather(
        layer_norm(middle, gain_rows[norm_index + 1], bias_rows[norm_index + 1]).astype(BF16)
    )
    upward, downward = forward_of(normed_all)
    hidden = dot_nn(second_all, upward)
    active = jax.nn.gelu(hidden).astype(BF16)
    outcome = middle + quad_scatter(dot_nt(active, downward))
    return (
        outcome,
        (stream, normed_all, packed, mixture, softened, middle, second_all, hidden, active),
        (joint_proj, output_proj, upward, downward),
    )


def layer_backward(grad_layer, saved, weights, gain_rows, bias_rows, norm_index, places, ties):
    stream, normed_all, packed, mixture, softened, middle, second_all, hidden, active = saved
    joint_proj, output_proj, upward, downward = weights
    grad_all = quad_gather(after(grad_layer.astype(BF16), *ties[0]))
    grad_active = dot_nn(grad_all, downward)
    gelu_value, gelu_pull = jax.vjp(jax.nn.gelu, hidden)
    grad_hidden = gelu_pull(grad_active)[0].astype(BF16)
    grad_second = quad_scatter(after(dot_nt(grad_hidden, upward), *ties[1]))
    forward_grads = jnp.concatenate(
        [dot_tn(second_all, grad_hidden).astype(BF16), dot_tn(grad_all, active).astype(BF16)], axis=1
    )
    norm_value, second_pull = jax.vjp(
        layer_norm, middle, gain_rows[norm_index + 1], bias_rows[norm_index + 1]
    )
    grad_middle_norm, grad_gain_two, grad_bias_two = second_pull(grad_second)
    grad_middle = grad_layer + grad_middle_norm
    grad_branch = quad_gather(after(grad_middle.astype(BF16), forward_grads, *ties[2]))
    grad_mix = dot_nn(grad_branch, output_proj).astype(BF16)
    forward_half = y_scatter(forward_grads.reshape(ties[5] + (-1,)))
    grad_packed = attend_backward(packed, softened, grad_mix, places)
    grad_normed = quad_scatter(after(dot_nt(grad_packed, joint_proj), *ties[3]))
    attend_grads = jnp.concatenate(
        [dot_tn(normed_all, grad_packed).astype(BF16), dot_tn(grad_branch, mixture).astype(BF16)], axis=1
    )
    first_value, first_pull = jax.vjp(
        layer_norm, stream, gain_rows[norm_index], bias_rows[norm_index]
    )
    grad_stream_norm, grad_gain_one, grad_bias_one = first_pull(grad_normed)
    grad_stream = grad_middle + grad_stream_norm
    grad_start = quad_gather(after(grad_stream.astype(BF16), *ties[4]))
    attend_half = y_scatter(attend_grads.reshape(ties[5] + (-1,)))
    return (
        grad_start,
        attend_half,
        forward_half,
        (grad_gain_one, grad_gain_two),
        (grad_bias_one, grad_bias_two),
    )


def norm_forward(stream, gain_row, bias_row):
    centered = stream - jnp.mean(stream, axis=-1, keepdims=True)
    scale = lax.rsqrt(jnp.mean(centered * centered, axis=-1, keepdims=True) + EPSILON)
    unit = centered * scale
    return unit * gain_row + bias_row, unit, scale


def norm_backward(grad_out, unit, scale, gain_row):
    grad_unit = grad_out * gain_row
    first = jnp.mean(grad_unit, axis=-1, keepdims=True)
    second = jnp.mean(grad_unit * unit, axis=-1, keepdims=True)
    grad_in = scale * (grad_unit - first - unit * second)
    grad_gain = jnp.sum(grad_out * unit, axis=0, keepdims=True)
    grad_bias = jnp.sum(grad_out, axis=0, keepdims=True)
    return grad_in, grad_gain, grad_bias


GELU_A = 0.7978845608028654
GELU_B = 0.044715
TILE = 256
BAND = 128
PAIR = 2 * HD


def local_body(tiles, wide, *refs):
    @pl.when(pl.program_id(0) < tiles)
    def _():
        local_rows(wide, *refs)

    @pl.when(pl.program_id(0) >= tiles)
    def _():
        local_grads(tiles, wide, *refs)


def local_rows(
    wide,
    scalars_ref, masked_ref, part_0_ref, part_1_ref, part_2_ref, part_3_ref, cotangent_ref,
    gain_ref, bias_ref, first_ref, last_ref,
    result_ref, grad_ref, give_0_ref, give_1_ref, give_2_ref, give_3_ref, norms_ref, weights_out_ref,
    factors_ref, normed_all_ref, branch_all_ref, second_all_ref, grad_out_all_ref,
    turned_ref, branch_turned_ref, probs_ref, stream_ref,
):
    rows = masked_ref.shape[0]
    hidden_width = first_ref.shape[3] // 2 - 2 * wide
    here = pl.ds(pl.multiple_of(pl.program_id(0) * rows, rows), rows)
    normed_ref, branch_ref = normed_all_ref.at[here], branch_all_ref.at[here]
    second_ref, grad_out_ref = second_all_ref.at[here], grad_out_all_ref.at[here]

    def factor(start, width):
        return [factors_ref.at[side, here, start : start + width] for side in range(2)]

    grad_joints, grad_values = factor(0, 2 * wide), factor(2 * wide, wide)
    mixtures = factor(3 * wide, wide)
    hiddens = factor(4 * wide, hidden_width)
    actives = factor(4 * wide + hidden_width, hidden_width)

    def weight(side, start, stop):
        return (first_ref, last_ref)[side][:, 0, :, start:stop].reshape(D, stop - start)

    bands = rows // BAND
    pairs = wide // PAIR

    row = pl.program_id(0) * rows + lax.broadcasted_iota(jnp.int32, (rows, 1), 0)
    keep = (row < scalars_ref[0]).astype(F32)
    place = scalars_ref[1]
    part_width = D // QUAD
    for slot in range(QUAD):
        columns = slice(slot * part_width, (slot + 1) * part_width)
        for bits, part_ref in enumerate((part_0_ref, part_1_ref, part_2_ref, part_3_ref)):

            @pl.when((place ^ bits) == slot)
            def _(part_ref=part_ref, columns=columns):
                stream_ref[:, columns] = masked_ref[:, columns].astype(F32) + part_ref[...].astype(F32)

    stream = stream_ref[...]
    gain_one, gain_two = gain_ref[2:3, :], gain_ref[3:4, :]
    normed, unit_one, scale_one = norm_forward(stream, gain_one, bias_ref[2:3, :])
    normed = normed.astype(BF16)
    normed_ref[...] = normed
    packs = [dot_nn(normed, weight(side, 0, 3 * wide)).astype(BF16) for side in range(2)]

    lanes = lax.broadcasted_iota(jnp.int32, (BAND, PAIR), 1)
    low_head = lanes < HD
    down_rows = lax.broadcasted_iota(jnp.int32, (2 * BAND, BAND), 0) % BAND
    key_rows = lax.broadcasted_iota(jnp.int32, (2 * BAND, BAND), 1)
    allowed = (down_rows // P_SIZE == key_rows // P_SIZE) & (down_rows >= key_rows)

    def apart(pair_values):
        zero = jnp.zeros_like(pair_values)
        return jnp.concatenate(
            [jnp.where(low_head, pair_values, zero), jnp.where(low_head, zero, pair_values)], axis=0
        )

    def joined(stacked):
        return jnp.where(low_head, stacked[:BAND], stacked[BAND:])

    def piece(values_in, band, part, pair):
        start = part * wide + pair * PAIR
        return values_in[band * BAND : (band + 1) * BAND, start : start + PAIR]

    scale = HD ** (-0.5)
    for side in range(2):
        for band in range(bands):
            for pair in range(pairs):
                queries = apart(piece(packs[side], band, 0, pair)) * jnp.asarray(scale, BF16)
                scores = dot_nt(queries, piece(packs[side], band, 1, pair))
                scores = jnp.where(allowed, scores, NEGATIVE)
                shifted = jnp.exp(scores - jnp.max(scores, axis=-1, keepdims=True))
                probs = shifted / jnp.sum(shifted, axis=-1, keepdims=True)
                probs_ref[(side * bands + band) * pairs + pair] = probs
                mixed = dot_nn(probs.astype(BF16), piece(packs[side], band, 2, pair))
                mixtures[side][
                    band * BAND : (band + 1) * BAND, pair * PAIR : (pair + 1) * PAIR
                ] = joined(mixed).astype(BF16)

    middle = stream
    for side in range(2):
        middle = middle + dot_nt(mixtures[side][...], weight(side, 3 * wide, 4 * wide))
    second, unit_two, scale_two = norm_forward(middle, gain_two, bias_ref[3:4, :])
    second = second.astype(BF16)
    second_ref[...] = second
    grad_final = cotangent_ref[...].astype(F32) * keep
    grad_out = grad_final.astype(BF16)
    grad_out_ref[...] = grad_out

    lifted = jnp.zeros_like(middle)
    grad_second = jnp.zeros_like(middle)
    chunk = min(768, hidden_width)
    for side in range(2):
        for start in range(0, hidden_width, chunk):
            first = 4 * wide + start
            upward = weight(side, first, first + chunk)
            downward = weight(side, first + hidden_width, first + hidden_width + chunk)
            hidden = dot_nn(second, upward)
            square = hidden * hidden
            bent = jnp.tanh(GELU_A * hidden * (1.0 + GELU_B * square))
            half = 0.5 * (1.0 + bent)
            active = (hidden * half).astype(BF16)
            slope = half + 0.5 * hidden * (1.0 - bent * bent) * GELU_A * (1.0 + 3.0 * GELU_B * square)
            actives[side][:, start : start + chunk] = active
            lifted = lifted + dot_nt(active, downward)
            grad_hidden = (dot_nn(grad_out, downward) * slope).astype(BF16)
            hiddens[side][:, start : start + chunk] = grad_hidden
            grad_second = grad_second + dot_nt(grad_hidden, upward)
    result_ref[...] = (middle + lifted).astype(BF16)

    grad_in, gain_grad_two, bias_grad_two = norm_backward(grad_second, unit_two, scale_two, gain_two)
    grad_middle = grad_final + grad_in
    branch = grad_middle.astype(BF16)
    branch_ref[...] = branch
    grad_normed = jnp.zeros_like(middle)
    for side in range(2):
        grad_mix = dot_nn(branch, weight(side, 3 * wide, 4 * wide)).astype(BF16)
        for band in range(bands):
            for pair in range(pairs):
                probs = probs_ref[(side * bands + band) * pairs + pair]
                grad_pair = apart(piece(grad_mix, band, 0, pair))
                grad_soft = dot_nt(grad_pair, piece(packs[side], band, 2, pair))
                centre = jnp.sum(grad_soft * probs, axis=-1, keepdims=True)
                grad_scores = (probs * (grad_soft - centre)).astype(BF16)
                queries = apart(piece(packs[side], band, 0, pair))
                grads = (
                    joined(dot_nn(grad_scores, piece(packs[side], band, 1, pair))) * scale,
                    dot_tn(grad_scores, queries) * scale,
                    dot_tn(probs.astype(BF16), grad_pair),
                )
                rows_here = slice(band * BAND, (band + 1) * BAND)
                for part in range(2):
                    first = part * wide + pair * PAIR
                    grad_joints[side][rows_here, first : first + PAIR] = grads[part].astype(BF16)
                grad_values[side][rows_here, pair * PAIR : (pair + 1) * PAIR] = grads[2].astype(BF16)
        grad_normed = grad_normed + dot_nt(grad_joints[side][...], weight(side, 0, 2 * wide))
        grad_normed = grad_normed + dot_nt(grad_values[side][...], weight(side, 2 * wide, 3 * wide))
    grad_in, gain_grad_one, bias_grad_one = norm_backward(grad_normed, unit_one, scale_one, gain_one)
    grad_stream = grad_middle + grad_in
    grad_ref[...] = grad_stream
    for slot in range(QUAD):
        columns = slice(slot * part_width, (slot + 1) * part_width)
        for bits, give_ref in enumerate((give_0_ref, give_1_ref, give_2_ref, give_3_ref)):

            @pl.when((place ^ bits) == slot)
            def _(give_ref=give_ref, columns=columns):
                give_ref[...] = grad_stream[:, columns].astype(BF16)


    @pl.when(pl.program_id(0) == 0)
    def _():
        norms_ref[...] = jnp.zeros_like(norms_ref)

    for place, value in enumerate((gain_grad_one, gain_grad_two, bias_grad_one, bias_grad_two)):
        norms_ref[place : place + 1, :] += value


def local_grads(
    tiles, wide,
    scalars_ref, masked_ref, part_0_ref, part_1_ref, part_2_ref, part_3_ref, cotangent_ref,
    gain_ref, bias_ref, first_ref, last_ref,
    result_ref, grad_ref, give_0_ref, give_1_ref, give_2_ref, give_3_ref, norms_ref, weights_out_ref,
    factors_ref, normed_ref, branch_ref, second_ref, grad_out_ref,
    turned_ref, branch_turned_ref, probs_ref, stream_ref,
):
    step = pl.program_id(0) - tiles
    block, side = step // 2, step % 2
    width = weights_out_ref.shape[3]

    @pl.when(step == 0)
    def _():
        turned_ref[...] = normed_ref[...].T
        branch_turned_ref[...] = branch_ref[...].T

    @pl.when(step == 4)
    def _():
        turned_ref[...] = second_ref[...].T

    @pl.when(step == 8)
    def _():
        turned_ref[...] = grad_out_ref[...].T

    def give(left_ref, right, columns):
        product = dot_nn(left_ref[...], right).astype(BF16)
        weights_out_ref[:, :, :, columns] = product.reshape(
            weights_out_ref.shape[:3] + (product.shape[1],)
        )

    @pl.when(block == 1)
    def _():
        give(turned_ref, factors_ref[side, :, 2 * wide : 3 * wide], slice(0, wide))
        give(branch_turned_ref, factors_ref[side, :, 3 * wide : 4 * wide], slice(wide, 2 * wide))

    @pl.when(block != 1)
    def _():
        start = pl.multiple_of(block * width, width)
        give(turned_ref, factors_ref[side, :, pl.ds(start, width)], slice(None))


def local_layer(scalars, masked_low, spread_parts, cotangent, gain_rows, bias_rows, weights, wide):
    rows = masked_low.shape[0]
    tiles = rows // TILE
    columns = weights.shape[3]
    width = 2 * wide
    assert columns == 6 * width
    tiled = lambda size: pl.BlockSpec((TILE, size), lambda i: (jnp.minimum(i, tiles - 1), 0))
    fixed = lambda array: pl.BlockSpec(array.shape, lambda i: (0, 0), pipeline_mode=pl.Buffered(1))
    outs = [(D, BF16), (D, F32)] + [(D // QUAD, BF16)] * QUAD

    def grads_place(i):
        step = jnp.maximum(i - tiles, 0)
        return (0, step % 2, 0, step // 2)

    return pl.pallas_call(
        lambda *refs: local_body(tiles, wide, *refs),
        grid=(tiles + 2 * (columns // width),),
        in_specs=[pl.BlockSpec(memory_space=pltpu.SMEM)]
        + [tiled(D)] + [tiled(D // QUAD)] * QUAD + [tiled(D)]
        + [fixed(array) for array in (gain_rows, bias_rows)]
        + [
            pl.BlockSpec(
                (weights.shape[0], 1) + weights.shape[2:],
                lambda i, side=side: (0, side, 0, 0),
                pipeline_mode=pl.Buffered(1),
            )
            for side in range(2)
        ],
        out_specs=[tiled(size) for size, _ in outs]
        + [
            pl.BlockSpec((8, D), lambda i: (0, 0)),
            pl.BlockSpec((weights.shape[0], 1, weights.shape[2], width), grads_place),
        ],
        out_shape=[jax.ShapeDtypeStruct((rows, size), kind) for size, kind in outs]
        + [jax.ShapeDtypeStruct((8, D), F32), jax.ShapeDtypeStruct(weights.shape, BF16)],
        scratch_shapes=[pltpu.VMEM((2, rows, columns), BF16)]
        + [pltpu.VMEM((rows, D), BF16)] * 4
        + [pltpu.VMEM((D, rows), BF16)] * 2
        + [
            pltpu.VMEM((2 * (TILE // BAND) * (wide // PAIR), 2 * BAND, BAND), F32),
            pltpu.VMEM((TILE, D), F32),
        ],
        compiler_params=pltpu.CompilerParams(
            dimension_semantics=("arbitrary",), vmem_limit_bytes=58 * 1024 * 1024
        ),
        cost_estimate=pl.CostEstimate(
            flops=12 * rows * D * columns,
            transcendentals=rows * columns,
            bytes_accessed=2 * 4 * D * columns,
        ),
    )(scalars, masked_low, *spread_parts, cotangent, gain_rows, bias_rows, weights, weights)


def shards(
    embedded,
    lengths,
    patch_proj,
    global_proj,
    qkv_weight,
    out_weight,
    up_weight,
    down_weight,
    norm_gain,
    norm_bias,
    cotangent,
):
    half_rows = embedded.shape[1]
    patch_rows = half_rows // P_SIZE
    shard_rows = qkv_weight.shape[1]
    proj_rows = patch_proj.shape[0]
    norm_part = norm_gain.shape[0]
    cells = 2 * line_size()
    heads_width = qkv_weight.shape[3]
    hidden_width = up_weight.shape[2]
    x_here = x_place()

    positions = lax.axis_index("tensor") * half_rows + jnp.arange(half_rows, dtype=jnp.int32)
    keep_mask = (positions < lengths[0]).astype(F32)[:, None]
    masked_low = jnp.where(keep_mask > 0, embedded[0], jnp.zeros_like(embedded[0]))
    masked_low = lax.optimization_barrier(masked_low)

    joint_part = jnp.transpose(qkv_weight, (0, 2, 1, 3))
    output_part = jnp.transpose(out_weight, (0, 2, 1))
    down_part = jnp.transpose(down_weight, (0, 2, 1))

    norm_row = jnp.pad(
        jnp.concatenate([norm_gain, norm_bias]).reshape(1, -1), ((0, 0), (0, D - 2 * norm_part))
    )
    local_shard = jnp.concatenate(
        [joint_part[1, 0], joint_part[1, 1], joint_part[1, 2], output_part[1], up_weight[1], down_part[1]],
        axis=-1,
    )
    local_whole = lax.all_gather(local_shard, ("dp", "tensor"), axis=0)

    patch_pieces = masked_low.reshape(patch_rows, cells, QUAD, proj_rows)
    patches_dealt = quad_deal(patch_pieces)
    queue = LineQueue()
    patch_lined = line_gather(jnp.concatenate([patch_proj, norm_row], axis=0), queue)
    patch_whole = y_gather(patch_lined)
    patch_whole = patch_whole.reshape(cells, proj_rows + 1, D)
    patch_mat = patch_whole[:, :proj_rows].reshape(cells * proj_rows, D)
    norm_cells = patch_whole[:, proj_rows, : 2 * norm_part]
    norm_all = quad_collect(
        jnp.broadcast_to(norm_cells[None], (QUAD,) + norm_cells.shape)
    )[0].astype(F32)
    gain_rows = norm_all[..., :norm_part].reshape(NORMS, D)
    bias_rows = norm_all[..., norm_part:].reshape(NORMS, D)
    gain_rows, bias_rows = lax.optimization_barrier((gain_rows, bias_rows))

    def x_half(part):
        return part.reshape(part.shape[:-1] + (2, part.shape[-1] // 2))

    def global_part(layer):
        pieces = []
        for piece in (
            joint_part[layer, 0],
            joint_part[layer, 1],
            joint_part[layer, 2],
            output_part[layer],
            up_weight[layer],
            down_part[layer],
        ):
            halves = x_half(piece)
            pieces.append(halves)
        return jnp.concatenate(pieces, axis=-1)

    halves = global_part(0)
    own_half = lax.dynamic_index_in_dim(halves, x_here, 1, keepdims=False)
    their_half = lax.dynamic_index_in_dim(halves, 1 - x_here, 1, keepdims=False)
    global_shard = pair_up(own_half, flip_dp(their_half, 1), x_here)
    global_shard = global_shard.reshape(2 * shard_rows, -1)
    attend_columns = 2 * heads_width
    global_blocks = line_pass(global_shard, queue, (patch_whole,))
    attend_lined = line_place_blocks([block[:, :attend_columns] for block in global_blocks])
    forward_lined = line_place_blocks([block[:, attend_columns:] for block in global_blocks])
    proj_part = jnp.transpose(global_proj)
    proj_pair = pair_up(proj_part, flip_dp(proj_part, 2), y_place())
    spread_lined = line_gather(proj_pair, queue)
    joint_columns = 3 * heads_width // 2

    patches_mat = patches_dealt.reshape(QUAD * patch_rows, cells * proj_rows)
    start_partial = dot_nn(patches_mat, patch_mat)
    initial = quad_scatter(start_partial)

    def attend_of():
        whole = y_gather(after(attend_lined, start_partial)).reshape(D, -1)
        return whole[:, :joint_columns], whole[:, joint_columns:]

    def forward_of(marker):
        whole = y_gather(after(forward_lined, marker)).reshape(D, -1)
        return whole[:, : hidden_width // 2], whole[:, hidden_width // 2 :]

    core = lax.axis_index("tensor")
    steps = jnp.arange(patch_rows, dtype=jnp.int32)
    global_places = jnp.concatenate([core * patch_rows + steps, (1 - core) * patch_rows + steps])
    global_out, first_saved, first_weights = layer_forward(
        initial, attend_of, forward_of, gain_rows, bias_rows, 0, global_places
    )
    spread_mat = spread_lined.reshape(cells * proj_rows, D)
    global_low = quad_gather(global_out.astype(BF16))
    spread_dealt = dot_nt(global_low, spread_mat).astype(BF16)
    spread_blocks = spread_dealt.reshape(QUAD * patch_rows, cells, proj_rows)
    byte_cells = cells == P_SIZE
    if byte_cells:
        part_place = quad_place()
        spread_parts = [
            spread_blocks[bits * patch_rows : (bits + 1) * patch_rows] for bits in range(QUAD)
        ]
        spread_parts = [
            (flip_quad(part, bits) if bits else part).reshape(half_rows, proj_rows)
            for bits, part in enumerate(spread_parts)
        ]
    else:
        part_place = jnp.int32(0)
        spread = quad_collect(spread_blocks).reshape(half_rows, D)
        spread_parts = jnp.split(spread, QUAD, axis=1)

    dp = dp_size()
    whole_rows = shard_rows % 16 == 0
    local_weights = local_whole.reshape(dp, 2, shard_rows, -1)
    if not whole_rows:
        local_weights = jnp.transpose(local_weights, (1, 0, 2, 3)).reshape(1, 2, D, -1)
    bound = jnp.clip(lengths[0] - lax.axis_index("tensor") * half_rows, 0, half_rows)
    scalars = jnp.stack([bound, part_place.astype(jnp.int32)])
    local_outs = local_layer(
        scalars, masked_low, spread_parts, cotangent[0], gain_rows, bias_rows, local_weights, heads_width
    )
    outcome, grad_local = local_outs[:2]
    grad_parts = local_outs[2 : 2 + QUAD]
    local_norms, local_grads_out = local_outs[2 + QUAD :]
    second_gains, second_biases = (local_norms[0], local_norms[1]), (local_norms[2], local_norms[3])
    if byte_cells:
        spread_grads = jnp.concatenate(
            [
                (flip_quad(part, bits) if bits else part).reshape(patch_rows, cells, proj_rows)
                for bits, part in enumerate(grad_parts)
            ],
            axis=0,
        )
    else:
        grad_low = jnp.concatenate(grad_parts, axis=1)
        spread_grads = quad_deal(grad_low.reshape(patch_rows, cells, QUAD, proj_rows))
    spread_grads = spread_grads.reshape(QUAD * patch_rows, cells * proj_rows)
    if not whole_rows:
        local_grads_out = jnp.transpose(
            local_grads_out.reshape(2, dp, shard_rows, -1), (1, 0, 2, 3)
        )
    local_summed = lax.psum_scatter(
        local_grads_out.reshape(2 * dp, shard_rows, -1), ("dp", "tensor"), scatter_dimension=0
    ).astype(F32)

    grad_global = quad_scatter(dot_nn(spread_grads, spread_mat))
    proj_grads = dot_tn(spread_grads, global_low).astype(BF16).reshape(cells, proj_rows, D)
    marks = []
    grad_proj = line_scatter(proj_grads.reshape(line_size(), 2, proj_rows, D), marks)
    grad_proj = halve(grad_proj, y_place(), 0, 2)
    ties = ((), (), tuple(marks[:1]), (), tuple(marks[1:2]), (cells, 2 * shard_rows))
    grad_start, attend_half, forward_half, first_gains, first_biases = layer_backward(
        grad_global, first_saved, first_weights, gain_rows, bias_rows, 0, global_places, ties
    )
    global_summed = line_scatter(jnp.concatenate([attend_half, forward_half], axis=2))
    grad_patch_mat = dot_tn(patches_mat, grad_start).astype(BF16).reshape(cells, proj_rows, D)
    grad_patches = after(dot_nt(grad_start, patch_mat).astype(BF16), forward_half, *marks[2:3])
    grad_patches = quad_collect(grad_patches.reshape(QUAD * patch_rows, cells, proj_rows))
    grad_patches = grad_patches.reshape(half_rows, D).astype(F32)
    grad_input = ((grad_local + grad_patches) * keep_mask).astype(BF16)[None]

    gain_grads = jnp.stack([first_gains[0], first_gains[1], second_gains[0], second_gains[1]])
    bias_grads = jnp.stack([first_biases[0], first_biases[1], second_biases[0], second_biases[1]])
    norm_grads = jnp.concatenate(
        [
            gain_grads.reshape(cells, QUAD, norm_part),
            bias_grads.reshape(cells, QUAD, norm_part),
        ],
        axis=2,
    )
    place = quad_place()
    norm_sum = lax.dynamic_index_in_dim(norm_grads, place, 1, keepdims=False)
    for bits in range(1, QUAD):
        piece = lax.dynamic_index_in_dim(norm_grads, place ^ bits, 1, keepdims=False)
        norm_sum = norm_sum + flip_quad(piece, bits)
    norm_rows = jnp.pad(norm_sum[:, None, :].astype(BF16), ((0, 0), (0, 0), (0, D - 2 * norm_part)))
    patch_summed = line_y_scatter(jnp.concatenate([grad_patch_mat, norm_rows], axis=1))

    def x_restore(summed):
        shaped = summed.reshape(2, shard_rows, -1)
        own = lax.dynamic_index_in_dim(shaped, x_here, 0, keepdims=False)
        theirs = lax.dynamic_index_in_dim(shaped, 1 - x_here, 0, keepdims=False)
        return pair_up(own, flip_dp(theirs.astype(BF16), 1).astype(F32), x_here)

    global_summed = x_restore(global_summed)
    attend_global = global_summed[..., :attend_columns]
    forward_global = global_summed[..., attend_columns:]

    def x_columns(source, start, width):
        return jnp.concatenate([source[0, :, start : start + width], source[1, :, start : start + width]], axis=1)

    half_heads, half_hidden = heads_width // 2, hidden_width // 2
    joint_out = jnp.stack(
        [
            jnp.stack([x_columns(attend_global, k * half_heads, half_heads) for k in range(3)], axis=1),
            local_summed[:, : 3 * heads_width].reshape(shard_rows, 3, heads_width),
        ]
    )
    output_out = jnp.stack(
        [
            jnp.transpose(x_columns(attend_global, 3 * half_heads, half_heads)),
            jnp.transpose(local_summed[:, 3 * heads_width : 4 * heads_width]),
        ]
    )
    up_out = jnp.stack([x_columns(forward_global, 0, half_hidden), local_summed[:, 4 * heads_width : 4 * heads_width + hidden_width]])
    down_out = jnp.stack(
        [
            jnp.transpose(x_columns(forward_global, half_hidden, half_hidden)),
            jnp.transpose(local_summed[:, 4 * heads_width + hidden_width :]),
        ]
    )
    return (
        outcome[None],
        grad_input,
        patch_summed[:proj_rows],
        jnp.transpose(grad_proj),
        joint_out,
        output_out,
        up_out,
        down_out,
        patch_summed[proj_rows, :norm_part],
        patch_summed[proj_rows, norm_part : 2 * norm_part],
    )


def solution(mesh):
    placed = (
        P("dp", "tensor", None),
        P("dp"),
        P(("dp", "tensor"), None),
        P(None, ("dp", "tensor")),
        P(None, "dp", None, "tensor"),
        P(None, "tensor", "dp"),
        P(None, "dp", "tensor"),
        P(None, "tensor", "dp"),
        P(("dp", "tensor")),
        P(("dp", "tensor")),
        P("dp", "tensor", None),
    )
    return jax.shard_map(
        shards,
        mesh=mesh,
        in_specs=placed,
        out_specs=(
            P("dp", "tensor", None),
            P("dp", "tensor", None),
            P(("dp", "tensor"), None),
            P(None, ("dp", "tensor")),
            P(None, "dp", None, "tensor"),
            P(None, "tensor", "dp"),
            P(None, "dp", "tensor"),
            P(None, "tensor", "dp"),
            P(("dp", "tensor")),
            P(("dp", "tensor")),
        ),
        check_vma=False,
    )
```

```python
import jax
import jax.numpy as jnp
from jax import lax
from jax.experimental import pallas as pl
from jax.experimental.pallas import tpu as pltpu
from jax.sharding import PartitionSpec as P

D = 768
HD = 64
P_SIZE = 8
NORMS = 4
QUAD = 4

EPSILON = 1e-05
NEGATIVE = -1e30
BF16 = jnp.bfloat16
F32 = jnp.float32


def dp_size():
    return lax.axis_size("dp")


def line_size():
    return dp_size() // 4


def x_place():
    return lax.axis_index("dp") % 2


def y_place():
    return (lax.axis_index("dp") // 2) % 2


def line_place():
    return lax.axis_index("dp") // 4


def quad_place():
    return x_place() * 2 + lax.axis_index("tensor")


def flip_dp(values_in, bit):
    return lax.ppermute(values_in, "dp", [(i, i ^ bit) for i in range(dp_size())])


def flip_core(values_in):
    return lax.ppermute(values_in, "tensor", [(0, 1), (1, 0)])


def flip_quad(values_in, bits):
    return lax.ppermute(
        values_in, ("dp", "tensor"), [(i, i ^ bits) for i in range(2 * dp_size())]
    )


def step_line(values_in, offset):
    count = dp_size()
    return lax.ppermute(values_in, "dp", [(i, (i + 4 * offset) % count) for i in range(count)])


def after(values_in, *earlier):
    return lax.optimization_barrier((values_in,) + earlier)[0]


def line_groups():
    return [[line * 4 + rest for line in range(line_size())] for rest in range(4)]


def pick(place, choices):
    if len(choices) == 2:
        return lax.select_n(place == 1, *choices)
    return lax.select_n(place, *choices)


class LineQueue:
    def __init__(self):
        self.arrived = [(), ()]

    def step(self, values_in):
        got = step_line(after(values_in, *self.arrived.pop(0)), 1)
        self.arrived.append((got,))
        return got

    def hold(self, *earlier):
        self.arrived[0] = self.arrived[0] + earlier


def line_pass(values_in, queue, holds=()):
    count = line_size()
    if count > 4:
        whole = lax.all_gather(values_in, "dp", axis=0, axis_index_groups=line_groups())
        return [whole[slot] for slot in range(count)]
    got = [values_in]
    for step in range(1, count):
        if step == count - 1 and holds:
            queue.hold(*holds)
        got.append(queue.step(got[-1]))
    return got


def line_place_blocks(got):
    count = len(got)
    if count == 1:
        return got[0][None]
    if count > 4:
        return jnp.stack(got)
    place = line_place()
    return jnp.stack(
        [pick(place, [got[(here - slot) % count] for here in range(count)]) for slot in range(count)]
    )


def line_gather(values_in, queue):
    return line_place_blocks(line_pass(values_in, queue))


def pair_up(own, other, place):
    return jnp.stack([pick(place, [own, other]), pick(place, [other, own])], axis=0)


def y_gather(lined):
    other = flip_dp(lined, 2)
    place = y_place()
    return jnp.stack([pick(place, [lined, other]), pick(place, [other, lined])], axis=1)


def line_scatter(parts, marks=None):
    count = line_size()
    if count > 4:
        return lax.psum_scatter(
            parts.astype(F32), "dp", scatter_dimension=0, axis_index_groups=line_groups(), tiled=False
        )
    place = line_place()

    def slot(offset):
        return lax.dynamic_index_in_dim(parts, (place + count + offset) % count, 0, keepdims=False)

    total = slot(-1).astype(F32)
    for back in range(2, count + 1):
        got = step_line(total.astype(BF16), 1)
        if marks is not None:
            marks.append(got)
        total = slot(-back).astype(F32) + got.astype(F32)
    return total


def halve(parts, place, axis, bit):
    own = lax.dynamic_index_in_dim(parts, place, axis, keepdims=False)
    theirs = lax.dynamic_index_in_dim(parts, 1 - place, axis, keepdims=False)
    return own.astype(F32) + flip_dp(theirs.astype(BF16), bit).astype(F32)


def y_scatter(parts):
    return halve(parts.reshape((line_size(), 2) + parts.shape[1:]), y_place(), 1, 2)


def line_y_scatter(parts):
    return line_scatter(y_scatter(parts))


def quad_gather(values_in):
    return jnp.concatenate(
        [values_in] + [flip_quad(values_in, bits) for bits in range(1, QUAD)], axis=0
    )


def quad_scatter(partial_value):
    rows = partial_value.shape[0] // QUAD
    low = partial_value.astype(BF16)
    total = partial_value[:rows].astype(F32)
    for bits in range(1, QUAD):
        total = total + flip_quad(low[bits * rows : (bits + 1) * rows], bits).astype(F32)
    return total


def quad_deal(blocks):
    place = quad_place()
    taken = []
    for bits in range(QUAD):
        piece = lax.dynamic_index_in_dim(blocks, place ^ bits, 2, keepdims=False)
        taken.append(flip_quad(piece, bits) if bits else piece)
    return jnp.concatenate(taken, axis=0)


def quad_collect(blocks):
    rows = blocks.shape[0] // QUAD
    place = quad_place()
    got = [
        flip_quad(blocks[bits * rows : (bits + 1) * rows], bits)
        if bits
        else blocks[bits * rows : (bits + 1) * rows]
        for bits in range(QUAD)
    ]
    return jnp.stack(
        [pick(place, [got[slot ^ here] for here in range(QUAD)]) for slot in range(QUAD)], axis=2
    )


def layer_norm(stream, gain_row, bias_row):
    average = jnp.mean(stream, axis=-1, keepdims=True)
    centered = stream - average
    variance = jnp.mean(centered * centered, axis=-1, keepdims=True)
    return centered * lax.rsqrt(variance + EPSILON) * gain_row + bias_row


def dot_nn(left, right):
    return lax.dot_general(left, right, (((1,), (0,)), ((), ())), preferred_element_type=F32)


def dot_nt(left, right):
    return lax.dot_general(left, right, (((1,), (1,)), ((), ())), preferred_element_type=F32)


def dot_tn(left, right):
    return lax.dot_general(left, right, (((0,), (0,)), ((), ())), preferred_element_type=F32)


def split_heads(packed, group_size):
    row_count, columns = packed.shape
    head_count = columns // (3 * HD)
    shaped = packed.reshape(row_count // group_size, group_size, 3, head_count, HD)
    return shaped[:, :, 0], shaped[:, :, 1], shaped[:, :, 2]


def causal_scores(queries, keys_all, places):
    scores = jnp.einsum(
        "gihe,gjhe->ghij", queries, keys_all, preferred_element_type=F32
    ) * HD ** (-0.5)
    return jnp.where(places[:, None] >= places[None, :], scores, NEGATIVE)


def attend_forward(packed, places):
    queries, keys_all, values_all = split_heads(packed, places.shape[0])
    scores = causal_scores(queries, keys_all, places)
    row_max = jnp.max(scores, axis=-1, keepdims=True)
    shifted = jnp.exp(scores - row_max)
    softened = shifted / jnp.sum(shifted, axis=-1, keepdims=True)
    mixture = jnp.einsum(
        "ghij,gjhe->gihe", softened.astype(BF16), values_all, preferred_element_type=F32
    )
    return mixture.reshape(packed.shape[0], -1).astype(BF16), softened


def attend_backward(packed, softened, grad_mix, places):
    queries, keys_all, values_all = split_heads(packed, places.shape[0])
    grad_heads = grad_mix.reshape(queries.shape)
    grad_soft = jnp.einsum(
        "gihe,gjhe->ghij", grad_heads, values_all, preferred_element_type=F32
    )
    centre = jnp.sum(grad_soft * softened, axis=-1, keepdims=True)
    grad_scores = (softened * (grad_soft - centre)).astype(BF16)
    grad_values = jnp.einsum(
        "ghij,gihe->gjhe", softened.astype(BF16), grad_heads, preferred_element_type=F32
    )
    grad_queries = jnp.einsum(
        "ghij,gjhe->gihe", grad_scores, keys_all, preferred_element_type=F32
    ) * HD ** (-0.5)
    grad_keys = jnp.einsum(
        "ghij,gihe->gjhe", grad_scores, queries, preferred_element_type=F32
    ) * HD ** (-0.5)
    row_count = packed.shape[0]
    return jnp.concatenate(
        [part.reshape(row_count, -1) for part in (grad_queries, grad_keys, grad_values)], axis=1
    ).astype(BF16)


def layer_forward(stream, attend_of, forward_of, gain_rows, bias_rows, norm_index, places):
    normed = layer_norm(stream, gain_rows[norm_index], bias_rows[norm_index]).astype(BF16)
    normed_all = quad_gather(normed)
    joint_proj, output_proj = attend_of()
    packed = dot_nn(normed_all, joint_proj).astype(BF16)
    mixture, softened = attend_forward(packed, places)
    middle = stream + quad_scatter(dot_nt(mixture, output_proj))
    second_all = quad_gather(
        layer_norm(middle, gain_rows[norm_index + 1], bias_rows[norm_index + 1]).astype(BF16)
    )
    upward, downward = forward_of(normed_all)
    hidden = dot_nn(second_all, upward)
    active = jax.nn.gelu(hidden).astype(BF16)
    outcome = middle + quad_scatter(dot_nt(active, downward))
    return (
        outcome,
        (stream, normed_all, packed, mixture, softened, middle, second_all, hidden, active),
        (joint_proj, output_proj, upward, downward),
    )


def layer_backward(grad_layer, saved, weights, gain_rows, bias_rows, norm_index, places, ties):
    stream, normed_all, packed, mixture, softened, middle, second_all, hidden, active = saved
    joint_proj, output_proj, upward, downward = weights
    grad_all = quad_gather(after(grad_layer.astype(BF16), *ties[0]))
    grad_active = dot_nn(grad_all, downward)
    gelu_value, gelu_pull = jax.vjp(jax.nn.gelu, hidden)
    grad_hidden = gelu_pull(grad_active)[0].astype(BF16)
    grad_second = quad_scatter(after(dot_nt(grad_hidden, upward), *ties[1]))
    forward_grads = jnp.concatenate(
        [dot_tn(second_all, grad_hidden).astype(BF16), dot_tn(grad_all, active).astype(BF16)], axis=1
    )
    norm_value, second_pull = jax.vjp(
        layer_norm, middle, gain_rows[norm_index + 1], bias_rows[norm_index + 1]
    )
    grad_middle_norm, grad_gain_two, grad_bias_two = second_pull(grad_second)
    grad_middle = grad_layer + grad_middle_norm
    grad_branch = quad_gather(after(grad_middle.astype(BF16), forward_grads, *ties[2]))
    grad_mix = dot_nn(grad_branch, output_proj).astype(BF16)
    forward_half = y_scatter(forward_grads.reshape(ties[5] + (-1,)))
    grad_packed = attend_backward(packed, softened, grad_mix, places)
    grad_normed = quad_scatter(after(dot_nt(grad_packed, joint_proj), *ties[3]))
    attend_grads = jnp.concatenate(
        [dot_tn(normed_all, grad_packed).astype(BF16), dot_tn(grad_branch, mixture).astype(BF16)], axis=1
    )
    first_value, first_pull = jax.vjp(
        layer_norm, stream, gain_rows[norm_index], bias_rows[norm_index]
    )
    grad_stream_norm, grad_gain_one, grad_bias_one = first_pull(grad_normed)
    grad_stream = grad_middle + grad_stream_norm
    grad_start = quad_gather(after(grad_stream.astype(BF16), *ties[4]))
    attend_half = y_scatter(attend_grads.reshape(ties[5] + (-1,)))
    return (
        grad_start,
        attend_half,
        forward_half,
        (grad_gain_one, grad_gain_two),
        (grad_bias_one, grad_bias_two),
    )


def norm_forward(stream, gain_row, bias_row):
    centered = stream - jnp.mean(stream, axis=-1, keepdims=True)
    scale = lax.rsqrt(jnp.mean(centered * centered, axis=-1, keepdims=True) + EPSILON)
    unit = centered * scale
    return unit * gain_row + bias_row, unit, scale


def norm_backward(grad_out, unit, scale, gain_row):
    grad_unit = grad_out * gain_row
    first = jnp.mean(grad_unit, axis=-1, keepdims=True)
    second = jnp.mean(grad_unit * unit, axis=-1, keepdims=True)
    grad_in = scale * (grad_unit - first - unit * second)
    grad_gain = jnp.sum(grad_out * unit, axis=0, keepdims=True)
    grad_bias = jnp.sum(grad_out, axis=0, keepdims=True)
    return grad_in, grad_gain, grad_bias


GELU_A = 0.7978845608028654
GELU_B = 0.044715
TILE = 256
BAND = 128
PAIR = 2 * HD


def local_body(tiles, wide, *refs):
    @pl.when(pl.program_id(0) < tiles)
    def _():
        local_rows(wide, *refs)

    @pl.when(pl.program_id(0) >= tiles)
    def _():
        local_grads(tiles, wide, *refs)


def local_rows(
    wide,
    scalars_ref, masked_ref, part_0_ref, part_1_ref, part_2_ref, part_3_ref, cotangent_ref,
    gain_ref, bias_ref, first_ref, last_ref,
    result_ref, grad_ref, give_0_ref, give_1_ref, give_2_ref, give_3_ref, norms_ref, weights_out_ref,
    factors_ref, normed_all_ref, branch_all_ref, second_all_ref, grad_out_all_ref,
    turned_ref, branch_turned_ref, probs_ref, stream_ref,
):
    rows = masked_ref.shape[0]
    hidden_width = first_ref.shape[3] // 2 - 2 * wide
    here = pl.ds(pl.multiple_of(pl.program_id(0) * rows, rows), rows)
    normed_ref, branch_ref = normed_all_ref.at[here], branch_all_ref.at[here]
    second_ref, grad_out_ref = second_all_ref.at[here], grad_out_all_ref.at[here]

    def factor(start, width):
        return [factors_ref.at[side, here, start : start + width] for side in range(2)]

    grad_joints, grad_values = factor(0, 2 * wide), factor(2 * wide, wide)
    mixtures = factor(3 * wide, wide)
    hiddens = factor(4 * wide, hidden_width)
    actives = factor(4 * wide + hidden_width, hidden_width)

    def weight(side, start, stop):
        return (first_ref, last_ref)[side][:, 0, :, start:stop].reshape(D, stop - start)

    bands = rows // BAND
    pairs = wide // PAIR

    row = pl.program_id(0) * rows + lax.broadcasted_iota(jnp.int32, (rows, 1), 0)
    keep = (row < scalars_ref[0]).astype(F32)
    place = scalars_ref[1]
    part_width = D // QUAD
    for slot in range(QUAD):
        columns = slice(slot * part_width, (slot + 1) * part_width)
        for bits, part_ref in enumerate((part_0_ref, part_1_ref, part_2_ref, part_3_ref)):

            @pl.when((place ^ bits) == slot)
            def _(part_ref=part_ref, columns=columns):
                stream_ref[:, columns] = masked_ref[:, columns].astype(F32) + part_ref[...].astype(F32)

    stream = stream_ref[...]
    gain_one, gain_two = gain_ref[2:3, :], gain_ref[3:4, :]
    normed, unit_one, scale_one = norm_forward(stream, gain_one, bias_ref[2:3, :])
    normed = normed.astype(BF16)
    normed_ref[...] = normed
    packs = [dot_nn(normed, weight(side, 0, 3 * wide)).astype(BF16) for side in range(2)]

    lanes = lax.broadcasted_iota(jnp.int32, (BAND, PAIR), 1)
    low_head = lanes < HD
    down_rows = lax.broadcasted_iota(jnp.int32, (2 * BAND, BAND), 0) % BAND
    key_rows = lax.broadcasted_iota(jnp.int32, (2 * BAND, BAND), 1)
    allowed = (down_rows // P_SIZE == key_rows // P_SIZE) & (down_rows >= key_rows)

    def apart(pair_values):
        zero = jnp.zeros_like(pair_values)
        return jnp.concatenate(
            [jnp.where(low_head, pair_values, zero), jnp.where(low_head, zero, pair_values)], axis=0
        )

    def joined(stacked):
        return jnp.where(low_head, stacked[:BAND], stacked[BAND:])

    def piece(values_in, band, part, pair):
        start = part * wide + pair * PAIR
        return values_in[band * BAND : (band + 1) * BAND, start : start + PAIR]

    scale = HD ** (-0.5)
    for side in range(2):
        for band in range(bands):
            for pair in range(pairs):
                queries = apart(piece(packs[side], band, 0, pair)) * jnp.asarray(scale, BF16)
                scores = dot_nt(queries, piece(packs[side], band, 1, pair))
                scores = jnp.where(allowed, scores, NEGATIVE)
                shifted = jnp.exp(scores - jnp.max(scores, axis=-1, keepdims=True))
                probs = shifted / jnp.sum(shifted, axis=-1, keepdims=True)
                probs_ref[(side * bands + band) * pairs + pair] = probs
                mixed = dot_nn(probs.astype(BF16), piece(packs[side], band, 2, pair))
                mixtures[side][
                    band * BAND : (band + 1) * BAND, pair * PAIR : (pair + 1) * PAIR
                ] = joined(mixed).astype(BF16)

    middle = stream
    for side in range(2):
        middle = middle + dot_nt(mixtures[side][...], weight(side, 3 * wide, 4 * wide))
    second, unit_two, scale_two = norm_forward(middle, gain_two, bias_ref[3:4, :])
    second = second.astype(BF16)
    second_ref[...] = second
    grad_final = cotangent_ref[...].astype(F32) * keep
    grad_out = grad_final.astype(BF16)
    grad_out_ref[...] = grad_out

    lifted = jnp.zeros_like(middle)
    grad_second = jnp.zeros_like(middle)
    chunk = min(768, hidden_width)
    for side in range(2):
        for start in range(0, hidden_width, chunk):
            first = 4 * wide + start
            upward = weight(side, first, first + chunk)
            downward = weight(side, first + hidden_width, first + hidden_width + chunk)
            hidden = dot_nn(second, upward)
            square = hidden * hidden
            bent = jnp.tanh(GELU_A * hidden * (1.0 + GELU_B * square))
            half = 0.5 * (1.0 + bent)
            active = (hidden * half).astype(BF16)
            slope = half + 0.5 * hidden * (1.0 - bent * bent) * GELU_A * (1.0 + 3.0 * GELU_B * square)
            actives[side][:, start : start + chunk] = active
            lifted = lifted + dot_nt(active, downward)
            grad_hidden = (dot_nn(grad_out, downward) * slope).astype(BF16)
            hiddens[side][:, start : start + chunk] = grad_hidden
            grad_second = grad_second + dot_nt(grad_hidden, upward)
    result_ref[...] = (middle + lifted).astype(BF16)

    grad_in, gain_grad_two, bias_grad_two = norm_backward(grad_second, unit_two, scale_two, gain_two)
    grad_middle = grad_final + grad_in
    branch = grad_middle.astype(BF16)
    branch_ref[...] = branch
    grad_normed = jnp.zeros_like(middle)
    for side in range(2):
        grad_mix = dot_nn(branch, weight(side, 3 * wide, 4 * wide)).astype(BF16)
        for band in range(bands):
            for pair in range(pairs):
                probs = probs_ref[(side * bands + band) * pairs + pair]
                grad_pair = apart(piece(grad_mix, band, 0, pair))
                grad_soft = dot_nt(grad_pair, piece(packs[side], band, 2, pair))
                centre = jnp.sum(grad_soft * probs, axis=-1, keepdims=True)
                grad_scores = (probs * (grad_soft - centre)).astype(BF16)
                queries = apart(piece(packs[side], band, 0, pair))
                grads = (
                    joined(dot_nn(grad_scores, piece(packs[side], band, 1, pair))) * scale,
                    dot_tn(grad_scores, queries) * scale,
                    dot_tn(probs.astype(BF16), grad_pair),
                )
                rows_here = slice(band * BAND, (band + 1) * BAND)
                for part in range(2):
                    first = part * wide + pair * PAIR
                    grad_joints[side][rows_here, first : first + PAIR] = grads[part].astype(BF16)
                grad_values[side][rows_here, pair * PAIR : (pair + 1) * PAIR] = grads[2].astype(BF16)
        grad_normed = grad_normed + dot_nt(grad_joints[side][...], weight(side, 0, 2 * wide))
        grad_normed = grad_normed + dot_nt(grad_values[side][...], weight(side, 2 * wide, 3 * wide))
    grad_in, gain_grad_one, bias_grad_one = norm_backward(grad_normed, unit_one, scale_one, gain_one)
    grad_stream = grad_middle + grad_in
    grad_ref[...] = grad_stream
    for slot in range(QUAD):
        columns = slice(slot * part_width, (slot + 1) * part_width)
        for bits, give_ref in enumerate((give_0_ref, give_1_ref, give_2_ref, give_3_ref)):

            @pl.when((place ^ bits) == slot)
            def _(give_ref=give_ref, columns=columns):
                give_ref[...] = grad_stream[:, columns].astype(BF16)


    @pl.when(pl.program_id(0) == 0)
    def _():
        norms_ref[...] = jnp.zeros_like(norms_ref)

    for place, value in enumerate((gain_grad_one, gain_grad_two, bias_grad_one, bias_grad_two)):
        norms_ref[place : place + 1, :] += value


def local_grads(
    tiles, wide,
    scalars_ref, masked_ref, part_0_ref, part_1_ref, part_2_ref, part_3_ref, cotangent_ref,
    gain_ref, bias_ref, first_ref, last_ref,
    result_ref, grad_ref, give_0_ref, give_1_ref, give_2_ref, give_3_ref, norms_ref, weights_out_ref,
    factors_ref, normed_ref, branch_ref, second_ref, grad_out_ref,
    turned_ref, branch_turned_ref, probs_ref, stream_ref,
):
    step = pl.program_id(0) - tiles
    block, side = step // 2, step % 2
    width = weights_out_ref.shape[3]

    @pl.when(step == 0)
    def _():
        turned_ref[...] = normed_ref[...].T
        branch_turned_ref[...] = branch_ref[...].T

    @pl.when(step == 4)
    def _():
        turned_ref[...] = second_ref[...].T

    @pl.when(step == 8)
    def _():
        turned_ref[...] = grad_out_ref[...].T

    def give(left_ref, right, columns):
        product = dot_nn(left_ref[...], right).astype(BF16)
        weights_out_ref[:, :, :, columns] = product.reshape(
            weights_out_ref.shape[:3] + (product.shape[1],)
        )

    @pl.when(block == 1)
    def _():
        give(turned_ref, factors_ref[side, :, 2 * wide : 3 * wide], slice(0, wide))
        give(branch_turned_ref, factors_ref[side, :, 3 * wide : 4 * wide], slice(wide, 2 * wide))

    @pl.when(block != 1)
    def _():
        start = pl.multiple_of(block * width, width)
        give(turned_ref, factors_ref[side, :, pl.ds(start, width)], slice(None))


def local_layer(scalars, masked_low, spread_parts, cotangent, gain_rows, bias_rows, weights, wide):
    rows = masked_low.shape[0]
    tiles = rows // TILE
    columns = weights.shape[3]
    width = 2 * wide
    assert columns == 6 * width
    tiled = lambda size: pl.BlockSpec((TILE, size), lambda i: (jnp.minimum(i, tiles - 1), 0))
    fixed = lambda array: pl.BlockSpec(array.shape, lambda i: (0, 0), pipeline_mode=pl.Buffered(1))
    outs = [(D, BF16), (D, F32)] + [(D // QUAD, BF16)] * QUAD

    def grads_place(i):
        step = jnp.maximum(i - tiles, 0)
        return (0, step % 2, 0, step // 2)

    return pl.pallas_call(
        lambda *refs: local_body(tiles, wide, *refs),
        grid=(tiles + 2 * (columns // width),),
        in_specs=[pl.BlockSpec(memory_space=pltpu.SMEM)]
        + [tiled(D)] + [tiled(D // QUAD)] * QUAD + [tiled(D)]
        + [fixed(array) for array in (gain_rows, bias_rows)]
        + [
            pl.BlockSpec(
                (weights.shape[0], 1) + weights.shape[2:],
                lambda i, side=side: (0, side, 0, 0),
                pipeline_mode=pl.Buffered(1),
            )
            for side in range(2)
        ],
        out_specs=[tiled(size) for size, _ in outs]
        + [
            pl.BlockSpec((8, D), lambda i: (0, 0)),
            pl.BlockSpec((weights.shape[0], 1, weights.shape[2], width), grads_place),
        ],
        out_shape=[jax.ShapeDtypeStruct((rows, size), kind) for size, kind in outs]
        + [jax.ShapeDtypeStruct((8, D), F32), jax.ShapeDtypeStruct(weights.shape, BF16)],
        scratch_shapes=[pltpu.VMEM((2, rows, columns), BF16)]
        + [pltpu.VMEM((rows, D), BF16)] * 4
        + [pltpu.VMEM((D, rows), BF16)] * 2
        + [
            pltpu.VMEM((2 * (TILE // BAND) * (wide // PAIR), 2 * BAND, BAND), F32),
            pltpu.VMEM((TILE, D), F32),
        ],
        compiler_params=pltpu.CompilerParams(
            dimension_semantics=("arbitrary",), vmem_limit_bytes=58 * 1024 * 1024
        ),
        cost_estimate=pl.CostEstimate(
            flops=12 * rows * D * columns,
            transcendentals=rows * columns,
            bytes_accessed=2 * 4 * D * columns,
        ),
    )(scalars, masked_low, *spread_parts, cotangent, gain_rows, bias_rows, weights, weights)


def shards(
    embedded,
    lengths,
    patch_proj,
    global_proj,
    qkv_weight,
    out_weight,
    up_weight,
    down_weight,
    norm_gain,
    norm_bias,
    cotangent,
):
    half_rows = embedded.shape[1]
    patch_rows = half_rows // P_SIZE
    shard_rows = qkv_weight.shape[1]
    proj_rows = patch_proj.shape[0]
    norm_part = norm_gain.shape[0]
    cells = 2 * line_size()
    heads_width = qkv_weight.shape[3]
    hidden_width = up_weight.shape[2]
    x_here = x_place()

    positions = lax.axis_index("tensor") * half_rows + jnp.arange(half_rows, dtype=jnp.int32)
    keep_mask = (positions < lengths[0]).astype(F32)[:, None]
    masked_low = jnp.where(keep_mask > 0, embedded[0], jnp.zeros_like(embedded[0]))
    masked_low = lax.optimization_barrier(masked_low)

    joint_part = jnp.transpose(qkv_weight, (0, 2, 1, 3))
    output_part = jnp.transpose(out_weight, (0, 2, 1))
    down_part = jnp.transpose(down_weight, (0, 2, 1))

    norm_row = jnp.pad(
        jnp.concatenate([norm_gain, norm_bias]).reshape(1, -1), ((0, 0), (0, D - 2 * norm_part))
    )
    local_shard = jnp.concatenate(
        [joint_part[1, 0], joint_part[1, 1], joint_part[1, 2], output_part[1], up_weight[1], down_part[1]],
        axis=-1,
    )
    local_whole = lax.all_gather(local_shard, ("dp", "tensor"), axis=0)

    patch_pieces = masked_low.reshape(patch_rows, cells, QUAD, proj_rows)
    patches_dealt = quad_deal(patch_pieces)
    queue = LineQueue()
    patch_lined = line_gather(jnp.concatenate([patch_proj, norm_row], axis=0), queue)
    patch_whole = y_gather(patch_lined)
    patch_whole = patch_whole.reshape(cells, proj_rows + 1, D)
    patch_mat = patch_whole[:, :proj_rows].reshape(cells * proj_rows, D)
    norm_cells = patch_whole[:, proj_rows, : 2 * norm_part]
    norm_all = quad_collect(
        jnp.broadcast_to(norm_cells[None], (QUAD,) + norm_cells.shape)
    )[0].astype(F32)
    gain_rows = norm_all[..., :norm_part].reshape(NORMS, D)
    bias_rows = norm_all[..., norm_part:].reshape(NORMS, D)
    gain_rows, bias_rows = lax.optimization_barrier((gain_rows, bias_rows))

    def x_half(part):
        return part.reshape(part.shape[:-1] + (2, part.shape[-1] // 2))

    def global_part(layer):
        pieces = []
        for piece in (
            joint_part[layer, 0],
            joint_part[layer, 1],
            joint_part[layer, 2],
            output_part[layer],
            up_weight[layer],
            down_part[layer],
        ):
            halves = x_half(piece)
            pieces.append(halves)
        return jnp.concatenate(pieces, axis=-1)

    halves = global_part(0)
    own_half = lax.dynamic_index_in_dim(halves, x_here, 1, keepdims=False)
    their_half = lax.dynamic_index_in_dim(halves, 1 - x_here, 1, keepdims=False)
    global_shard = pair_up(own_half, flip_dp(their_half, 1), x_here)
    global_shard = global_shard.reshape(2 * shard_rows, -1)
    attend_columns = 2 * heads_width
    global_blocks = line_pass(global_shard, queue, (patch_whole,))
    queue.hold(global_blocks[-1])
    attend_lined = line_place_blocks([block[:, :attend_columns] for block in global_blocks])
    forward_lined = line_place_blocks([block[:, attend_columns:] for block in global_blocks])
    proj_part = jnp.transpose(global_proj)
    proj_pair = pair_up(proj_part, flip_dp(proj_part, 2), y_place())
    spread_lined = line_gather(proj_pair, queue)
    joint_columns = 3 * heads_width // 2

    patches_mat = patches_dealt.reshape(QUAD * patch_rows, cells * proj_rows)
    start_partial = dot_nn(patches_mat, patch_mat)
    initial = quad_scatter(start_partial)

    def attend_of():
        whole = y_gather(after(attend_lined, start_partial)).reshape(D, -1)
        return whole[:, :joint_columns], whole[:, joint_columns:]

    def forward_of(marker):
        whole = y_gather(after(forward_lined, marker)).reshape(D, -1)
        return whole[:, : hidden_width // 2], whole[:, hidden_width // 2 :]

    core = lax.axis_index("tensor")
    steps = jnp.arange(patch_rows, dtype=jnp.int32)
    global_places = jnp.concatenate([core * patch_rows + steps, (1 - core) * patch_rows + steps])
    global_out, first_saved, first_weights = layer_forward(
        initial, attend_of, forward_of, gain_rows, bias_rows, 0, global_places
    )
    spread_mat = spread_lined.reshape(cells * proj_rows, D)
    global_low = quad_gather(global_out.astype(BF16))
    spread_dealt = dot_nt(global_low, spread_mat).astype(BF16)
    spread_blocks = spread_dealt.reshape(QUAD * patch_rows, cells, proj_rows)
    byte_cells = cells == P_SIZE
    if byte_cells:
        part_place = quad_place()
        spread_parts = [
            spread_blocks[bits * patch_rows : (bits + 1) * patch_rows] for bits in range(QUAD)
        ]
        spread_parts = [
            (flip_quad(part, bits) if bits else part).reshape(half_rows, proj_rows)
            for bits, part in enumerate(spread_parts)
        ]
    else:
        part_place = jnp.int32(0)
        spread = quad_collect(spread_blocks).reshape(half_rows, D)
        spread_parts = jnp.split(spread, QUAD, axis=1)

    dp = dp_size()
    whole_rows = shard_rows % 16 == 0
    local_weights = local_whole.reshape(dp, 2, shard_rows, -1)
    if not whole_rows:
        local_weights = jnp.transpose(local_weights, (1, 0, 2, 3)).reshape(1, 2, D, -1)
    bound = jnp.clip(lengths[0] - lax.axis_index("tensor") * half_rows, 0, half_rows)
    scalars = jnp.stack([bound, part_place.astype(jnp.int32)])
    local_outs = local_layer(
        scalars, masked_low, spread_parts, cotangent[0], gain_rows, bias_rows, local_weights, heads_width
    )
    outcome, grad_local = local_outs[:2]
    grad_parts = local_outs[2 : 2 + QUAD]
    local_norms, local_grads_out = local_outs[2 + QUAD :]
    second_gains, second_biases = (local_norms[0], local_norms[1]), (local_norms[2], local_norms[3])
    if byte_cells:
        spread_grads = jnp.concatenate(
            [
                (flip_quad(part, bits) if bits else part).reshape(patch_rows, cells, proj_rows)
                for bits, part in enumerate(grad_parts)
            ],
            axis=0,
        )
    else:
        grad_low = jnp.concatenate(grad_parts, axis=1)
        spread_grads = quad_deal(grad_low.reshape(patch_rows, cells, QUAD, proj_rows))
    spread_grads = spread_grads.reshape(QUAD * patch_rows, cells * proj_rows)
    if not whole_rows:
        local_grads_out = jnp.transpose(
            local_grads_out.reshape(2, dp, shard_rows, -1), (1, 0, 2, 3)
        )
    local_summed = lax.psum_scatter(
        local_grads_out.reshape(2 * dp, shard_rows, -1), ("dp", "tensor"), scatter_dimension=0
    ).astype(F32)

    grad_global = quad_scatter(dot_nn(spread_grads, spread_mat))
    proj_grads = dot_tn(spread_grads, global_low).astype(BF16).reshape(cells, proj_rows, D)
    marks = []
    grad_proj = line_scatter(proj_grads.reshape(line_size(), 2, proj_rows, D), marks)
    grad_proj = halve(grad_proj, y_place(), 0, 2)
    ties = ((), (), tuple(marks[:1]), (), tuple(marks[1:2]), (cells, 2 * shard_rows))
    grad_start, attend_half, forward_half, first_gains, first_biases = layer_backward(
        grad_global, first_saved, first_weights, gain_rows, bias_rows, 0, global_places, ties
    )
    global_summed = line_scatter(jnp.concatenate([attend_half, forward_half], axis=2))
    grad_patch_mat = dot_tn(patches_mat, grad_start).astype(BF16).reshape(cells, proj_rows, D)
    grad_patches = after(dot_nt(grad_start, patch_mat).astype(BF16), forward_half, *marks[2:3])
    grad_patches = quad_collect(grad_patches.reshape(QUAD * patch_rows, cells, proj_rows))
    grad_patches = grad_patches.reshape(half_rows, D).astype(F32)
    grad_input = ((grad_local + grad_patches) * keep_mask).astype(BF16)[None]

    gain_grads = jnp.stack([first_gains[0], first_gains[1], second_gains[0], second_gains[1]])
    bias_grads = jnp.stack([first_biases[0], first_biases[1], second_biases[0], second_biases[1]])
    norm_grads = jnp.concatenate(
        [
            gain_grads.reshape(cells, QUAD, norm_part),
            bias_grads.reshape(cells, QUAD, norm_part),
        ],
        axis=2,
    )
    place = quad_place()
    norm_sum = lax.dynamic_index_in_dim(norm_grads, place, 1, keepdims=False)
    for bits in range(1, QUAD):
        piece = lax.dynamic_index_in_dim(norm_grads, place ^ bits, 1, keepdims=False)
        norm_sum = norm_sum + flip_quad(piece, bits)
    norm_rows = jnp.pad(norm_sum[:, None, :].astype(BF16), ((0, 0), (0, 0), (0, D - 2 * norm_part)))
    patch_summed = line_y_scatter(jnp.concatenate([grad_patch_mat, norm_rows], axis=1))

    def x_restore(summed):
        shaped = summed.reshape(2, shard_rows, -1)
        own = lax.dynamic_index_in_dim(shaped, x_here, 0, keepdims=False)
        theirs = lax.dynamic_index_in_dim(shaped, 1 - x_here, 0, keepdims=False)
        return pair_up(own, flip_dp(theirs.astype(BF16), 1).astype(F32), x_here)

    global_summed = x_restore(global_summed)
    attend_global = global_summed[..., :attend_columns]
    forward_global = global_summed[..., attend_columns:]

    def x_columns(source, start, width):
        return jnp.concatenate([source[0, :, start : start + width], source[1, :, start : start + width]], axis=1)

    half_heads, half_hidden = heads_width // 2, hidden_width // 2
    joint_out = jnp.stack(
        [
            jnp.stack([x_columns(attend_global, k * half_heads, half_heads) for k in range(3)], axis=1),
            local_summed[:, : 3 * heads_width].reshape(shard_rows, 3, heads_width),
        ]
    )
    output_out = jnp.stack(
        [
            jnp.transpose(x_columns(attend_global, 3 * half_heads, half_heads)),
            jnp.transpose(local_summed[:, 3 * heads_width : 4 * heads_width]),
        ]
    )
    up_out = jnp.stack([x_columns(forward_global, 0, half_hidden), local_summed[:, 4 * heads_width : 4 * heads_width + hidden_width]])
    down_out = jnp.stack(
        [
            jnp.transpose(x_columns(forward_global, half_hidden, half_hidden)),
            jnp.transpose(local_summed[:, 4 * heads_width + hidden_width :]),
        ]
    )
    return (
        outcome[None],
        grad_input,
        patch_summed[:proj_rows],
        jnp.transpose(grad_proj),
        joint_out,
        output_out,
        up_out,
        down_out,
        patch_summed[proj_rows, :norm_part],
        patch_summed[proj_rows, norm_part : 2 * norm_part],
    )


def solution(mesh):
    placed = (
        P("dp", "tensor", None),
        P("dp"),
        P(("dp", "tensor"), None),
        P(None, ("dp", "tensor")),
        P(None, "dp", None, "tensor"),
        P(None, "tensor", "dp"),
        P(None, "dp", "tensor"),
        P(None, "tensor", "dp"),
        P(("dp", "tensor")),
        P(("dp", "tensor")),
        P("dp", "tensor", None),
    )
    return jax.shard_map(
        shards,
        mesh=mesh,
        in_specs=placed,
        out_specs=(
            P("dp", "tensor", None),
            P("dp", "tensor", None),
            P(("dp", "tensor"), None),
            P(None, ("dp", "tensor")),
            P(None, "dp", None, "tensor"),
            P(None, "tensor", "dp"),
            P(None, "dp", "tensor"),
            P(None, "tensor", "dp"),
            P(("dp", "tensor")),
            P(("dp", "tensor")),
        ),
        check_vma=False,
    )
```

```python
import jax
import jax.numpy as jnp
from jax import lax
from jax.experimental import pallas as pl
from jax.experimental.pallas import tpu as pltpu
from jax.sharding import PartitionSpec as P

D = 768
HD = 64
P_SIZE = 8
NORMS = 4
QUAD = 4

EPSILON = 1e-05
NEGATIVE = -1e30
BF16 = jnp.bfloat16
F32 = jnp.float32


def dp_size():
    return lax.axis_size("dp")


def line_size():
    return dp_size() // 4


def x_place():
    return lax.axis_index("dp") % 2


def y_place():
    return (lax.axis_index("dp") // 2) % 2


def line_place():
    return lax.axis_index("dp") // 4


def quad_place():
    return x_place() * 2 + lax.axis_index("tensor")


def flip_dp(values_in, bit):
    return lax.ppermute(values_in, "dp", [(i, i ^ bit) for i in range(dp_size())])


def flip_core(values_in):
    return lax.ppermute(values_in, "tensor", [(0, 1), (1, 0)])


def flip_quad(values_in, bits):
    return lax.ppermute(
        values_in, ("dp", "tensor"), [(i, i ^ bits) for i in range(2 * dp_size())]
    )


def step_line(values_in, offset):
    count = dp_size()
    return lax.ppermute(values_in, "dp", [(i, (i + 4 * offset) % count) for i in range(count)])


def after(values_in, *earlier):
    return lax.optimization_barrier((values_in,) + earlier)[0]


def line_groups():
    return [[line * 4 + rest for line in range(line_size())] for rest in range(4)]


def pick(place, choices):
    if len(choices) == 2:
        return lax.select_n(place == 1, *choices)
    return lax.select_n(place, *choices)


class LineQueue:
    def __init__(self):
        self.arrived = [(), ()]

    def step(self, values_in):
        got = step_line(after(values_in, *self.arrived.pop(0)), 1)
        self.arrived.append((got,))
        return got

    def hold(self, *earlier):
        self.arrived[0] = self.arrived[0] + earlier


def line_pass(values_in, queue, holds=()):
    count = line_size()
    if count > 4:
        whole = lax.all_gather(values_in, "dp", axis=0, axis_index_groups=line_groups())
        return [whole[slot] for slot in range(count)]
    got = [values_in]
    for step in range(1, count):
        if step == count - 1 and holds:
            queue.hold(*holds)
        got.append(queue.step(got[-1]))
    return got


def line_place_blocks(got):
    count = len(got)
    if count == 1:
        return got[0][None]
    if count > 4:
        return jnp.stack(got)
    place = line_place()
    return jnp.stack(
        [pick(place, [got[(here - slot) % count] for here in range(count)]) for slot in range(count)]
    )


def line_gather(values_in, queue):
    return line_place_blocks(line_pass(values_in, queue))


def pair_up(own, other, place):
    return jnp.stack([pick(place, [own, other]), pick(place, [other, own])], axis=0)


def y_gather(lined):
    other = flip_dp(lined, 2)
    place = y_place()
    return jnp.stack([pick(place, [lined, other]), pick(place, [other, lined])], axis=1)


def line_scatter(parts, marks=None):
    count = line_size()
    if count > 4:
        return lax.psum_scatter(
            parts.astype(F32), "dp", scatter_dimension=0, axis_index_groups=line_groups(), tiled=False
        )
    place = line_place()

    def slot(offset):
        return lax.dynamic_index_in_dim(parts, (place + count + offset) % count, 0, keepdims=False)

    total = slot(-1).astype(F32)
    for back in range(2, count + 1):
        got = step_line(total.astype(BF16), 1)
        if marks is not None:
            marks.append(got)
        total = slot(-back).astype(F32) + got.astype(F32)
    return total


def halve(parts, place, axis, bit):
    own = lax.dynamic_index_in_dim(parts, place, axis, keepdims=False)
    theirs = lax.dynamic_index_in_dim(parts, 1 - place, axis, keepdims=False)
    return own.astype(F32) + flip_dp(theirs.astype(BF16), bit).astype(F32)


def y_scatter(parts):
    return halve(parts.reshape((line_size(), 2) + parts.shape[1:]), y_place(), 1, 2)


def line_y_scatter(parts):
    return line_scatter(y_scatter(parts))


def quad_gather(values_in):
    return jnp.concatenate(
        [values_in] + [flip_quad(values_in, bits) for bits in range(1, QUAD)], axis=0
    )


def quad_scatter(partial_value):
    rows = partial_value.shape[0] // QUAD
    low = partial_value.astype(BF16)
    total = partial_value[:rows].astype(F32)
    for bits in range(1, QUAD):
        total = total + flip_quad(low[bits * rows : (bits + 1) * rows], bits).astype(F32)
    return total


def quad_deal(blocks):
    place = quad_place()
    taken = []
    for bits in range(QUAD):
        piece = lax.dynamic_index_in_dim(blocks, place ^ bits, 2, keepdims=False)
        taken.append(flip_quad(piece, bits) if bits else piece)
    return jnp.concatenate(taken, axis=0)


def quad_collect(blocks):
    rows = blocks.shape[0] // QUAD
    place = quad_place()
    got = [
        flip_quad(blocks[bits * rows : (bits + 1) * rows], bits)
        if bits
        else blocks[bits * rows : (bits + 1) * rows]
        for bits in range(QUAD)
    ]
    return jnp.stack(
        [pick(place, [got[slot ^ here] for here in range(QUAD)]) for slot in range(QUAD)], axis=2
    )


def layer_norm(stream, gain_row, bias_row):
    average = jnp.mean(stream, axis=-1, keepdims=True)
    centered = stream - average
    variance = jnp.mean(centered * centered, axis=-1, keepdims=True)
    return centered * lax.rsqrt(variance + EPSILON) * gain_row + bias_row


def dot_nn(left, right):
    return lax.dot_general(left, right, (((1,), (0,)), ((), ())), preferred_element_type=F32)


def dot_nt(left, right):
    return lax.dot_general(left, right, (((1,), (1,)), ((), ())), preferred_element_type=F32)


def dot_tn(left, right):
    return lax.dot_general(left, right, (((0,), (0,)), ((), ())), preferred_element_type=F32)


def split_heads(packed, group_size):
    row_count, columns = packed.shape
    head_count = columns // (3 * HD)
    shaped = packed.reshape(row_count // group_size, group_size, 3, head_count, HD)
    return shaped[:, :, 0], shaped[:, :, 1], shaped[:, :, 2]


def causal_scores(queries, keys_all, places):
    scores = jnp.einsum(
        "gihe,gjhe->ghij", queries, keys_all, preferred_element_type=F32
    ) * HD ** (-0.5)
    return jnp.where(places[:, None] >= places[None, :], scores, NEGATIVE)


def attend_forward(packed, places):
    queries, keys_all, values_all = split_heads(packed, places.shape[0])
    scores = causal_scores(queries, keys_all, places)
    row_max = jnp.max(scores, axis=-1, keepdims=True)
    shifted = jnp.exp(scores - row_max)
    softened = shifted / jnp.sum(shifted, axis=-1, keepdims=True)
    mixture = jnp.einsum(
        "ghij,gjhe->gihe", softened.astype(BF16), values_all, preferred_element_type=F32
    )
    return mixture.reshape(packed.shape[0], -1).astype(BF16), softened


def attend_backward(packed, softened, grad_mix, places):
    queries, keys_all, values_all = split_heads(packed, places.shape[0])
    grad_heads = grad_mix.reshape(queries.shape)
    grad_soft = jnp.einsum(
        "gihe,gjhe->ghij", grad_heads, values_all, preferred_element_type=F32
    )
    centre = jnp.sum(grad_soft * softened, axis=-1, keepdims=True)
    grad_scores = (softened * (grad_soft - centre)).astype(BF16)
    grad_values = jnp.einsum(
        "ghij,gihe->gjhe", softened.astype(BF16), grad_heads, preferred_element_type=F32
    )
    grad_queries = jnp.einsum(
        "ghij,gjhe->gihe", grad_scores, keys_all, preferred_element_type=F32
    ) * HD ** (-0.5)
    grad_keys = jnp.einsum(
        "ghij,gihe->gjhe", grad_scores, queries, preferred_element_type=F32
    ) * HD ** (-0.5)
    row_count = packed.shape[0]
    return jnp.concatenate(
        [part.reshape(row_count, -1) for part in (grad_queries, grad_keys, grad_values)], axis=1
    ).astype(BF16)


def layer_forward(stream, attend_of, forward_of, gain_rows, bias_rows, norm_index, places):
    normed = layer_norm(stream, gain_rows[norm_index], bias_rows[norm_index]).astype(BF16)
    normed_all = quad_gather(normed)
    joint_proj, output_proj = attend_of()
    packed = dot_nn(normed_all, joint_proj).astype(BF16)
    mixture, softened = attend_forward(packed, places)
    middle = stream + quad_scatter(dot_nt(mixture, output_proj))
    second_all = quad_gather(
        layer_norm(middle, gain_rows[norm_index + 1], bias_rows[norm_index + 1]).astype(BF16)
    )
    upward, downward = forward_of(normed_all)
    hidden = dot_nn(second_all, upward)
    active = jax.nn.gelu(hidden).astype(BF16)
    outcome = middle + quad_scatter(dot_nt(active, downward))
    return (
        outcome,
        (stream, normed_all, packed, mixture, softened, middle, second_all, hidden, active),
        (joint_proj, output_proj, upward, downward),
    )


def layer_backward(grad_layer, saved, weights, gain_rows, bias_rows, norm_index, places, ties):
    stream, normed_all, packed, mixture, softened, middle, second_all, hidden, active = saved
    joint_proj, output_proj, upward, downward = weights
    grad_all = quad_gather(after(grad_layer.astype(BF16), *ties[0]))
    grad_active = dot_nn(grad_all, downward)
    gelu_value, gelu_pull = jax.vjp(jax.nn.gelu, hidden)
    grad_hidden = gelu_pull(grad_active)[0].astype(BF16)
    grad_second = quad_scatter(after(dot_nt(grad_hidden, upward), *ties[1]))
    forward_grads = jnp.concatenate(
        [dot_tn(second_all, grad_hidden).astype(BF16), dot_tn(grad_all, active).astype(BF16)], axis=1
    )
    norm_value, second_pull = jax.vjp(
        layer_norm, middle, gain_rows[norm_index + 1], bias_rows[norm_index + 1]
    )
    grad_middle_norm, grad_gain_two, grad_bias_two = second_pull(grad_second)
    grad_middle = grad_layer + grad_middle_norm
    grad_branch = quad_gather(after(grad_middle.astype(BF16), forward_grads, *ties[2]))
    grad_mix = dot_nn(grad_branch, output_proj).astype(BF16)
    forward_half = y_scatter(forward_grads.reshape(ties[5] + (-1,)))
    grad_packed = attend_backward(packed, softened, grad_mix, places)
    grad_normed = quad_scatter(after(dot_nt(grad_packed, joint_proj), *ties[3]))
    attend_grads = jnp.concatenate(
        [dot_tn(normed_all, grad_packed).astype(BF16), dot_tn(grad_branch, mixture).astype(BF16)], axis=1
    )
    first_value, first_pull = jax.vjp(
        layer_norm, stream, gain_rows[norm_index], bias_rows[norm_index]
    )
    grad_stream_norm, grad_gain_one, grad_bias_one = first_pull(grad_normed)
    grad_stream = grad_middle + grad_stream_norm
    grad_start = quad_gather(after(grad_stream.astype(BF16), *ties[4]))
    attend_half = y_scatter(attend_grads.reshape(ties[5] + (-1,)))
    return (
        grad_start,
        attend_half,
        forward_half,
        (grad_gain_one, grad_gain_two),
        (grad_bias_one, grad_bias_two),
    )


def norm_forward(stream, gain_row, bias_row):
    centered = stream - jnp.mean(stream, axis=-1, keepdims=True)
    scale = lax.rsqrt(jnp.mean(centered * centered, axis=-1, keepdims=True) + EPSILON)
    unit = centered * scale
    return unit * gain_row + bias_row, unit, scale


def norm_backward(grad_out, unit, scale, gain_row):
    grad_unit = grad_out * gain_row
    first = jnp.mean(grad_unit, axis=-1, keepdims=True)
    second = jnp.mean(grad_unit * unit, axis=-1, keepdims=True)
    grad_in = scale * (grad_unit - first - unit * second)
    grad_gain = jnp.sum(grad_out * unit, axis=0, keepdims=True)
    grad_bias = jnp.sum(grad_out, axis=0, keepdims=True)
    return grad_in, grad_gain, grad_bias


GELU_A = 0.7978845608028654
GELU_B = 0.044715
TILE = 256
BAND = 128
PAIR = 2 * HD


def local_body(tiles, wide, *refs):
    @pl.when(pl.program_id(0) < tiles)
    def _():
        local_rows(wide, *refs)

    @pl.when(pl.program_id(0) >= tiles)
    def _():
        local_grads(tiles, wide, *refs)


def local_rows(
    wide,
    scalars_ref, masked_ref, part_0_ref, part_1_ref, part_2_ref, part_3_ref, cotangent_ref,
    gain_ref, bias_ref, first_ref, last_ref,
    result_ref, grad_ref, give_0_ref, give_1_ref, give_2_ref, give_3_ref, norms_ref, weights_out_ref,
    factors_ref, normed_all_ref, branch_all_ref, second_all_ref, grad_out_all_ref,
    turned_ref, branch_turned_ref, probs_ref, stream_ref,
):
    rows = masked_ref.shape[0]
    hidden_width = first_ref.shape[3] // 2 - 2 * wide
    here = pl.ds(pl.multiple_of(pl.program_id(0) * rows, rows), rows)
    normed_ref, branch_ref = normed_all_ref.at[here], branch_all_ref.at[here]
    second_ref, grad_out_ref = second_all_ref.at[here], grad_out_all_ref.at[here]

    def factor(start, width):
        return [factors_ref.at[side, here, start : start + width] for side in range(2)]

    grad_joints, grad_values = factor(0, 2 * wide), factor(2 * wide, wide)
    mixtures = factor(3 * wide, wide)
    hiddens = factor(4 * wide, hidden_width)
    actives = factor(4 * wide + hidden_width, hidden_width)

    def weight(side, start, stop):
        return (first_ref, last_ref)[side][:, 0, :, start:stop].reshape(D, stop - start)

    bands = rows // BAND
    pairs = wide // PAIR

    row = pl.program_id(0) * rows + lax.broadcasted_iota(jnp.int32, (rows, 1), 0)
    keep = (row < scalars_ref[0]).astype(F32)
    place = scalars_ref[1]
    part_width = D // QUAD
    for slot in range(QUAD):
        columns = slice(slot * part_width, (slot + 1) * part_width)
        for bits, part_ref in enumerate((part_0_ref, part_1_ref, part_2_ref, part_3_ref)):

            @pl.when((place ^ bits) == slot)
            def _(part_ref=part_ref, columns=columns):
                stream_ref[:, columns] = masked_ref[:, columns].astype(F32) + part_ref[...].astype(F32)

    stream = stream_ref[...]
    gain_one, gain_two = gain_ref[2:3, :], gain_ref[3:4, :]
    normed, unit_one, scale_one = norm_forward(stream, gain_one, bias_ref[2:3, :])
    normed = normed.astype(BF16)
    normed_ref[...] = normed
    packs = [dot_nn(normed, weight(side, 0, 3 * wide)).astype(BF16) for side in range(2)]

    lanes = lax.broadcasted_iota(jnp.int32, (BAND, PAIR), 1)
    low_head = lanes < HD
    down_rows = lax.broadcasted_iota(jnp.int32, (2 * BAND, BAND), 0) % BAND
    key_rows = lax.broadcasted_iota(jnp.int32, (2 * BAND, BAND), 1)
    allowed = (down_rows // P_SIZE == key_rows // P_SIZE) & (down_rows >= key_rows)

    def apart(pair_values):
        zero = jnp.zeros_like(pair_values)
        return jnp.concatenate(
            [jnp.where(low_head, pair_values, zero), jnp.where(low_head, zero, pair_values)], axis=0
        )

    def joined(stacked):
        return jnp.where(low_head, stacked[:BAND], stacked[BAND:])

    def piece(values_in, band, part, pair):
        start = part * wide + pair * PAIR
        return values_in[band * BAND : (band + 1) * BAND, start : start + PAIR]

    scale = HD ** (-0.5)
    for side in range(2):
        for band in range(bands):
            for pair in range(pairs):
                queries = apart(piece(packs[side], band, 0, pair)) * jnp.asarray(scale, BF16)
                scores = dot_nt(queries, piece(packs[side], band, 1, pair))
                scores = jnp.where(allowed, scores, NEGATIVE)
                shifted = jnp.exp(scores - jnp.max(scores, axis=-1, keepdims=True))
                probs = shifted / jnp.sum(shifted, axis=-1, keepdims=True)
                probs_ref[(side * bands + band) * pairs + pair] = probs
                mixed = dot_nn(probs.astype(BF16), piece(packs[side], band, 2, pair))
                mixtures[side][
                    band * BAND : (band + 1) * BAND, pair * PAIR : (pair + 1) * PAIR
                ] = joined(mixed).astype(BF16)

    middle = stream
    for side in range(2):
        middle = middle + dot_nt(mixtures[side][...], weight(side, 3 * wide, 4 * wide))
    second, unit_two, scale_two = norm_forward(middle, gain_two, bias_ref[3:4, :])
    second = second.astype(BF16)
    second_ref[...] = second
    grad_final = cotangent_ref[...].astype(F32) * keep
    grad_out = grad_final.astype(BF16)
    grad_out_ref[...] = grad_out

    lifted = jnp.zeros_like(middle)
    grad_second = jnp.zeros_like(middle)
    chunk = min(768, hidden_width)
    for side in range(2):
        for start in range(0, hidden_width, chunk):
            first = 4 * wide + start
            upward = weight(side, first, first + chunk)
            downward = weight(side, first + hidden_width, first + hidden_width + chunk)
            hidden = dot_nn(second, upward)
            square = hidden * hidden
            bent = jnp.tanh(GELU_A * hidden * (1.0 + GELU_B * square))
            half = 0.5 * (1.0 + bent)
            active = (hidden * half).astype(BF16)
            slope = half + 0.5 * hidden * (1.0 - bent * bent) * GELU_A * (1.0 + 3.0 * GELU_B * square)
            actives[side][:, start : start + chunk] = active
            lifted = lifted + dot_nt(active, downward)
            grad_hidden = (dot_nn(grad_out, downward) * slope).astype(BF16)
            hiddens[side][:, start : start + chunk] = grad_hidden
            grad_second = grad_second + dot_nt(grad_hidden, upward)
    result_ref[...] = (middle + lifted).astype(BF16)

    grad_in, gain_grad_two, bias_grad_two = norm_backward(grad_second, unit_two, scale_two, gain_two)
    grad_middle = grad_final + grad_in
    branch = grad_middle.astype(BF16)
    branch_ref[...] = branch
    grad_normed = jnp.zeros_like(middle)
    for side in range(2):
        grad_mix = dot_nn(branch, weight(side, 3 * wide, 4 * wide)).astype(BF16)
        for band in range(bands):
            for pair in range(pairs):
                probs = probs_ref[(side * bands + band) * pairs + pair]
                grad_pair = apart(piece(grad_mix, band, 0, pair))
                grad_soft = dot_nt(grad_pair, piece(packs[side], band, 2, pair))
                centre = jnp.sum(grad_soft * probs, axis=-1, keepdims=True)
                grad_scores = (probs * (grad_soft - centre)).astype(BF16)
                queries = apart(piece(packs[side], band, 0, pair))
                grads = (
                    joined(dot_nn(grad_scores, piece(packs[side], band, 1, pair))) * scale,
                    dot_tn(grad_scores, queries) * scale,
                    dot_tn(probs.astype(BF16), grad_pair),
                )
                rows_here = slice(band * BAND, (band + 1) * BAND)
                for part in range(2):
                    first = part * wide + pair * PAIR
                    grad_joints[side][rows_here, first : first + PAIR] = grads[part].astype(BF16)
                grad_values[side][rows_here, pair * PAIR : (pair + 1) * PAIR] = grads[2].astype(BF16)
        grad_normed = grad_normed + dot_nt(grad_joints[side][...], weight(side, 0, 2 * wide))
        grad_normed = grad_normed + dot_nt(grad_values[side][...], weight(side, 2 * wide, 3 * wide))
    grad_in, gain_grad_one, bias_grad_one = norm_backward(grad_normed, unit_one, scale_one, gain_one)
    grad_stream = grad_middle + grad_in
    grad_ref[...] = grad_stream
    for slot in range(QUAD):
        columns = slice(slot * part_width, (slot + 1) * part_width)
        for bits, give_ref in enumerate((give_0_ref, give_1_ref, give_2_ref, give_3_ref)):

            @pl.when((place ^ bits) == slot)
            def _(give_ref=give_ref, columns=columns):
                give_ref[...] = grad_stream[:, columns].astype(BF16)


    @pl.when(pl.program_id(0) == 0)
    def _():
        norms_ref[...] = jnp.zeros_like(norms_ref)

    for place, value in enumerate((gain_grad_one, gain_grad_two, bias_grad_one, bias_grad_two)):
        norms_ref[place : place + 1, :] += value


def local_grads(
    tiles, wide,
    scalars_ref, masked_ref, part_0_ref, part_1_ref, part_2_ref, part_3_ref, cotangent_ref,
    gain_ref, bias_ref, first_ref, last_ref,
    result_ref, grad_ref, give_0_ref, give_1_ref, give_2_ref, give_3_ref, norms_ref, weights_out_ref,
    factors_ref, normed_ref, branch_ref, second_ref, grad_out_ref,
    turned_ref, branch_turned_ref, probs_ref, stream_ref,
):
    step = pl.program_id(0) - tiles
    block, side = step // 2, step % 2
    width = weights_out_ref.shape[3]

    @pl.when(step == 0)
    def _():
        turned_ref[...] = normed_ref[...].T
        branch_turned_ref[...] = branch_ref[...].T

    @pl.when(step == 2)
    def _():
        turned_ref[...] = second_ref[...].T

    @pl.when(step == 4)
    def _():
        turned_ref[...] = grad_out_ref[...].T

    def give(left_ref, right, columns):
        product = dot_nn(left_ref[...], right).astype(BF16)
        weights_out_ref[:, :, :, columns] = product.reshape(
            weights_out_ref.shape[:3] + (product.shape[1],)
        )

    @pl.when(block == 0)
    def _():
        give(turned_ref, factors_ref[side, :, : 3 * wide], slice(0, 3 * wide))
        give(branch_turned_ref, factors_ref[side, :, 3 * wide : 4 * wide], slice(3 * wide, 4 * wide))

    @pl.when(block != 0)
    def _():
        start = pl.multiple_of(block * width, width)
        give(turned_ref, factors_ref[side, :, pl.ds(start, width)], slice(None))


def local_layer(scalars, masked_low, spread_parts, cotangent, gain_rows, bias_rows, weights, wide):
    rows = masked_low.shape[0]
    tiles = rows // TILE
    columns = weights.shape[3]
    width = 4 * wide
    assert columns == 3 * width
    tiled = lambda size: pl.BlockSpec((TILE, size), lambda i: (jnp.minimum(i, tiles - 1), 0))
    fixed = lambda array: pl.BlockSpec(array.shape, lambda i: (0, 0), pipeline_mode=pl.Buffered(1))
    outs = [(D, BF16), (D, F32)] + [(D // QUAD, BF16)] * QUAD

    def grads_place(i):
        step = jnp.maximum(i - tiles, 0)
        return (0, step % 2, 0, step // 2)

    return pl.pallas_call(
        lambda *refs: local_body(tiles, wide, *refs),
        grid=(tiles + 2 * (columns // width),),
        in_specs=[pl.BlockSpec(memory_space=pltpu.SMEM)]
        + [tiled(D)] + [tiled(D // QUAD)] * QUAD + [tiled(D)]
        + [fixed(array) for array in (gain_rows, bias_rows)]
        + [
            pl.BlockSpec(
                (weights.shape[0], 1) + weights.shape[2:],
                lambda i, side=side: (0, side, 0, 0),
                pipeline_mode=pl.Buffered(1),
            )
            for side in range(2)
        ],
        out_specs=[tiled(size) for size, _ in outs]
        + [
            pl.BlockSpec((8, D), lambda i: (0, 0)),
            pl.BlockSpec((weights.shape[0], 1, weights.shape[2], width), grads_place),
        ],
        out_shape=[jax.ShapeDtypeStruct((rows, size), kind) for size, kind in outs]
        + [jax.ShapeDtypeStruct((8, D), F32), jax.ShapeDtypeStruct(weights.shape, BF16)],
        scratch_shapes=[pltpu.VMEM((2, rows, columns), BF16)]
        + [pltpu.VMEM((rows, D), BF16)] * 4
        + [pltpu.VMEM((D, rows), BF16)] * 2
        + [
            pltpu.VMEM((2 * (TILE // BAND) * (wide // PAIR), 2 * BAND, BAND), F32),
            pltpu.VMEM((TILE, D), F32),
        ],
        compiler_params=pltpu.CompilerParams(
            dimension_semantics=("arbitrary",), vmem_limit_bytes=58 * 1024 * 1024
        ),
        cost_estimate=pl.CostEstimate(
            flops=12 * rows * D * columns,
            transcendentals=rows * columns,
            bytes_accessed=2 * 4 * D * columns,
        ),
    )(scalars, masked_low, *spread_parts, cotangent, gain_rows, bias_rows, weights, weights)


def shards(
    embedded,
    lengths,
    patch_proj,
    global_proj,
    qkv_weight,
    out_weight,
    up_weight,
    down_weight,
    norm_gain,
    norm_bias,
    cotangent,
):
    half_rows = embedded.shape[1]
    patch_rows = half_rows // P_SIZE
    shard_rows = qkv_weight.shape[1]
    proj_rows = patch_proj.shape[0]
    norm_part = norm_gain.shape[0]
    cells = 2 * line_size()
    heads_width = qkv_weight.shape[3]
    hidden_width = up_weight.shape[2]
    x_here = x_place()

    positions = lax.axis_index("tensor") * half_rows + jnp.arange(half_rows, dtype=jnp.int32)
    keep_mask = (positions < lengths[0]).astype(F32)[:, None]
    masked_low = jnp.where(keep_mask > 0, embedded[0], jnp.zeros_like(embedded[0]))
    masked_low = lax.optimization_barrier(masked_low)

    joint_part = jnp.transpose(qkv_weight, (0, 2, 1, 3))
    output_part = jnp.transpose(out_weight, (0, 2, 1))
    down_part = jnp.transpose(down_weight, (0, 2, 1))

    norm_row = jnp.pad(
        jnp.concatenate([norm_gain, norm_bias]).reshape(1, -1), ((0, 0), (0, D - 2 * norm_part))
    )
    local_shard = jnp.concatenate(
        [joint_part[1, 0], joint_part[1, 1], joint_part[1, 2], output_part[1], up_weight[1], down_part[1]],
        axis=-1,
    )
    local_whole = lax.all_gather(local_shard, ("dp", "tensor"), axis=0)

    patch_pieces = masked_low.reshape(patch_rows, cells, QUAD, proj_rows)
    patches_dealt = quad_deal(patch_pieces)
    queue = LineQueue()
    patch_lined = line_gather(jnp.concatenate([patch_proj, norm_row], axis=0), queue)
    patch_whole = y_gather(patch_lined)
    patch_whole = patch_whole.reshape(cells, proj_rows + 1, D)
    patch_mat = patch_whole[:, :proj_rows].reshape(cells * proj_rows, D)
    norm_cells = patch_whole[:, proj_rows, : 2 * norm_part]
    norm_all = quad_collect(
        jnp.broadcast_to(norm_cells[None], (QUAD,) + norm_cells.shape)
    )[0].astype(F32)
    gain_rows = norm_all[..., :norm_part].reshape(NORMS, D)
    bias_rows = norm_all[..., norm_part:].reshape(NORMS, D)
    gain_rows, bias_rows = lax.optimization_barrier((gain_rows, bias_rows))

    def x_half(part):
        return part.reshape(part.shape[:-1] + (2, part.shape[-1] // 2))

    def global_part(layer):
        pieces = []
        for piece in (
            joint_part[layer, 0],
            joint_part[layer, 1],
            joint_part[layer, 2],
            output_part[layer],
            up_weight[layer],
            down_part[layer],
        ):
            halves = x_half(piece)
            pieces.append(halves)
        return jnp.concatenate(pieces, axis=-1)

    halves = global_part(0)
    own_half = lax.dynamic_index_in_dim(halves, x_here, 1, keepdims=False)
    their_half = lax.dynamic_index_in_dim(halves, 1 - x_here, 1, keepdims=False)
    global_shard = pair_up(own_half, flip_dp(their_half, 1), x_here)
    global_shard = global_shard.reshape(2 * shard_rows, -1)
    attend_columns = 2 * heads_width
    global_blocks = line_pass(global_shard, queue, (patch_whole,))
    queue.hold(global_blocks[-1])
    attend_lined = line_place_blocks([block[:, :attend_columns] for block in global_blocks])
    forward_lined = line_place_blocks([block[:, attend_columns:] for block in global_blocks])
    proj_part = jnp.transpose(global_proj)
    proj_pair = pair_up(proj_part, flip_dp(proj_part, 2), y_place())
    spread_lined = line_gather(proj_pair, queue)
    joint_columns = 3 * heads_width // 2

    patches_mat = patches_dealt.reshape(QUAD * patch_rows, cells * proj_rows)
    start_partial = dot_nn(patches_mat, patch_mat)
    initial = quad_scatter(start_partial)

    def attend_of():
        whole = y_gather(after(attend_lined, start_partial)).reshape(D, -1)
        return whole[:, :joint_columns], whole[:, joint_columns:]

    def forward_of(marker):
        whole = y_gather(after(forward_lined, marker)).reshape(D, -1)
        return whole[:, : hidden_width // 2], whole[:, hidden_width // 2 :]

    core = lax.axis_index("tensor")
    steps = jnp.arange(patch_rows, dtype=jnp.int32)
    global_places = jnp.concatenate([core * patch_rows + steps, (1 - core) * patch_rows + steps])
    global_out, first_saved, first_weights = layer_forward(
        initial, attend_of, forward_of, gain_rows, bias_rows, 0, global_places
    )
    spread_mat = spread_lined.reshape(cells * proj_rows, D)
    global_low = quad_gather(global_out.astype(BF16))
    spread_dealt = dot_nt(global_low, spread_mat).astype(BF16)
    spread_blocks = spread_dealt.reshape(QUAD * patch_rows, cells, proj_rows)
    byte_cells = cells == P_SIZE
    if byte_cells:
        part_place = quad_place()
        spread_parts = [
            spread_blocks[bits * patch_rows : (bits + 1) * patch_rows] for bits in range(QUAD)
        ]
        spread_parts = [
            (flip_quad(part, bits) if bits else part).reshape(half_rows, proj_rows)
            for bits, part in enumerate(spread_parts)
        ]
    else:
        part_place = jnp.int32(0)
        spread = quad_collect(spread_blocks).reshape(half_rows, D)
        spread_parts = jnp.split(spread, QUAD, axis=1)

    dp = dp_size()
    whole_rows = shard_rows % 16 == 0
    local_weights = local_whole.reshape(dp, 2, shard_rows, -1)
    if not whole_rows:
        local_weights = jnp.transpose(local_weights, (1, 0, 2, 3)).reshape(1, 2, D, -1)
    bound = jnp.clip(lengths[0] - lax.axis_index("tensor") * half_rows, 0, half_rows)
    scalars = jnp.stack([bound, part_place.astype(jnp.int32)])
    local_outs = local_layer(
        scalars, masked_low, spread_parts, cotangent[0], gain_rows, bias_rows, local_weights, heads_width
    )
    outcome, grad_local = local_outs[:2]
    grad_parts = local_outs[2 : 2 + QUAD]
    local_norms, local_grads_out = local_outs[2 + QUAD :]
    second_gains, second_biases = (local_norms[0], local_norms[1]), (local_norms[2], local_norms[3])
    if byte_cells:
        spread_grads = jnp.concatenate(
            [
                (flip_quad(part, bits) if bits else part).reshape(patch_rows, cells, proj_rows)
                for bits, part in enumerate(grad_parts)
            ],
            axis=0,
        )
    else:
        grad_low = jnp.concatenate(grad_parts, axis=1)
        spread_grads = quad_deal(grad_low.reshape(patch_rows, cells, QUAD, proj_rows))
    spread_grads = spread_grads.reshape(QUAD * patch_rows, cells * proj_rows)
    if not whole_rows:
        local_grads_out = jnp.transpose(
            local_grads_out.reshape(2, dp, shard_rows, -1), (1, 0, 2, 3)
        )
    local_summed = lax.psum_scatter(
        local_grads_out.reshape(2 * dp, shard_rows, -1), ("dp", "tensor"), scatter_dimension=0
    ).astype(F32)

    grad_global = quad_scatter(dot_nn(spread_grads, spread_mat))
    proj_grads = dot_tn(spread_grads, global_low).astype(BF16).reshape(cells, proj_rows, D)
    marks = []
    grad_proj = line_scatter(proj_grads.reshape(line_size(), 2, proj_rows, D), marks)
    grad_proj = halve(grad_proj, y_place(), 0, 2)
    ties = ((), (), tuple(marks[:1]), (), tuple(marks[1:2]), (cells, 2 * shard_rows))
    grad_start, attend_half, forward_half, first_gains, first_biases = layer_backward(
        grad_global, first_saved, first_weights, gain_rows, bias_rows, 0, global_places, ties
    )
    global_summed = line_scatter(jnp.concatenate([attend_half, forward_half], axis=2))
    grad_patch_mat = dot_tn(patches_mat, grad_start).astype(BF16).reshape(cells, proj_rows, D)
    gain_grads = jnp.stack([first_gains[0], first_gains[1], second_gains[0], second_gains[1]])
    bias_grads = jnp.stack([first_biases[0], first_biases[1], second_biases[0], second_biases[1]])
    norm_grads = jnp.concatenate(
        [
            gain_grads.reshape(cells, QUAD, norm_part),
            bias_grads.reshape(cells, QUAD, norm_part),
        ],
        axis=2,
    )
    place = quad_place()
    norm_sum = lax.dynamic_index_in_dim(norm_grads, place, 1, keepdims=False)
    for bits in range(1, QUAD):
        piece = lax.dynamic_index_in_dim(norm_grads, place ^ bits, 1, keepdims=False)
        norm_sum = norm_sum + flip_quad(piece, bits)
    norm_rows = jnp.pad(norm_sum[:, None, :].astype(BF16), ((0, 0), (0, 0), (0, D - 2 * norm_part)))
    patch_marks = []
    patch_terms = jnp.concatenate([grad_patch_mat, norm_rows], axis=1)
    patch_half = y_scatter(patch_terms)
    patch_summed = line_scatter(patch_half, patch_marks)
    grad_patches = after(dot_nt(grad_start, patch_mat).astype(BF16), forward_half, patch_terms)
    grad_patches = quad_collect(grad_patches.reshape(QUAD * patch_rows, cells, proj_rows))
    grad_patches = grad_patches.reshape(half_rows, D).astype(F32)
    grad_patches = after(grad_patches, *patch_marks[:1])
    grad_input = ((grad_local + grad_patches) * keep_mask).astype(BF16)[None]

    def x_restore(summed):
        shaped = summed.reshape(2, shard_rows, -1)
        own = lax.dynamic_index_in_dim(shaped, x_here, 0, keepdims=False)
        theirs = lax.dynamic_index_in_dim(shaped, 1 - x_here, 0, keepdims=False)
        return pair_up(own, flip_dp(theirs.astype(BF16), 1).astype(F32), x_here)

    global_summed = x_restore(global_summed)
    attend_global = global_summed[..., :attend_columns]
    forward_global = global_summed[..., attend_columns:]

    def x_columns(source, start, width):
        return jnp.concatenate([source[0, :, start : start + width], source[1, :, start : start + width]], axis=1)

    half_heads, half_hidden = heads_width // 2, hidden_width // 2
    joint_out = jnp.stack(
        [
            jnp.stack([x_columns(attend_global, k * half_heads, half_heads) for k in range(3)], axis=1),
            local_summed[:, : 3 * heads_width].reshape(shard_rows, 3, heads_width),
        ]
    )
    output_out = jnp.stack(
        [
            jnp.transpose(x_columns(attend_global, 3 * half_heads, half_heads)),
            jnp.transpose(local_summed[:, 3 * heads_width : 4 * heads_width]),
        ]
    )
    up_out = jnp.stack([x_columns(forward_global, 0, half_hidden), local_summed[:, 4 * heads_width : 4 * heads_width + hidden_width]])
    down_out = jnp.stack(
        [
            jnp.transpose(x_columns(forward_global, half_hidden, half_hidden)),
            jnp.transpose(local_summed[:, 4 * heads_width + hidden_width :]),
        ]
    )
    return (
        outcome[None],
        grad_input,
        patch_summed[:proj_rows],
        jnp.transpose(grad_proj),
        joint_out,
        output_out,
        up_out,
        down_out,
        patch_summed[proj_rows, :norm_part],
        patch_summed[proj_rows, norm_part : 2 * norm_part],
    )


def solution(mesh):
    placed = (
        P("dp", "tensor", None),
        P("dp"),
        P(("dp", "tensor"), None),
        P(None, ("dp", "tensor")),
        P(None, "dp", None, "tensor"),
        P(None, "tensor", "dp"),
        P(None, "dp", "tensor"),
        P(None, "tensor", "dp"),
        P(("dp", "tensor")),
        P(("dp", "tensor")),
        P("dp", "tensor", None),
    )
    return jax.shard_map(
        shards,
        mesh=mesh,
        in_specs=placed,
        out_specs=(
            P("dp", "tensor", None),
            P("dp", "tensor", None),
            P(("dp", "tensor"), None),
            P(None, ("dp", "tensor")),
            P(None, "dp", None, "tensor"),
            P(None, "tensor", "dp"),
            P(None, "dp", "tensor"),
            P(None, "tensor", "dp"),
            P(("dp", "tensor")),
            P(("dp", "tensor")),
        ),
        check_vma=False,
    )
```

```python
import jax
import jax.numpy as jnp
from jax import lax
from jax.experimental import pallas as pl
from jax.experimental.pallas import tpu as pltpu
from jax.sharding import PartitionSpec as P

D = 768
HD = 64
P_SIZE = 8
NORMS = 4
QUAD = 4

EPSILON = 1e-05
NEGATIVE = -1e30
BF16 = jnp.bfloat16
F32 = jnp.float32


def dp_size():
    return lax.axis_size("dp")


def line_size():
    return dp_size() // 4


def x_place():
    return lax.axis_index("dp") % 2


def y_place():
    return (lax.axis_index("dp") // 2) % 2


def line_place():
    return lax.axis_index("dp") // 4


def quad_place():
    return x_place() * 2 + lax.axis_index("tensor")


def flip_dp(values_in, bit):
    return lax.ppermute(values_in, "dp", [(i, i ^ bit) for i in range(dp_size())])


def flip_core(values_in):
    return lax.ppermute(values_in, "tensor", [(0, 1), (1, 0)])


def flip_quad(values_in, bits):
    return lax.ppermute(
        values_in, ("dp", "tensor"), [(i, i ^ bits) for i in range(2 * dp_size())]
    )


def step_line(values_in, offset):
    count = dp_size()
    return lax.ppermute(values_in, "dp", [(i, (i + 4 * offset) % count) for i in range(count)])


def after(values_in, *earlier):
    return lax.optimization_barrier((values_in,) + earlier)[0]


def line_groups():
    return [[line * 4 + rest for line in range(line_size())] for rest in range(4)]


def pick(place, choices):
    if len(choices) == 2:
        return lax.select_n(place == 1, *choices)
    return lax.select_n(place, *choices)


class LineQueue:
    def __init__(self):
        self.arrived = [(), ()]

    def step(self, values_in):
        got = step_line(after(values_in, *self.arrived.pop(0)), 1)
        self.arrived.append((got,))
        return got

    def hold(self, *earlier):
        self.arrived[0] = self.arrived[0] + earlier


def line_pass(values_in, queue, holds=()):
    count = line_size()
    if count > 4:
        whole = lax.all_gather(values_in, "dp", axis=0, axis_index_groups=line_groups())
        return [whole[slot] for slot in range(count)]
    got = [values_in]
    for step in range(1, count):
        if step == count - 1 and holds:
            queue.hold(*holds)
        got.append(queue.step(got[-1]))
    return got


def line_place_blocks(got):
    count = len(got)
    if count == 1:
        return got[0][None]
    if count > 4:
        return jnp.stack(got)
    place = line_place()
    return jnp.stack(
        [pick(place, [got[(here - slot) % count] for here in range(count)]) for slot in range(count)]
    )


def line_gather(values_in, queue):
    return line_place_blocks(line_pass(values_in, queue))


def pair_up(own, other, place):
    return jnp.stack([pick(place, [own, other]), pick(place, [other, own])], axis=0)


def y_gather(lined):
    other = flip_dp(lined, 2)
    place = y_place()
    return jnp.stack([pick(place, [lined, other]), pick(place, [other, lined])], axis=1)


def line_scatter(parts, marks=None):
    count = line_size()
    if count > 4:
        return lax.psum_scatter(
            parts.astype(F32), "dp", scatter_dimension=0, axis_index_groups=line_groups(), tiled=False
        )
    place = line_place()

    def slot(offset):
        return lax.dynamic_index_in_dim(parts, (place + count + offset) % count, 0, keepdims=False)

    total = slot(-1).astype(F32)
    for back in range(2, count + 1):
        got = step_line(total.astype(BF16), 1)
        if marks is not None:
            marks.append(got)
        total = slot(-back).astype(F32) + got.astype(F32)
    return total


def halve(parts, place, axis, bit):
    own = lax.dynamic_index_in_dim(parts, place, axis, keepdims=False)
    theirs = lax.dynamic_index_in_dim(parts, 1 - place, axis, keepdims=False)
    return own.astype(F32) + flip_dp(theirs.astype(BF16), bit).astype(F32)


def y_scatter(parts):
    return halve(parts.reshape((line_size(), 2) + parts.shape[1:]), y_place(), 1, 2)


def line_y_scatter(parts):
    return line_scatter(y_scatter(parts))


def quad_gather(values_in):
    return jnp.concatenate(
        [values_in] + [flip_quad(values_in, bits) for bits in range(1, QUAD)], axis=0
    )


def quad_scatter(partial_value):
    rows = partial_value.shape[0] // QUAD
    low = partial_value.astype(BF16)
    total = partial_value[:rows].astype(F32)
    for bits in range(1, QUAD):
        total = total + flip_quad(low[bits * rows : (bits + 1) * rows], bits).astype(F32)
    return total


def quad_deal(blocks):
    place = quad_place()
    taken = []
    for bits in range(QUAD):
        piece = lax.dynamic_index_in_dim(blocks, place ^ bits, 2, keepdims=False)
        taken.append(flip_quad(piece, bits) if bits else piece)
    return jnp.concatenate(taken, axis=0)


def quad_collect(blocks):
    rows = blocks.shape[0] // QUAD
    place = quad_place()
    got = [
        flip_quad(blocks[bits * rows : (bits + 1) * rows], bits)
        if bits
        else blocks[bits * rows : (bits + 1) * rows]
        for bits in range(QUAD)
    ]
    return jnp.stack(
        [pick(place, [got[slot ^ here] for here in range(QUAD)]) for slot in range(QUAD)], axis=2
    )


def layer_norm(stream, gain_row, bias_row):
    average = jnp.mean(stream, axis=-1, keepdims=True)
    centered = stream - average
    variance = jnp.mean(centered * centered, axis=-1, keepdims=True)
    return centered * lax.rsqrt(variance + EPSILON) * gain_row + bias_row


def dot_nn(left, right):
    return lax.dot_general(left, right, (((1,), (0,)), ((), ())), preferred_element_type=F32)


def dot_nt(left, right):
    return lax.dot_general(left, right, (((1,), (1,)), ((), ())), preferred_element_type=F32)


def dot_tn(left, right):
    return lax.dot_general(left, right, (((0,), (0,)), ((), ())), preferred_element_type=F32)


def split_heads(packed, group_size):
    row_count, columns = packed.shape
    head_count = columns // (3 * HD)
    shaped = packed.reshape(row_count // group_size, group_size, 3, head_count, HD)
    return shaped[:, :, 0], shaped[:, :, 1], shaped[:, :, 2]


def causal_scores(queries, keys_all, places):
    scores = jnp.einsum(
        "gihe,gjhe->ghij", queries, keys_all, preferred_element_type=F32
    ) * HD ** (-0.5)
    return jnp.where(places[:, None] >= places[None, :], scores, NEGATIVE)


def attend_forward(packed, places):
    queries, keys_all, values_all = split_heads(packed, places.shape[0])
    scores = causal_scores(queries, keys_all, places)
    row_max = jnp.max(scores, axis=-1, keepdims=True)
    shifted = jnp.exp(scores - row_max)
    softened = shifted / jnp.sum(shifted, axis=-1, keepdims=True)
    mixture = jnp.einsum(
        "ghij,gjhe->gihe", softened.astype(BF16), values_all, preferred_element_type=F32
    )
    return mixture.reshape(packed.shape[0], -1).astype(BF16), softened


def attend_backward(packed, softened, grad_mix, places):
    queries, keys_all, values_all = split_heads(packed, places.shape[0])
    grad_heads = grad_mix.reshape(queries.shape)
    grad_soft = jnp.einsum(
        "gihe,gjhe->ghij", grad_heads, values_all, preferred_element_type=F32
    )
    centre = jnp.sum(grad_soft * softened, axis=-1, keepdims=True)
    grad_scores = (softened * (grad_soft - centre)).astype(BF16)
    grad_values = jnp.einsum(
        "ghij,gihe->gjhe", softened.astype(BF16), grad_heads, preferred_element_type=F32
    )
    grad_queries = jnp.einsum(
        "ghij,gjhe->gihe", grad_scores, keys_all, preferred_element_type=F32
    ) * HD ** (-0.5)
    grad_keys = jnp.einsum(
        "ghij,gihe->gjhe", grad_scores, queries, preferred_element_type=F32
    ) * HD ** (-0.5)
    row_count = packed.shape[0]
    return jnp.concatenate(
        [part.reshape(row_count, -1) for part in (grad_queries, grad_keys, grad_values)], axis=1
    ).astype(BF16)


def layer_forward(stream, attend_of, forward_of, gain_rows, bias_rows, norm_index, places):
    normed = layer_norm(stream, gain_rows[norm_index], bias_rows[norm_index]).astype(BF16)
    normed_all = quad_gather(normed)
    joint_proj, output_proj = attend_of()
    packed = dot_nn(normed_all, joint_proj).astype(BF16)
    mixture, softened = attend_forward(packed, places)
    middle = stream + quad_scatter(dot_nt(mixture, output_proj))
    second_all = quad_gather(
        layer_norm(middle, gain_rows[norm_index + 1], bias_rows[norm_index + 1]).astype(BF16)
    )
    upward, downward = forward_of(normed_all)
    hidden = dot_nn(second_all, upward)
    active = jax.nn.gelu(hidden).astype(BF16)
    outcome = middle + quad_scatter(dot_nt(active, downward))
    return (
        outcome,
        (stream, normed_all, packed, mixture, softened, middle, second_all, hidden, active),
        (joint_proj, output_proj, upward, downward),
    )


def layer_backward(grad_layer, saved, weights, gain_rows, bias_rows, norm_index, places, ties):
    stream, normed_all, packed, mixture, softened, middle, second_all, hidden, active = saved
    joint_proj, output_proj, upward, downward = weights
    grad_all = quad_gather(after(grad_layer.astype(BF16), *ties[0]))
    grad_active = dot_nn(grad_all, downward)
    gelu_value, gelu_pull = jax.vjp(jax.nn.gelu, hidden)
    grad_hidden = gelu_pull(grad_active)[0].astype(BF16)
    grad_second = quad_scatter(after(dot_nt(grad_hidden, upward), *ties[1]))
    forward_grads = jnp.concatenate(
        [dot_tn(second_all, grad_hidden).astype(BF16), dot_tn(grad_all, active).astype(BF16)], axis=1
    )
    norm_value, second_pull = jax.vjp(
        layer_norm, middle, gain_rows[norm_index + 1], bias_rows[norm_index + 1]
    )
    grad_middle_norm, grad_gain_two, grad_bias_two = second_pull(grad_second)
    grad_middle = grad_layer + grad_middle_norm
    grad_branch = quad_gather(after(grad_middle.astype(BF16), forward_grads, *ties[2]))
    grad_mix = dot_nn(grad_branch, output_proj).astype(BF16)
    forward_half = y_scatter(forward_grads.reshape(ties[5] + (-1,)))
    grad_packed = attend_backward(packed, softened, grad_mix, places)
    grad_normed = quad_scatter(after(dot_nt(grad_packed, joint_proj), *ties[3]))
    attend_grads = jnp.concatenate(
        [dot_tn(normed_all, grad_packed).astype(BF16), dot_tn(grad_branch, mixture).astype(BF16)], axis=1
    )
    first_value, first_pull = jax.vjp(
        layer_norm, stream, gain_rows[norm_index], bias_rows[norm_index]
    )
    grad_stream_norm, grad_gain_one, grad_bias_one = first_pull(grad_normed)
    grad_stream = grad_middle + grad_stream_norm
    grad_start = quad_gather(after(grad_stream.astype(BF16), *ties[4]))
    attend_half = y_scatter(attend_grads.reshape(ties[5] + (-1,)))
    return (
        grad_start,
        attend_half,
        forward_half,
        (grad_gain_one, grad_gain_two),
        (grad_bias_one, grad_bias_two),
    )


def norm_forward(stream, gain_row, bias_row):
    centered = stream - jnp.mean(stream, axis=-1, keepdims=True)
    scale = lax.rsqrt(jnp.mean(centered * centered, axis=-1, keepdims=True) + EPSILON)
    unit = centered * scale
    return unit * gain_row + bias_row, unit, scale


def norm_backward(grad_out, unit, scale, gain_row):
    grad_unit = grad_out * gain_row
    first = jnp.mean(grad_unit, axis=-1, keepdims=True)
    second = jnp.mean(grad_unit * unit, axis=-1, keepdims=True)
    grad_in = scale * (grad_unit - first - unit * second)
    grad_gain = jnp.sum(grad_out * unit, axis=0, keepdims=True)
    grad_bias = jnp.sum(grad_out, axis=0, keepdims=True)
    return grad_in, grad_gain, grad_bias


GELU_A = 0.7978845608028654
GELU_B = 0.044715
TILE = 256
BAND = 128
PAIR = 2 * HD


def local_body(tiles, wide, *refs):
    @pl.when(pl.program_id(0) < tiles)
    def _():
        local_rows(wide, *refs)

    @pl.when(pl.program_id(0) >= tiles)
    def _():
        local_grads(tiles, wide, *refs)


def local_rows(
    wide,
    scalars_ref, masked_ref, part_0_ref, part_1_ref, part_2_ref, part_3_ref, cotangent_ref,
    gain_ref, bias_ref, weights_ref,
    result_ref, grad_ref, give_0_ref, give_1_ref, give_2_ref, give_3_ref, norms_ref, weights_out_ref,
    factors_ref, normed_all_ref, branch_all_ref, second_all_ref, grad_out_all_ref,
    turned_ref, branch_turned_ref, probs_ref, stream_ref, held_ref, sems,
):
    rows = masked_ref.shape[0]
    hidden_width = weights_ref.shape[3] // 2 - 2 * wide
    here = pl.ds(pl.multiple_of(pl.program_id(0) * rows, rows), rows)
    normed_ref, branch_ref = normed_all_ref.at[here], branch_all_ref.at[here]
    second_ref, grad_out_ref = second_all_ref.at[here], grad_out_all_ref.at[here]

    def factor(start, width):
        return [factors_ref.at[side, here, start : start + width] for side in range(2)]

    grad_joints, grad_values = factor(0, 2 * wide), factor(2 * wide, wide)
    mixtures = factor(3 * wide, wide)
    hiddens = factor(4 * wide, hidden_width)
    actives = factor(4 * wide + hidden_width, hidden_width)

    bounds = (0, 4 * wide, 4 * wide + hidden_width, 4 * wide + 2 * hidden_width)
    opening = pl.program_id(0) == 0

    def copy(side, part):
        columns = slice(bounds[part], bounds[part + 1])
        return pltpu.make_async_copy(
            weights_ref.at[:, side, :, columns], held_ref.at[side, :, :, columns], sems.at[side, part]
        )

    @pl.when(opening)
    def _():
        for side, part in ((0, 0), (1, 0), (0, 1), (0, 2), (1, 1), (1, 2)):
            copy(side, part).start()

    def arrive(*places):
        @pl.when(opening)
        def _():
            for side, part in places:
                copy(side, part).wait()

    def weight(side, start, stop):
        return held_ref[side, :, :, start:stop].reshape(D, stop - start)

    bands = rows // BAND
    pairs = wide // PAIR

    row = pl.program_id(0) * rows + lax.broadcasted_iota(jnp.int32, (rows, 1), 0)
    keep = (row < scalars_ref[0]).astype(F32)
    place = scalars_ref[1]
    part_width = D // QUAD
    for slot in range(QUAD):
        columns = slice(slot * part_width, (slot + 1) * part_width)
        for bits, part_ref in enumerate((part_0_ref, part_1_ref, part_2_ref, part_3_ref)):

            @pl.when((place ^ bits) == slot)
            def _(part_ref=part_ref, columns=columns):
                stream_ref[:, columns] = masked_ref[:, columns].astype(F32) + part_ref[...].astype(F32)

    stream = stream_ref[...]
    gain_one, gain_two = gain_ref[2:3, :], gain_ref[3:4, :]
    normed, unit_one, scale_one = norm_forward(stream, gain_one, bias_ref[2:3, :])
    normed = normed.astype(BF16)
    normed_ref[...] = normed
    arrive((0, 0), (1, 0))
    packs = [dot_nn(normed, weight(side, 0, 3 * wide)).astype(BF16) for side in range(2)]

    lanes = lax.broadcasted_iota(jnp.int32, (BAND, PAIR), 1)
    low_head = lanes < HD
    down_rows = lax.broadcasted_iota(jnp.int32, (2 * BAND, BAND), 0) % BAND
    key_rows = lax.broadcasted_iota(jnp.int32, (2 * BAND, BAND), 1)
    allowed = (down_rows // P_SIZE == key_rows // P_SIZE) & (down_rows >= key_rows)

    def apart(pair_values):
        zero = jnp.zeros_like(pair_values)
        return jnp.concatenate(
            [jnp.where(low_head, pair_values, zero), jnp.where(low_head, zero, pair_values)], axis=0
        )

    def joined(stacked):
        return jnp.where(low_head, stacked[:BAND], stacked[BAND:])

    def piece(values_in, band, part, pair):
        start = part * wide + pair * PAIR
        return values_in[band * BAND : (band + 1) * BAND, start : start + PAIR]

    scale = HD ** (-0.5)
    for side in range(2):
        for band in range(bands):
            for pair in range(pairs):
                queries = apart(piece(packs[side], band, 0, pair)) * jnp.asarray(scale, BF16)
                scores = dot_nt(queries, piece(packs[side], band, 1, pair))
                scores = jnp.where(allowed, scores, NEGATIVE)
                shifted = jnp.exp(scores - jnp.max(scores, axis=-1, keepdims=True))
                probs = shifted / jnp.sum(shifted, axis=-1, keepdims=True)
                probs_ref[(side * bands + band) * pairs + pair] = probs
                mixed = dot_nn(probs.astype(BF16), piece(packs[side], band, 2, pair))
                mixtures[side][
                    band * BAND : (band + 1) * BAND, pair * PAIR : (pair + 1) * PAIR
                ] = joined(mixed).astype(BF16)

    middle = stream
    for side in range(2):
        middle = middle + dot_nt(mixtures[side][...], weight(side, 3 * wide, 4 * wide))
    second, unit_two, scale_two = norm_forward(middle, gain_two, bias_ref[3:4, :])
    second = second.astype(BF16)
    second_ref[...] = second
    grad_final = cotangent_ref[...].astype(F32) * keep
    grad_out = grad_final.astype(BF16)
    grad_out_ref[...] = grad_out

    lifted = jnp.zeros_like(middle)
    grad_second = jnp.zeros_like(middle)
    chunk = min(768, hidden_width)
    for side in range(2):
        arrive((side, 1), (side, 2))
        for start in range(0, hidden_width, chunk):
            first = 4 * wide + start
            upward = weight(side, first, first + chunk)
            downward = weight(side, first + hidden_width, first + hidden_width + chunk)
            hidden = dot_nn(second, upward)
            square = hidden * hidden
            bent = jnp.tanh(GELU_A * hidden * (1.0 + GELU_B * square))
            half = 0.5 * (1.0 + bent)
            active = (hidden * half).astype(BF16)
            slope = half + 0.5 * hidden * (1.0 - bent * bent) * GELU_A * (1.0 + 3.0 * GELU_B * square)
            actives[side][:, start : start + chunk] = active
            lifted = lifted + dot_nt(active, downward)
            grad_hidden = (dot_nn(grad_out, downward) * slope).astype(BF16)
            hiddens[side][:, start : start + chunk] = grad_hidden
            grad_second = grad_second + dot_nt(grad_hidden, upward)
    result_ref[...] = (middle + lifted).astype(BF16)

    grad_in, gain_grad_two, bias_grad_two = norm_backward(grad_second, unit_two, scale_two, gain_two)
    grad_middle = grad_final + grad_in
    branch = grad_middle.astype(BF16)
    branch_ref[...] = branch
    grad_normed = jnp.zeros_like(middle)
    for side in range(2):
        grad_mix = dot_nn(branch, weight(side, 3 * wide, 4 * wide)).astype(BF16)
        for band in range(bands):
            for pair in range(pairs):
                probs = probs_ref[(side * bands + band) * pairs + pair]
                grad_pair = apart(piece(grad_mix, band, 0, pair))
                grad_soft = dot_nt(grad_pair, piece(packs[side], band, 2, pair))
                centre = jnp.sum(grad_soft * probs, axis=-1, keepdims=True)
                grad_scores = (probs * (grad_soft - centre)).astype(BF16)
                queries = apart(piece(packs[side], band, 0, pair))
                grads = (
                    joined(dot_nn(grad_scores, piece(packs[side], band, 1, pair))) * scale,
                    dot_tn(grad_scores, queries) * scale,
                    dot_tn(probs.astype(BF16), grad_pair),
                )
                rows_here = slice(band * BAND, (band + 1) * BAND)
                for part in range(2):
                    first = part * wide + pair * PAIR
                    grad_joints[side][rows_here, first : first + PAIR] = grads[part].astype(BF16)
                grad_values[side][rows_here, pair * PAIR : (pair + 1) * PAIR] = grads[2].astype(BF16)
        grad_normed = grad_normed + dot_nt(grad_joints[side][...], weight(side, 0, 2 * wide))
        grad_normed = grad_normed + dot_nt(grad_values[side][...], weight(side, 2 * wide, 3 * wide))
    grad_in, gain_grad_one, bias_grad_one = norm_backward(grad_normed, unit_one, scale_one, gain_one)
    grad_stream = grad_middle + grad_in
    grad_ref[...] = grad_stream
    for slot in range(QUAD):
        columns = slice(slot * part_width, (slot + 1) * part_width)
        for bits, give_ref in enumerate((give_0_ref, give_1_ref, give_2_ref, give_3_ref)):

            @pl.when((place ^ bits) == slot)
            def _(give_ref=give_ref, columns=columns):
                give_ref[...] = grad_stream[:, columns].astype(BF16)


    @pl.when(pl.program_id(0) == 0)
    def _():
        norms_ref[...] = jnp.zeros_like(norms_ref)

    for place, value in enumerate((gain_grad_one, gain_grad_two, bias_grad_one, bias_grad_two)):
        norms_ref[place : place + 1, :] += value


def local_grads(
    tiles, wide,
    scalars_ref, masked_ref, part_0_ref, part_1_ref, part_2_ref, part_3_ref, cotangent_ref,
    gain_ref, bias_ref, weights_ref,
    result_ref, grad_ref, give_0_ref, give_1_ref, give_2_ref, give_3_ref, norms_ref, weights_out_ref,
    factors_ref, normed_ref, branch_ref, second_ref, grad_out_ref,
    turned_ref, branch_turned_ref, probs_ref, stream_ref, held_ref, sems,
):
    step = pl.program_id(0) - tiles
    block, side = step // 2, step % 2
    width = weights_out_ref.shape[3]

    @pl.when(step == 0)
    def _():
        turned_ref[...] = normed_ref[...].T
        branch_turned_ref[...] = branch_ref[...].T

    @pl.when(step == 2)
    def _():
        turned_ref[...] = second_ref[...].T

    @pl.when(step == 4)
    def _():
        turned_ref[...] = grad_out_ref[...].T

    def give(left_ref, right, columns):
        product = dot_nn(left_ref[...], right).astype(BF16)
        weights_out_ref[:, :, :, columns] = product.reshape(
            weights_out_ref.shape[:3] + (product.shape[1],)
        )

    @pl.when(block == 0)
    def _():
        give(turned_ref, factors_ref[side, :, : 3 * wide], slice(0, 3 * wide))
        give(branch_turned_ref, factors_ref[side, :, 3 * wide : 4 * wide], slice(3 * wide, 4 * wide))

    @pl.when(block != 0)
    def _():
        start = pl.multiple_of(block * width, width)
        give(turned_ref, factors_ref[side, :, pl.ds(start, width)], slice(None))


def local_layer(scalars, masked_low, spread_parts, cotangent, gain_rows, bias_rows, weights, wide):
    rows = masked_low.shape[0]
    tiles = rows // TILE
    columns = weights.shape[3]
    width = 4 * wide
    assert columns == 3 * width
    tiled = lambda size: pl.BlockSpec((TILE, size), lambda i: (jnp.minimum(i, tiles - 1), 0))
    fixed = lambda array: pl.BlockSpec(array.shape, lambda i: (0, 0), pipeline_mode=pl.Buffered(1))
    outs = [(D, BF16), (D, F32)] + [(D // QUAD, BF16)] * QUAD

    def grads_place(i):
        step = jnp.maximum(i - tiles, 0)
        return (0, step % 2, 0, step // 2)

    return pl.pallas_call(
        lambda *refs: local_body(tiles, wide, *refs),
        grid=(tiles + 2 * (columns // width),),
        in_specs=[pl.BlockSpec(memory_space=pltpu.SMEM)]
        + [tiled(D)] + [tiled(D // QUAD)] * QUAD + [tiled(D)]
        + [fixed(array) for array in (gain_rows, bias_rows)]
        + [pl.BlockSpec(memory_space=pl.ANY)],
        out_specs=[tiled(size) for size, _ in outs]
        + [
            pl.BlockSpec((8, D), lambda i: (0, 0)),
            pl.BlockSpec((weights.shape[0], 1, weights.shape[2], width), grads_place),
        ],
        out_shape=[jax.ShapeDtypeStruct((rows, size), kind) for size, kind in outs]
        + [jax.ShapeDtypeStruct((8, D), F32), jax.ShapeDtypeStruct(weights.shape, BF16)],
        scratch_shapes=[pltpu.VMEM((2, rows, columns), BF16)]
        + [pltpu.VMEM((rows, D), BF16)] * 4
        + [pltpu.VMEM((D, rows), BF16)] * 2
        + [
            pltpu.VMEM((2 * (TILE // BAND) * (wide // PAIR), 2 * BAND, BAND), F32),
            pltpu.VMEM((TILE, D), F32),
            pltpu.VMEM((2, weights.shape[0]) + weights.shape[2:], BF16),
            pltpu.SemaphoreType.DMA((2, 3)),
        ],
        compiler_params=pltpu.CompilerParams(
            dimension_semantics=("arbitrary",), vmem_limit_bytes=58 * 1024 * 1024
        ),
        cost_estimate=pl.CostEstimate(
            flops=12 * rows * D * columns,
            transcendentals=rows * columns,
            bytes_accessed=2 * 4 * D * columns,
        ),
    )(scalars, masked_low, *spread_parts, cotangent, gain_rows, bias_rows, weights)


def shards(
    embedded,
    lengths,
    patch_proj,
    global_proj,
    qkv_weight,
    out_weight,
    up_weight,
    down_weight,
    norm_gain,
    norm_bias,
    cotangent,
):
    half_rows = embedded.shape[1]
    patch_rows = half_rows // P_SIZE
    shard_rows = qkv_weight.shape[1]
    proj_rows = patch_proj.shape[0]
    norm_part = norm_gain.shape[0]
    cells = 2 * line_size()
    heads_width = qkv_weight.shape[3]
    hidden_width = up_weight.shape[2]
    x_here = x_place()

    positions = lax.axis_index("tensor") * half_rows + jnp.arange(half_rows, dtype=jnp.int32)
    keep_mask = (positions < lengths[0]).astype(F32)[:, None]
    masked_low = jnp.where(keep_mask > 0, embedded[0], jnp.zeros_like(embedded[0]))
    masked_low = lax.optimization_barrier(masked_low)

    joint_part = jnp.transpose(qkv_weight, (0, 2, 1, 3))
    output_part = jnp.transpose(out_weight, (0, 2, 1))
    down_part = jnp.transpose(down_weight, (0, 2, 1))

    norm_row = jnp.pad(
        jnp.concatenate([norm_gain, norm_bias]).reshape(1, -1), ((0, 0), (0, D - 2 * norm_part))
    )
    local_shard = jnp.concatenate(
        [joint_part[1, 0], joint_part[1, 1], joint_part[1, 2], output_part[1], up_weight[1], down_part[1]],
        axis=-1,
    )
    local_whole = lax.all_gather(local_shard, ("dp", "tensor"), axis=0)

    patch_pieces = masked_low.reshape(patch_rows, cells, QUAD, proj_rows)
    patches_dealt = quad_deal(patch_pieces)
    queue = LineQueue()
    patch_lined = line_gather(jnp.concatenate([patch_proj, norm_row], axis=0), queue)
    patch_whole = y_gather(patch_lined)
    patch_whole = patch_whole.reshape(cells, proj_rows + 1, D)
    patch_mat = patch_whole[:, :proj_rows].reshape(cells * proj_rows, D)
    norm_cells = patch_whole[:, proj_rows, : 2 * norm_part]
    norm_all = quad_collect(
        jnp.broadcast_to(norm_cells[None], (QUAD,) + norm_cells.shape)
    )[0].astype(F32)
    gain_rows = norm_all[..., :norm_part].reshape(NORMS, D)
    bias_rows = norm_all[..., norm_part:].reshape(NORMS, D)
    gain_rows, bias_rows = lax.optimization_barrier((gain_rows, bias_rows))

    def x_half(part):
        return part.reshape(part.shape[:-1] + (2, part.shape[-1] // 2))

    def global_part(layer):
        pieces = []
        for piece in (
            joint_part[layer, 0],
            joint_part[layer, 1],
            joint_part[layer, 2],
            output_part[layer],
            up_weight[layer],
            down_part[layer],
        ):
            halves = x_half(piece)
            pieces.append(halves)
        return jnp.concatenate(pieces, axis=-1)

    halves = global_part(0)
    own_half = lax.dynamic_index_in_dim(halves, x_here, 1, keepdims=False)
    their_half = lax.dynamic_index_in_dim(halves, 1 - x_here, 1, keepdims=False)
    global_shard = pair_up(own_half, flip_dp(their_half, 1), x_here)
    global_shard = global_shard.reshape(2 * shard_rows, -1)
    attend_columns = 2 * heads_width
    global_blocks = line_pass(global_shard, queue, (patch_whole,))
    queue.hold(global_blocks[-1])
    attend_lined = line_place_blocks([block[:, :attend_columns] for block in global_blocks])
    forward_lined = line_place_blocks([block[:, attend_columns:] for block in global_blocks])
    proj_part = jnp.transpose(global_proj)
    proj_pair = pair_up(proj_part, flip_dp(proj_part, 2), y_place())
    spread_lined = line_gather(proj_pair, queue)
    joint_columns = 3 * heads_width // 2

    patches_mat = patches_dealt.reshape(QUAD * patch_rows, cells * proj_rows)
    start_partial = dot_nn(patches_mat, patch_mat)
    initial = quad_scatter(start_partial)

    def attend_of():
        whole = y_gather(after(attend_lined, start_partial)).reshape(D, -1)
        return whole[:, :joint_columns], whole[:, joint_columns:]

    def forward_of(marker):
        whole = y_gather(after(forward_lined, marker)).reshape(D, -1)
        return whole[:, : hidden_width // 2], whole[:, hidden_width // 2 :]

    core = lax.axis_index("tensor")
    steps = jnp.arange(patch_rows, dtype=jnp.int32)
    global_places = jnp.concatenate([core * patch_rows + steps, (1 - core) * patch_rows + steps])
    global_out, first_saved, first_weights = layer_forward(
        initial, attend_of, forward_of, gain_rows, bias_rows, 0, global_places
    )
    spread_mat = spread_lined.reshape(cells * proj_rows, D)
    global_low = quad_gather(global_out.astype(BF16))
    spread_dealt = dot_nt(global_low, spread_mat).astype(BF16)
    spread_blocks = spread_dealt.reshape(QUAD * patch_rows, cells, proj_rows)
    byte_cells = cells == P_SIZE
    if byte_cells:
        part_place = quad_place()
        spread_parts = [
            spread_blocks[bits * patch_rows : (bits + 1) * patch_rows] for bits in range(QUAD)
        ]
        spread_parts = [
            (flip_quad(part, bits) if bits else part).reshape(half_rows, proj_rows)
            for bits, part in enumerate(spread_parts)
        ]
    else:
        part_place = jnp.int32(0)
        spread = quad_collect(spread_blocks).reshape(half_rows, D)
        spread_parts = jnp.split(spread, QUAD, axis=1)

    dp = dp_size()
    whole_rows = shard_rows % 16 == 0
    local_weights = local_whole.reshape(dp, 2, shard_rows, -1)
    if not whole_rows:
        local_weights = jnp.transpose(local_weights, (1, 0, 2, 3)).reshape(1, 2, D, -1)
    bound = jnp.clip(lengths[0] - lax.axis_index("tensor") * half_rows, 0, half_rows)
    scalars = jnp.stack([bound, part_place.astype(jnp.int32)])
    local_outs = local_layer(
        scalars, masked_low, spread_parts, cotangent[0], gain_rows, bias_rows, local_weights, heads_width
    )
    outcome, grad_local = local_outs[:2]
    grad_parts = local_outs[2 : 2 + QUAD]
    local_norms, local_grads_out = local_outs[2 + QUAD :]
    second_gains, second_biases = (local_norms[0], local_norms[1]), (local_norms[2], local_norms[3])
    if byte_cells:
        spread_grads = jnp.concatenate(
            [
                (flip_quad(part, bits) if bits else part).reshape(patch_rows, cells, proj_rows)
                for bits, part in enumerate(grad_parts)
            ],
            axis=0,
        )
    else:
        grad_low = jnp.concatenate(grad_parts, axis=1)
        spread_grads = quad_deal(grad_low.reshape(patch_rows, cells, QUAD, proj_rows))
    spread_grads = spread_grads.reshape(QUAD * patch_rows, cells * proj_rows)
    if not whole_rows:
        local_grads_out = jnp.transpose(
            local_grads_out.reshape(2, dp, shard_rows, -1), (1, 0, 2, 3)
        )
    local_summed = lax.psum_scatter(
        local_grads_out.reshape(2 * dp, shard_rows, -1), ("dp", "tensor"), scatter_dimension=0
    ).astype(F32)

    grad_global = quad_scatter(dot_nn(spread_grads, spread_mat))
    proj_grads = dot_tn(spread_grads, global_low).astype(BF16).reshape(cells, proj_rows, D)
    marks = []
    grad_proj = line_scatter(proj_grads.reshape(line_size(), 2, proj_rows, D), marks)
    grad_proj = halve(grad_proj, y_place(), 0, 2)
    ties = ((), (), tuple(marks[:1]), (), tuple(marks[1:2]), (cells, 2 * shard_rows))
    grad_start, attend_half, forward_half, first_gains, first_biases = layer_backward(
        grad_global, first_saved, first_weights, gain_rows, bias_rows, 0, global_places, ties
    )
    global_summed = line_scatter(jnp.concatenate([attend_half, forward_half], axis=2))
    grad_patch_mat = dot_tn(patches_mat, grad_start).astype(BF16).reshape(cells, proj_rows, D)
    gain_grads = jnp.stack([first_gains[0], first_gains[1], second_gains[0], second_gains[1]])
    bias_grads = jnp.stack([first_biases[0], first_biases[1], second_biases[0], second_biases[1]])
    norm_grads = jnp.concatenate(
        [
            gain_grads.reshape(cells, QUAD, norm_part),
            bias_grads.reshape(cells, QUAD, norm_part),
        ],
        axis=2,
    )
    place = quad_place()
    norm_sum = lax.dynamic_index_in_dim(norm_grads, place, 1, keepdims=False)
    for bits in range(1, QUAD):
        piece = lax.dynamic_index_in_dim(norm_grads, place ^ bits, 1, keepdims=False)
        norm_sum = norm_sum + flip_quad(piece, bits)
    norm_rows = jnp.pad(norm_sum[:, None, :].astype(BF16), ((0, 0), (0, 0), (0, D - 2 * norm_part)))
    patch_marks = []
    patch_terms = jnp.concatenate([grad_patch_mat, norm_rows], axis=1)
    patch_half = y_scatter(patch_terms)
    patch_summed = line_scatter(patch_half, patch_marks)
    grad_patches = after(dot_nt(grad_start, patch_mat).astype(BF16), forward_half, patch_terms)
    grad_patches = quad_collect(grad_patches.reshape(QUAD * patch_rows, cells, proj_rows))
    grad_patches = grad_patches.reshape(half_rows, D).astype(F32)
    grad_patches = after(grad_patches, *patch_marks[:1])
    grad_input = ((grad_local + grad_patches) * keep_mask).astype(BF16)[None]

    def x_restore(summed):
        shaped = summed.reshape(2, shard_rows, -1)
        own = lax.dynamic_index_in_dim(shaped, x_here, 0, keepdims=False)
        theirs = lax.dynamic_index_in_dim(shaped, 1 - x_here, 0, keepdims=False)
        return pair_up(own, flip_dp(theirs.astype(BF16), 1).astype(F32), x_here)

    global_summed = x_restore(global_summed)
    attend_global = global_summed[..., :attend_columns]
    forward_global = global_summed[..., attend_columns:]

    def x_columns(source, start, width):
        return jnp.concatenate([source[0, :, start : start + width], source[1, :, start : start + width]], axis=1)

    half_heads, half_hidden = heads_width // 2, hidden_width // 2
    joint_out = jnp.stack(
        [
            jnp.stack([x_columns(attend_global, k * half_heads, half_heads) for k in range(3)], axis=1),
            local_summed[:, : 3 * heads_width].reshape(shard_rows, 3, heads_width),
        ]
    )
    output_out = jnp.stack(
        [
            jnp.transpose(x_columns(attend_global, 3 * half_heads, half_heads)),
            jnp.transpose(local_summed[:, 3 * heads_width : 4 * heads_width]),
        ]
    )
    up_out = jnp.stack([x_columns(forward_global, 0, half_hidden), local_summed[:, 4 * heads_width : 4 * heads_width + hidden_width]])
    down_out = jnp.stack(
        [
            jnp.transpose(x_columns(forward_global, half_hidden, half_hidden)),
            jnp.transpose(local_summed[:, 4 * heads_width + hidden_width :]),
        ]
    )
    return (
        outcome[None],
        grad_input,
        patch_summed[:proj_rows],
        jnp.transpose(grad_proj),
        joint_out,
        output_out,
        up_out,
        down_out,
        patch_summed[proj_rows, :norm_part],
        patch_summed[proj_rows, norm_part : 2 * norm_part],
    )


def solution(mesh):
    placed = (
        P("dp", "tensor", None),
        P("dp"),
        P(("dp", "tensor"), None),
        P(None, ("dp", "tensor")),
        P(None, "dp", None, "tensor"),
        P(None, "tensor", "dp"),
        P(None, "dp", "tensor"),
        P(None, "tensor", "dp"),
        P(("dp", "tensor")),
        P(("dp", "tensor")),
        P("dp", "tensor", None),
    )
    return jax.shard_map(
        shards,
        mesh=mesh,
        in_specs=placed,
        out_specs=(
            P("dp", "tensor", None),
            P("dp", "tensor", None),
            P(("dp", "tensor"), None),
            P(None, ("dp", "tensor")),
            P(None, "dp", None, "tensor"),
            P(None, "tensor", "dp"),
            P(None, "dp", "tensor"),
            P(None, "tensor", "dp"),
            P(("dp", "tensor")),
            P(("dp", "tensor")),
        ),
        check_vma=False,
    )
```
